32 devices in a mesh: mem: 4 (over y, core), lat: 4 (over z), lon: 2 (over x).
Axes of the slice: x: 2, y: 2, z: 4, core: 2. Of those that a mesh axis runs over, the one named last changes fastest.
Arguments:
- perturbations: bfloat16 [4, 8, 128, 256], P('mem', None, 'lat', 'lon'), may hold values from -6 to 6
- control: float32 [4, 8, 128, 256], P('mem', None, 'lat', 'lon'), may hold values from -6 to 6
- diffusivity: float32 [8, 128, 256], P(None, 'lat', 'lon'), may hold values from 0.03 to 0.24
- obs_cells: int32 [32, 512], P(('mem', 'lat', 'lon')), may hold values from 0 to 8191
- obs_counts: int32 [32], P(('mem', 'lat', 'lon')), may hold values from 256 to 512, as said below
- innovations: float32 [32, 512], P(('mem', 'lat', 'lon')), may hold values from -8 to 8
- obs_precision: float32 [32, 512], P(('mem', 'lat', 'lon')), may hold values from 0.5 to 2
Outputs:
- analysis_control: float32 [4, 8, 128, 256], P('mem', None, 'lat', 'lon')
The draws below stay inside these ranges and needn't reach their ends.
Inputs may be any that keep to these rules, and one draw needn't show every extreme that they name: `obs_cells`: an entry names a cell of its own tile, counted as level times 8 * 128 plus tile row times 128 plus tile column; one cell may be named by several slots. `obs_counts`: slots at and beyond a tile's count are ignored; in every draw some tile is full.
All inputs are finite; a program needn't handle non-finite values.
Results may differ from the reference program's by a relative error of at most 0.0003.
Values sent between devices are 32-bit elements; how exact they have to be, the bound alone decides.
A program may use at most 64 MiB of HBM per device.

```python
import math
import jax
import jax.numpy as jnp
from jax import lax

LEV = 8
LAT_DEV = 32
LON_DEV = 128
OBS_TILE = 512
SWEEPS = 4
STEPS = 2
MEMBERS = 4
NLAT = 128
NLON = 256
ROWS_TILE = 8
TILE_CELLS = 8192
TILES = 32
N_LAT = 4
N_LON = 2


def draw_obs_counts(key, part):
    count_key, pick_key = jax.random.split(jax.random.fold_in(key, 11))
    counts = jax.random.randint(count_key, (TILES,), OBS_TILE // 2, OBS_TILE + 1)
    chosen = jax.random.randint(pick_key, (), 0, TILES)
    return jnp.where(jnp.arange(TILES) == chosen, OBS_TILE, counts).astype(jnp.int32)


def place_ends(drawn, key, smallest, high):
    spot = [jax.random.randint(jax.random.fold_in(key, axis), (), 0, length) for axis, length in enumerate(drawn.shape)]
    main_axis = drawn.shape.index(max(drawn.shape))
    neighbour = spot[:main_axis] + [(spot[main_axis] + 1) % drawn.shape[main_axis]] + spot[main_axis + 1:]
    return drawn.at[tuple(spot)].set(smallest).at[tuple(neighbour)].set(high)


def shard_levels(key, shape, shards, least, largest):
    def one(position, parts):
        heights = jax.random.uniform(jax.random.fold_in(jax.random.fold_in(key, 6), position), (parts,), jnp.float32, least / len(shards), largest / len(shards))
        return jnp.repeat(jnp.exp(heights), shape[position] // parts).reshape((-1,) + (1,) * (len(shape) - position - 1))

    level = one(*shards[0])
    for cut in shards[1:]:
        level = level * one(*cut)
    return level


def bell_draw(stream_key, dims, scale, bound, shards=(), held_as=jnp.bfloat16):
    drawn = jax.random.normal(stream_key, dims, jnp.float32) * scale
    if len(shards) > 0:
        drawn = shard_levels(stream_key, dims, shards, -0.22, 0.18) * drawn
    return jnp.clip(drawn, min=-bound, max=bound).astype(held_as)


def setup_inputs(seed: int = 0) -> dict:
    key_of = jax.random.split(jax.random.key(seed), 8)
    return {
        "perturbations": bell_draw(key_of[0], (MEMBERS, LEV, NLAT, NLON), 1.0, 6.0, ((0, 4), (2, 4), (3, 2))),
        "control": bell_draw(key_of[1], (MEMBERS, LEV, NLAT, NLON), 1.0, 6.0, ((0, 4), (2, 4), (3, 2)), jnp.float32),
        "diffusivity": jnp.clip(jnp.exp(math.log(0.24) - 2.0794415 * jax.random.uniform(key_of[2], (LEV, NLAT, NLON), jnp.float32) ** shard_levels(key_of[2], (LEV, NLAT, NLON), ((1, 4), (2, 2)), -0.2, 0.2)), 0.03, 0.24),
        "obs_cells": place_ends(jax.random.randint(key_of[3], (TILES, OBS_TILE), 0, TILE_CELLS), jax.random.fold_in(key_of[3], 1), 0, TILE_CELLS - 1).astype(jnp.int32),
        "obs_counts": draw_obs_counts(jax.random.fold_in(key_of[7], 71), 0),
        "innovations": bell_draw(key_of[5], (TILES, OBS_TILE), 1.5, 8.0, ((0, 32),), jnp.float32),
        "obs_precision": jnp.clip(jnp.exp(math.log(2.0) - 1.3862944 * jax.random.uniform(key_of[6], (TILES, OBS_TILE), jnp.float32) ** shard_levels(key_of[6], (TILES, OBS_TILE), ((0, 32),), -0.2, 0.2)), 0.5, 2.0),
    }


huber_edge = 1.5
step_length = 0.5

def laplacian(state_field):
    padded = jnp.pad(state_field, ((0, 0), (1, 1), (0, 0)))
    return padded[:, :-2, :] + padded[:, 2:, :] + jnp.roll(state_field, 1, axis=2) + jnp.roll(state_field, -1, axis=2) - 4.0 * state_field

def smooth(state_field, diffusivity):
    for sweep_index in range(SWEEPS):
        state_field = state_field + diffusivity * laplacian(state_field)
    return state_field

def adjoint(state_field, diffusivity):
    for sweep_index in range(SWEEPS):
        state_field = state_field + laplacian(diffusivity * state_field)
    return state_field

def flat_positions(obs_cells):
    tile_ids = jnp.arange(TILES, dtype=jnp.int32)
    member_part = tile_ids // (N_LAT * N_LON)
    lat_part = tile_ids // N_LON % N_LAT
    lon_part = tile_ids % N_LON
    level_index = obs_cells // (ROWS_TILE * LON_DEV)
    tile_row = obs_cells // LON_DEV % ROWS_TILE
    tile_column = obs_cells % LON_DEV
    global_row = lat_part[:, None] * LAT_DEV + member_part[:, None] * ROWS_TILE + tile_row
    global_column = lon_part[:, None] * LON_DEV + tile_column
    return ((level_index * NLAT + global_row) * NLON + global_column).astype(jnp.int32)

def reference(perturbations, control, diffusivity, obs_cells, obs_counts, innovations, obs_precision):
    weight = 1.0 / math.sqrt(MEMBERS - 1)
    positions = flat_positions(obs_cells).reshape(-1)
    live_slots = (jnp.arange(OBS_TILE, dtype=jnp.int32)[None, :] < obs_counts[:, None]).astype(jnp.float32)
    alpha_all = control
    for step_index in range(STEPS):

        def accumulate(member_total, member_pair):
            member_x, member_alpha = member_pair
            return (member_total + member_x.astype(jnp.float32) * smooth(member_alpha, diffusivity), None)
        member_total, unused = lax.scan(accumulate, jnp.zeros((LEV, NLAT, NLON), jnp.float32), (perturbations, alpha_all))
        increment = weight * member_total
        observed = increment.reshape(-1)[positions].reshape(obs_cells.shape)
        misfit = (observed - innovations) * obs_precision
        pulled = jnp.clip(misfit, -huber_edge, huber_edge) * obs_precision * live_slots
        forcing = jnp.zeros((LEV * NLAT * NLON,), jnp.float32).at[positions].add(pulled.reshape(-1)).reshape(LEV, NLAT, NLON)

        def update(member_pair):
            member_x, member_alpha = member_pair
            gradient = member_alpha + adjoint(weight * member_x.astype(jnp.float32) * forcing, diffusivity)
            return member_alpha - step_length * gradient
        alpha_all = lax.map(update, (perturbations, alpha_all))
    return alpha_all
```

```python
import functools
import math

import jax
import jax.numpy as jnp
from jax import lax
from jax.experimental import pallas as pl
from jax.experimental.pallas import tpu as pltpu
from jax.sharding import PartitionSpec as P

SWEEPS = 4
STEPS = 2


huber_edge = 1.5
step_length = 0.5


def with_halo(cells, sides, width):
    for axis, dim in sides:
        count = lax.axis_size(axis)
        head = lax.slice_in_dim(cells, 0, width, axis=dim)
        tail = lax.slice_in_dim(cells, cells.shape[dim] - width, cells.shape[dim], axis=dim)
        cells = jnp.concatenate(
            [
                lax.ppermute(tail, axis, [(i, (i + 1) % count) for i in range(count)]),
                cells,
                lax.ppermute(head, axis, [((i + 1) % count, i) for i in range(count)]),
            ],
            axis=dim,
        )
    return cells


def inside_rows(lat_rows, margin):
    first_row = lax.axis_index("lat") * lat_rows - margin
    global_rows = first_row + jnp.arange(lat_rows + 2 * margin, dtype=jnp.int32)
    total_rows = lat_rows * lax.axis_size("lat")
    return ((global_rows >= 0) & (global_rows < total_rows)).astype(jnp.float32)[None, :, None]


def stencil(padded):
    center = padded[:, 1:-1, 1:-1]
    laplace_term = (
        padded[:, :-2, 1:-1]
        + padded[:, 2:, 1:-1]
        + padded[:, 1:-1, :-2]
        + padded[:, 1:-1, 2:]
        - 4.0 * center
    )
    return (laplace_term, center)


def smooth_deep(state_field, kappa_rim):
    lat_rows = state_field.shape[1]
    padded = with_halo(state_field, (("lat", 1), ("lon", 2)), SWEEPS)
    padded = padded * inside_rows(lat_rows, SWEEPS)
    for sweep_index in range(SWEEPS):
        offset = sweep_index + 1
        local_kappa = kappa_rim[
            :, offset : kappa_rim.shape[1] - offset, offset : kappa_rim.shape[2] - offset
        ]
        laplace_term, center = stencil(padded)
        padded = (center + local_kappa * laplace_term) * inside_rows(lat_rows, SWEEPS - offset)
    return padded


def adjoint_deep(state_field, kappa_rim):
    lat_rows = state_field.shape[1]
    padded = with_halo(state_field, (("lat", 1), ("lon", 2)), SWEEPS)
    padded = padded * inside_rows(lat_rows, SWEEPS)
    for sweep_index in range(SWEEPS):
        local_kappa = kappa_rim[
            :,
            sweep_index : kappa_rim.shape[1] - sweep_index,
            sweep_index : kappa_rim.shape[2] - sweep_index,
        ]
        laplace_term, center = stencil(local_kappa * padded)
        padded = (padded[:, 1:-1, 1:-1] + laplace_term) * inside_rows(
            lat_rows, SWEEPS - sweep_index - 1
        )
    return padded


def per_device(
    perturbations, control, diffusivity, obs_cells, obs_counts, innovations, obs_precision
):
    members = lax.axis_size("mem")
    weight = 1.0 / math.sqrt(members - 1)
    member_x = perturbations[0]
    alpha_now = control[0]
    live_slots = (
        jnp.arange(obs_cells.shape[1], dtype=jnp.int32)[None, :] < obs_counts[:, None]
    ).astype(jnp.float32)
    masked_weight = obs_precision * live_slots
    kappa_rim = with_halo(diffusivity, (("lat", 1), ("lon", 2)), SWEEPS)
    for step_index in range(STEPS):
        smoothed = smooth_deep(alpha_now, kappa_rim)
        member_term = member_x.astype(jnp.float32) * smoothed
        owned_piece = lax.psum_scatter(member_term, "mem", scatter_dimension=1, tiled=True)
        increment = weight * owned_piece
        tile_cells = obs_cells[0]
        observed = increment.reshape(-1)[tile_cells]
        misfit = (observed - innovations[0]) * masked_weight[0]
        pulled = jnp.clip(misfit, -huber_edge, huber_edge) * masked_weight[0]
        tile_field = (
            jnp.zeros((increment.size,), jnp.float32)
            .at[tile_cells]
            .add(pulled)
            .reshape(increment.shape)
        )
        forcing = lax.all_gather(tile_field, "mem", axis=1, tiled=True)
        source = weight * member_x.astype(jnp.float32) * forcing
        gradient = alpha_now + adjoint_deep(source, kappa_rim)
        alpha_now = alpha_now - step_length * gradient
    return alpha_now[None]


LANES = 128
SUBLANES = 8
HALO = STEPS * SWEEPS
SLOT = 2 * HALO
GROUP = LANES // SLOT
MESH = pl.DeviceIdType.MESH


def copy_plan(members, peers, edge_tiles):
    keys = []
    for field in ("alpha", "kappa", "kappa_far", "x"):
        keys += [(field, "row", side) for side in (-1, 1)]
    for pack in ("pack", "packx"):
        keys += [(pack, side, peer) for side in (-1, 0, 1) for peer in range(peers)]
    keys += [("cells", hop) for hop in range(1, members)]
    for step in range(STEPS):
        keys += [("sum", step, hop) for hop in range(1, members)]
        keys += [("tile", step, hop) for hop in range(1, members)]
        keys += [("edge", step, peer, hop) for peer in range(peers) for hop in range(members)]
    numbers = {key: number for number, key in enumerate(keys)}
    received = len(keys)
    for side in (-1, 1):
        numbers["cells_row", side] = received
        received += edge_tiles
    for step in range(STEPS):
        for side in (-1, 1):
            numbers["row", step, side] = received
            received += edge_tiles
            for peer in range(peers):
                numbers["corner", step, side, peer] = received
                received += edge_tiles
    sent = len(keys)
    for side in (-1, 1):
        numbers["cells_out", side] = sent
        sent += members
    for step in range(STEPS):
        for side in (-1, 1):
            numbers["row_out", step, side] = sent
            sent += members
            for peer in range(peers):
                numbers["corner_out", step, side, peer] = sent
                sent += members
    return numbers, sent, received


def kernel(
    members,
    lat_count,
    lon_count,
    tile_rows,
    x_in,
    control_in,
    kappa_in,
    cells_in,
    counts_ref,
    innovations_in,
    precision_in,
    out_ref,
    x_ref,
    control_ref,
    kappa_ref,
    cells_ref,
    innovations_ref,
    precision_ref,
    load_sems,
    x_flat,
    alpha_o,
    alpha_h,
    kappa_o,
    kappa_h,
    wx_o,
    wx_h,
    work_o,
    work_h,
    next_o,
    next_h,
    forcing_o,
    forcing_h,
    pack_out,
    pack_in,
    packx_out,
    packx_in,
    edge_out,
    edge_in,
    terms,
    pieces,
    pulled_out,
    pulled_in,
    cells_all,
    rows_hot,
    cols_hot,
    send_sems,
    recv_sems,
):
    levels = SUBLANES
    rows = control_ref.shape[0] // levels
    slots = cells_ref.shape[1]
    groups = rows // GROUP
    edge_tiles = HALO // tile_rows
    peers = [1] if lon_count == 2 else [1, lon_count - 1]
    numbers, _, _ = copy_plan(members, len(peers), edge_tiles)
    weight = 1.0 / math.sqrt(members - 1)
    mem = lax.axis_index("mem")
    lat = lax.axis_index("lat")
    lon = lax.axis_index("lon")
    has = {-1: lat > 0, 0: None, 1: lat < lat_count - 1}

    def guarded(condition, run):
        if condition is None:
            run()
        else:
            pl.when(condition)(run)

    def device(mem_hop, lat_hop, lon_hop):
        return (
            lax.rem(mem + mem_hop, members),
            lat + lat_hop,
            lax.rem(lon + lon_hop, lon_count),
        )

    def far(peer):
        return len(peers) - 1 - peer

    def remote(src, dst, send_number, recv_number, target):
        return pltpu.make_async_remote_copy(
            src_ref=src,
            dst_ref=dst,
            send_sem=send_sems.at[send_number],
            recv_sem=recv_sems.at[recv_number],
            device_id=target,
            device_id_type=MESH,
        )

    pending = []

    def send(condition, src, dst, send_number, recv_number, target):
        guarded(condition, lambda: remote(src, dst, send_number, recv_number, target).start())
        pending.append((condition, src, send_number))

    def settle(name=None):
        kept = []
        for condition, src, number in pending:
            if name is None or number in (numbers[name, "row", -1], numbers[name, "row", 1]):
                guarded(
                    condition,
                    lambda: remote(src, src, number, 0, device(0, 0, peers[0])).wait_send(),
                )
            else:
                kept.append((condition, src, number))
        pending[:] = kept

    def await_in(condition, dst, recv_number):
        guarded(
            condition,
            lambda: remote(dst, dst, 0, recv_number, device(0, 0, peers[0])).wait_recv(),
        )

    loads = [
        pltpu.make_async_copy(src, dst, load_sems.at[number])
        for number, (src, dst) in enumerate(
            (
                (control_in, control_ref),
                (kappa_in, kappa_ref),
                (x_in, x_ref),
                (cells_in, cells_ref),
                (innovations_in, innovations_ref),
                (precision_in, precision_ref),
            )
        )
    ]
    for load in loads:
        load.start()

    barrier = pltpu.get_barrier_semaphore()
    for lat_hop in (0, -1, 1):
        def greet(lat_hop=lat_hop):
            for lon_hop in [0] + peers:
                for mem_hop in range(members if lon_hop == 0 else 1):
                    if (lat_hop, lon_hop, mem_hop) != (0, 0, 0):
                        pl.semaphore_signal(
                            barrier,
                            inc=1,
                            device_id=device(mem_hop, lat_hop, lon_hop),
                            device_id_type=MESH,
                        )
        guarded(has[lat_hop], greet)

    lane = lax.broadcasted_iota(jnp.int32, (1, SUBLANES, LANES), 2)
    lane2 = lane[0]

    for load in loads:
        load.wait()
    x_flat[...] = weight * x_ref[...].astype(jnp.float32)
    for r in range(rows):
        level_rows = pl.ds(r, levels, stride=rows)
        alpha_o[HALO + r] = control_ref[level_rows, :]
        kappa_o[HALO + r] = kappa_ref[level_rows, :]
        wx_o[HALO + r] = x_flat[level_rows, :]

    def packed(read, count):
        total = jnp.zeros((SUBLANES, LANES), jnp.float32)
        for j in range(count):
            shifted = pltpu.roll(read(j), (HALO + SLOT * j) % LANES, 1)
            total = jnp.where(lane2 // SLOT == j, shifted, total)
        return total

    def unpacked(read, j):
        shift = (LANES - HALO - SLOT * j) % LANES
        parts = [pltpu.roll(read(peer), shift, 1) if shift else read(peer) for peer in range(len(peers))]
        if len(parts) == 1:
            return parts[0]
        return jnp.where(lane2 < LANES // 2, parts[0], parts[1])

    for g in range(groups):
        base = HALO + g * GROUP
        pack_out[g, 0] = packed(lambda j: alpha_o[base + j], GROUP)
        pack_out[g, 1] = packed(lambda j: kappa_o[base + j], GROUP)
        packx_out[g] = packed(lambda j: wx_o[base + j], GROUP)

    zero_rows = jnp.zeros((HALO, SUBLANES, LANES), jnp.float32)
    for side in (-1, 1):
        start = 0 if side < 0 else HALO + rows
        group = 0 if side < 0 else groups + 1
        tile = 0 if side < 0 else edge_tiles + members

        def clear(start=start, group=group, tile=tile):
            for ref in (alpha_o, kappa_o, wx_o):
                ref[start : start + HALO] = zero_rows
            cells_all[tile : tile + edge_tiles] = jnp.zeros((edge_tiles, 1, slots), jnp.int32)
            for step in range(STEPS):
                pulled_in[step, tile : tile + edge_tiles] = jnp.zeros(
                    (edge_tiles, 1, slots), jnp.float32
                )
            for peer in range(len(peers)):
                pack_in[peer, group] = jnp.zeros((2, SUBLANES, LANES), jnp.float32)
                packx_in[peer, group] = jnp.zeros((SUBLANES, LANES), jnp.float32)
                for step in range(STEPS):
                    edge_in[step, peer, tile : tile + edge_tiles] = jnp.zeros(
                        (edge_tiles, SUBLANES, LANES), jnp.float32
                    )

        guarded(jnp.logical_not(has[side]), clear)

    greeted = len(peers) + members
    lat_near = 1 + (lat > 0).astype(jnp.int32) + (lat < lat_count - 1).astype(jnp.int32)
    pl.semaphore_wait(barrier, greeted * lat_near - 1)

    def row_copies(name, field, width, skip=0):
        for side in (-1, 1):
            source = HALO + skip if side < 0 else HALO + rows - width - skip
            target = HALO + rows + skip if side < 0 else HALO - width - skip
            send(
                has[side],
                field.at[pl.ds(source, width)],
                field.at[pl.ds(target, width)],
                numbers[name, "row", side],
                numbers[name, "row", -side],
                device(0, side, 0),
            )

    def row_waits(name, field, width, skip=0):
        for side in (-1, 1):
            start = HALO - width - skip if side < 0 else HALO + rows + skip
            await_in(has[side], field.at[pl.ds(start, width)], numbers[name, "row", side])

    def pack_copies(name, source, target):
        for side in (0, -1, 1):
            for peer, hop in enumerate(peers):
                if side == 0:
                    src, dst = source, target.at[far(peer), pl.ds(1, groups)]
                elif side < 0:
                    src, dst = source.at[0], target.at[far(peer), groups + 1]
                else:
                    src, dst = source.at[groups - 1], target.at[far(peer), 0]
                send(
                    has[side],
                    src,
                    dst,
                    numbers[name, side, peer],
                    numbers[name, -side, far(peer)],
                    device(0, side, hop),
                )

    def pack_waits(name, target):
        for side in (0, -1, 1):
            for peer in range(len(peers)):
                if side == 0:
                    dst = target.at[peer, pl.ds(1, groups)]
                else:
                    dst = target.at[peer, 0 if side < 0 else groups + 1]
                await_in(has[side], dst, numbers[name, side, peer])

    pack_copies("pack", pack_out, pack_in)
    row_copies("alpha", alpha_o, SWEEPS)
    row_copies("kappa", kappa_o, SWEEPS)
    pack_copies("packx", packx_out, packx_in)
    row_copies("kappa_far", kappa_o, HALO - SWEEPS, SWEEPS)
    row_copies("x", wx_o, HALO)

    def to_group(step, source, target, name):
        for hop in range(1, members):
            send(
                None,
                source,
                target.at[edge_tiles + mem],
                numbers[name + (hop,)],
                numbers[name + (hop,)],
                device(hop, 0, 0),
            )
        outs, ins = ("cells_out", "cells_row") if step is None else ("row_out", "row")
        key = () if step is None else (step,)
        for side in (-1, 1):
            near = mem - (0 if side < 0 else members - edge_tiles)
            inside = near < edge_tiles if side < 0 else near >= 0
            for hop in range(members):
                send(
                    jnp.logical_and(has[side], inside),
                    source,
                    target.at[near + (edge_tiles + members if side < 0 else 0)],
                    numbers[(outs,) + key + (side,)] + hop,
                    numbers[(ins,) + key + (-side,)] + near,
                    device(hop, side, 0),
                )

    def others():
        for hop in range(1, members):
            yield None, hop, edge_tiles + lax.rem(mem + members - hop, members)
        for side in (-1, 1):
            for i in range(edge_tiles):
                yield side, i, i + (0 if side < 0 else edge_tiles + members)

    to_group(None, cells_ref, cells_all, ("cells",))

    spots = tile_rows * levels

    def hot(spot, cells):
        column = lax.rem(cells, LANES)
        tile_row = lax.rem(lax.div(cells, LANES), tile_rows)
        level = lax.div(cells, LANES * tile_rows)
        place = tile_row * levels + level
        rows_hot[spot] = (
            lax.broadcasted_iota(jnp.int32, (spots, slots), 0) == place
        ).astype(jnp.float32).astype(jnp.bfloat16)
        cols_hot[spot] = (
            lax.broadcasted_iota(jnp.int32, (LANES, slots), 0) == column
        ).astype(jnp.float32).astype(jnp.bfloat16)

    def spread(spot, pulled):
        tile = jnp.zeros((spots, LANES), jnp.float32)
        for half in halves(pulled):
            tile = tile + lax.dot_general(
                rows_hot[spot] * half,
                cols_hot[spot],
                (((1,), (1,)), ((), ())),
                preferred_element_type=jnp.float32,
            )
        return tile.reshape(tile_rows, SUBLANES, LANES)

    mine = edge_tiles + mem
    hot(mine, cells_ref[...])
    live = (
        lax.broadcasted_iota(jnp.int32, (1, slots), 1) < counts_ref[0]
    ).astype(jnp.float32)
    masked_weight = precision_ref[...] * live
    innovations = innovations_ref[...]

    def halves(value):
        high = value.astype(jnp.bfloat16)
        return high, (value - high.astype(jnp.float32)).astype(jnp.bfloat16)

    first_lane, last_lane = lane == 0, lane == LANES - 1

    def sides(own, near):
        own_w, near_w = pltpu.roll(own, 1, 2), pltpu.roll(near, 1, 2)
        own_e, near_e = pltpu.roll(own, LANES - 1, 2), pltpu.roll(near, LANES - 1, 2)
        return (
            jnp.where(first_lane, near_w, own_w) + jnp.where(last_lane, near_e, own_e),
            jnp.where(first_lane, own_w, near_w) + jnp.where(last_lane, own_e, near_e),
        )

    def chunks(margin):
        first, last = HALO - margin, HALO + rows + margin
        return [(a, min(a + 8, last)) for a in range(first, last, 8)]

    def smooth_sweep(src, dst, margin, emit=None):
        for a, b in chunks(margin):
            own, near = src[0][a:b], src[1][a:b]
            beside = sides(own, near)
            for ref, value, both, kappa, out in (
                (src[0], own, beside[0], kappa_o, dst[0]),
                (src[1], near, beside[1], kappa_h, dst[1]),
            ):
                if emit is not None and ref is src[1]:
                    continue
                total = ref[a - 1 : b - 1] + ref[a + 1 : b + 1] + both
                value = value + kappa[a:b] * (total - 4.0 * value)
                if emit is None:
                    out[a:b] = value
                else:
                    emit(a, b, value)

    def adjoint_sweep(src, dst, margin, emit=None, near_too=True):
        for a, b in chunks(margin):
            scaled = [
                kappa[a - 1 : b + 1] * ref[a - 1 : b + 1]
                for ref, kappa in ((src[0], kappa_o), (src[1], kappa_h))
            ]
            beside = sides(scaled[0][1:-1], scaled[1][1:-1])
            for which in (0, 1):
                if which and not near_too:
                    continue
                t = scaled[which]
                value = src[which][a:b] + (t[:-2] + t[2:] + beside[which] - 4.0 * t[1:-1])
                if emit is None:
                    dst[which][a:b] = value
                else:
                    emit(which, a, b, value)

    work, following = (work_o, work_h), (next_o, next_h)

    row_waits("alpha", alpha_o, SWEEPS)
    row_waits("kappa", kappa_o, SWEEPS)
    pack_waits("pack", pack_in)
    for e in range(rows + 2 * HALO):
        g, j = divmod(e, GROUP)
        alpha_h[e] = unpacked(lambda peer: pack_in[peer, g, 0], j)
        kappa_h[e] = unpacked(lambda peer: pack_in[peer, g, 1], j)

    for step in range(STEPS):
        term = terms.at[step]

        def emit_term(a, b, value):
            term[a - HALO : b - HALO] = wx_o[a:b] * value

        smooth_sweep((alpha_o, alpha_h), work, SWEEPS - 1)
        src, dst = work, following
        for sweep in range(1, SWEEPS):
            last = sweep == SWEEPS - 1
            smooth_sweep(src, dst, SWEEPS - 1 - sweep, emit_term if last else None)
            src, dst = dst, src

        for hop in range(1, members):
            target = lax.rem(mem + hop, members)
            send(
                None,
                term.at[pl.ds(target * tile_rows, tile_rows)],
                pieces.at[step, hop],
                numbers["sum", step, hop],
                numbers["sum", step, hop],
                device(hop, 0, 0),
            )
        total = term[pl.ds(mem * tile_rows, tile_rows)]
        if step == 0:
            row_waits("kappa_far", kappa_o, HALO - SWEEPS, SWEEPS)
            row_waits("x", wx_o, HALO)
            pack_waits("packx", packx_in)
            for e in range(rows + 2 * HALO):
                g, j = divmod(e, GROUP)
                wx_h[e] = unpacked(lambda peer: packx_in[peer, g], j)
            for side, i, spot in others():
                if side is None:
                    await_in(None, cells_all.at[spot], numbers["cells", i])
                else:
                    await_in(has[side], cells_all.at[spot], numbers["cells_row", side] + i)
            for _, _, spot in others():
                hot(spot, cells_all[spot])
        for hop in range(1, members):
            await_in(None, pieces.at[step, hop], numbers["sum", step, hop])
            total = total + pieces[step, hop]

        flipped = jnp.transpose(total.reshape(spots, LANES))
        hot_rows, hot_cols = rows_hot[mine], cols_hot[mine]
        observed = jnp.zeros((LANES, slots), jnp.float32)
        for half in halves(flipped):
            observed = observed + jnp.dot(half, hot_rows, preferred_element_type=jnp.float32)
        observed = jnp.sum(
            observed * hot_cols.astype(jnp.float32), axis=0, keepdims=True
        )
        misfit = (observed - innovations) * masked_weight
        pulled = jnp.clip(misfit, -huber_edge, huber_edge) * masked_weight
        pulled_out[step] = pulled
        to_group(step, pulled_out.at[step], pulled_in.at[step], ("tile", step))
        tile = spread(mine, pulled)
        edge_out[step] = packed(lambda j: tile[j], tile_rows)

        force_o, edges = forcing_o.at[step], edge_in.at[step]
        for side in (-1, 1):
            near = mem - (0 if side < 0 else members - edge_tiles)
            inside = near < edge_tiles if side < 0 else near >= 0
            condition = jnp.logical_and(has[side], inside)
            spot = near + (edge_tiles + members if side < 0 else 0)
            for peer, lon_hop in enumerate(peers):
                for hop in range(members):
                    send(
                        condition,
                        edge_out.at[step],
                        edges.at[far(peer), spot],
                        numbers["corner_out", step, side, peer] + hop,
                        numbers["corner", step, -side, far(peer)] + near,
                        device(hop, side, lon_hop),
                    )
        for peer, lon_hop in enumerate(peers):
            for hop in range(members):
                send(
                    None,
                    edge_out.at[step],
                    edges.at[far(peer), edge_tiles + mem],
                    numbers["edge", step, peer, hop],
                    numbers["edge", step, far(peer), hop],
                    device(hop, 0, lon_hop),
                )
        force_o[pl.ds(HALO + mem * tile_rows, tile_rows)] = tile

        for side, i, spot in others():
            if side is None:
                await_in(None, pulled_in.at[step, spot], numbers["tile", step, i])
            else:
                await_in(has[side], pulled_in.at[step, spot], numbers["row", step, side] + i)
        for _, _, spot in others():
            force_o[pl.ds(spot * tile_rows, tile_rows)] = spread(spot, pulled_in[step, spot])
        for peer in range(len(peers)):
            for hop in range(members):
                source = lax.rem(mem + members - hop, members)
                await_in(
                    None, edges.at[peer, edge_tiles + source], numbers["edge", step, peer, hop]
                )
        for side in (-1, 1):
            for i in range(edge_tiles):
                spot = i + (0 if side < 0 else edge_tiles + members)
                for peer in range(len(peers)):
                    await_in(
                        has[side],
                        edges.at[peer, spot],
                        numbers["corner", step, side, peer] + i,
                    )

        margin = HALO - step * SWEEPS
        for e in range(HALO - margin, HALO + rows + margin):
            t, j = divmod(e, tile_rows)
            forcing_h[e] = unpacked(lambda peer: edges[peer, t], j)
        for a, b in chunks(margin):
            work_o[a:b] = wx_o[a:b] * force_o[a:b]
            work_h[a:b] = wx_h[a:b] * forcing_h[a:b]

        final = step == STEPS - 1
        inside_top = (lat > 0).astype(jnp.float32)
        inside_bottom = (lat < lat_count - 1).astype(jnp.float32)

        def emit_alpha(which, a, b, value):
            held = (alpha_o, alpha_h)[which]
            old = held[a:b]
            if final:
                fresh = ((1.0 - step_length) / step_length) * old - value
                for r in range(a, b):
                    out_ref[pl.ds(r - HALO, levels, stride=rows), :] = fresh[r - a]
                return
            fresh = old - step_length * (old + value)
            for r in range(a, b):
                row = fresh[r - a]
                if r < HALO:
                    row = row * inside_top
                elif r >= HALO + rows:
                    row = row * inside_bottom
                held[r] = row

        if step == 0:
            settle("alpha")
        src, dst = work, following
        for sweep in range(SWEEPS):
            last = sweep == SWEEPS - 1
            adjoint_sweep(
                src, dst, margin - 1 - sweep, emit_alpha if last else None, not (last and final)
            )
            src, dst = dst, src

    settle()


def fused(members, lat_count, lon_count, tile_rows, x, control, kappa, cells, counts, innov, prec):
    _, levels, rows, columns = x.shape
    peers = 1 if lon_count == 2 else 2
    edge_tiles = HALO // tile_rows
    slots = cells.shape[1]
    groups = rows // GROUP
    _, sent, received = copy_plan(members, peers, edge_tiles)
    vregs = lambda *lead: pltpu.VMEM(lead + (SUBLANES, LANES), jnp.float32)
    deep = rows + 2 * HALO
    tiles = members + 2 * edge_tiles
    vmem = pl.BlockSpec(memory_space=pltpu.VMEM)
    place = pl.BlockSpec(memory_space=pltpu.HBM)
    in_hbm = lambda array: pltpu.with_memory_space_constraint(array, pltpu.HBM)
    flat = lambda dtype: pltpu.VMEM((levels * rows, columns), dtype)
    out = pl.pallas_call(
        functools.partial(kernel, members, lat_count, lon_count, tile_rows),
        out_shape=jax.ShapeDtypeStruct((levels * rows, columns), jnp.float32),
        in_specs=[place] * 4 + [pl.BlockSpec(memory_space=pltpu.SMEM)] + [place] * 2,
        out_specs=vmem,
        scratch_shapes=[
            flat(x.dtype),
            flat(jnp.float32),
            flat(jnp.float32),
            pltpu.VMEM(cells.shape, cells.dtype),
            pltpu.VMEM(innov.shape, innov.dtype),
            pltpu.VMEM(prec.shape, prec.dtype),
            pltpu.SemaphoreType.DMA((6,)),
            flat(jnp.float32),
        ]
        + [vregs(deep)] * 10
        + [
            vregs(STEPS, deep),
            vregs(deep),
            vregs(groups, 2),
            vregs(peers, groups + 2, 2),
            vregs(groups),
            vregs(peers, groups + 2),
            vregs(STEPS),
            vregs(STEPS, peers, tiles),
            vregs(STEPS, rows),
            vregs(STEPS, members, tile_rows),
            pltpu.VMEM((STEPS, 1, slots), jnp.float32),
            pltpu.VMEM((STEPS, tiles, 1, slots), jnp.float32),
            pltpu.VMEM((tiles, 1, slots), jnp.int32),
            pltpu.VMEM((tiles, tile_rows * levels, slots), jnp.bfloat16),
            pltpu.VMEM((tiles, LANES, slots), jnp.bfloat16),
            pltpu.SemaphoreType.DMA((sent,)),
            pltpu.SemaphoreType.DMA((received,)),
        ],
        compiler_params=pltpu.CompilerParams(
            collective_id=0, has_side_effects=True, vmem_limit_bytes=24 * 2**20
        ),
    )(
        in_hbm(x.reshape(levels * rows, columns)),
        in_hbm(control.reshape(levels * rows, columns)),
        in_hbm(kappa.reshape(levels * rows, columns)),
        in_hbm(cells),
        counts,
        in_hbm(innov),
        in_hbm(prec),
    )
    return (step_length * out).reshape(1, levels, rows, columns)


def fits(members, lat_count, lon_count, x, cells):
    _, levels, rows, columns = x.shape
    tile_rows = rows // members
    return (
        levels == SUBLANES
        and columns == LANES
        and rows % members == 0
        and rows % GROUP == 0
        and rows >= 2 * HALO
        and HALO % tile_rows == 0
        and tile_rows <= GROUP
        and HALO // tile_rows <= members
        and lon_count > 1
        and cells.shape[0] == 1
    )


def on_device(members, lat_count, lon_count, x, control, kappa, cells, counts, innov, prec):
    if not fits(members, lat_count, lon_count, x, cells):
        return per_device(x, control, kappa, cells, counts, innov, prec)
    tile_rows = x.shape[2] // members
    return fused(
        members, lat_count, lon_count, tile_rows, x, control, kappa, cells, counts, innov, prec
    )


def solution(mesh):
    return jax.shard_map(
        functools.partial(
            on_device, mesh.shape["mem"], mesh.shape["lat"], mesh.shape["lon"]
        ),
        mesh=mesh,
        in_specs=(
            P("mem", None, "lat", "lon"),
            P("mem", None, "lat", "lon"),
            P(None, "lat", "lon"),
            P(("mem", "lat", "lon"), None),
            P(("mem", "lat", "lon")),
            P(("mem", "lat", "lon"), None),
            P(("mem", "lat", "lon"), None),
        ),
        out_specs=P("mem", None, "lat", "lon"),
        check_vma=False,
    )
```

```python
import functools
import math

import jax
import jax.numpy as jnp
from jax import lax
from jax.experimental import pallas as pl
from jax.experimental.pallas import tpu as pltpu
from jax.sharding import PartitionSpec as P

SWEEPS = 4
STEPS = 2


huber_edge = 1.5
step_length = 0.5


def with_halo(cells, sides, width):
    for axis, dim in sides:
        count = lax.axis_size(axis)
        head = lax.slice_in_dim(cells, 0, width, axis=dim)
        tail = lax.slice_in_dim(cells, cells.shape[dim] - width, cells.shape[dim], axis=dim)
        cells = jnp.concatenate(
            [
                lax.ppermute(tail, axis, [(i, (i + 1) % count) for i in range(count)]),
                cells,
                lax.ppermute(head, axis, [((i + 1) % count, i) for i in range(count)]),
            ],
            axis=dim,
        )
    return cells


def inside_rows(lat_rows, margin):
    first_row = lax.axis_index("lat") * lat_rows - margin
    global_rows = first_row + jnp.arange(lat_rows + 2 * margin, dtype=jnp.int32)
    total_rows = lat_rows * lax.axis_size("lat")
    return ((global_rows >= 0) & (global_rows < total_rows)).astype(jnp.float32)[None, :, None]


def stencil(padded):
    center = padded[:, 1:-1, 1:-1]
    laplace_term = (
        padded[:, :-2, 1:-1]
        + padded[:, 2:, 1:-1]
        + padded[:, 1:-1, :-2]
        + padded[:, 1:-1, 2:]
        - 4.0 * center
    )
    return (laplace_term, center)


def smooth_deep(state_field, kappa_rim):
    lat_rows = state_field.shape[1]
    padded = with_halo(state_field, (("lat", 1), ("lon", 2)), SWEEPS)
    padded = padded * inside_rows(lat_rows, SWEEPS)
    for sweep_index in range(SWEEPS):
        offset = sweep_index + 1
        local_kappa = kappa_rim[
            :, offset : kappa_rim.shape[1] - offset, offset : kappa_rim.shape[2] - offset
        ]
        laplace_term, center = stencil(padded)
        padded = (center + local_kappa * laplace_term) * inside_rows(lat_rows, SWEEPS - offset)
    return padded


def adjoint_deep(state_field, kappa_rim):
    lat_rows = state_field.shape[1]
    padded = with_halo(state_field, (("lat", 1), ("lon", 2)), SWEEPS)
    padded = padded * inside_rows(lat_rows, SWEEPS)
    for sweep_index in range(SWEEPS):
        local_kappa = kappa_rim[
            :,
            sweep_index : kappa_rim.shape[1] - sweep_index,
            sweep_index : kappa_rim.shape[2] - sweep_index,
        ]
        laplace_term, center = stencil(local_kappa * padded)
        padded = (padded[:, 1:-1, 1:-1] + laplace_term) * inside_rows(
            lat_rows, SWEEPS - sweep_index - 1
        )
    return padded


def per_device(
    perturbations, control, diffusivity, obs_cells, obs_counts, innovations, obs_precision
):
    members = lax.axis_size("mem")
    weight = 1.0 / math.sqrt(members - 1)
    member_x = perturbations[0]
    alpha_now = control[0]
    live_slots = (
        jnp.arange(obs_cells.shape[1], dtype=jnp.int32)[None, :] < obs_counts[:, None]
    ).astype(jnp.float32)
    masked_weight = obs_precision * live_slots
    kappa_rim = with_halo(diffusivity, (("lat", 1), ("lon", 2)), SWEEPS)
    for step_index in range(STEPS):
        smoothed = smooth_deep(alpha_now, kappa_rim)
        member_term = member_x.astype(jnp.float32) * smoothed
        owned_piece = lax.psum_scatter(member_term, "mem", scatter_dimension=1, tiled=True)
        increment = weight * owned_piece
        tile_cells = obs_cells[0]
        observed = increment.reshape(-1)[tile_cells]
        misfit = (observed - innovations[0]) * masked_weight[0]
        pulled = jnp.clip(misfit, -huber_edge, huber_edge) * masked_weight[0]
        tile_field = (
            jnp.zeros((increment.size,), jnp.float32)
            .at[tile_cells]
            .add(pulled)
            .reshape(increment.shape)
        )
        forcing = lax.all_gather(tile_field, "mem", axis=1, tiled=True)
        source = weight * member_x.astype(jnp.float32) * forcing
        gradient = alpha_now + adjoint_deep(source, kappa_rim)
        alpha_now = alpha_now - step_length * gradient
    return alpha_now[None]


LANES = 128
SUBLANES = 8
HALO = STEPS * SWEEPS
SLOT = 2 * HALO
GROUP = LANES // SLOT
MESH = pl.DeviceIdType.MESH


def copy_plan(members, peers, edge_tiles):
    keys = []
    for field in ("alpha", "kappa", "kappa_far", "x"):
        keys += [(field, "row", side) for side in (-1, 1)]
    for pack in ("pack", "packx"):
        keys += [(pack, side, peer) for side in (-1, 0, 1) for peer in range(peers)]
    keys += [("cells", hop) for hop in range(1, members)]
    for step in range(STEPS):
        keys += [("sum", step, hop) for hop in range(1, members)]
        keys += [("tile", step, hop) for hop in range(1, members)]
        keys += [("edge", step, peer, hop) for peer in range(peers) for hop in range(members)]
    numbers = {key: number for number, key in enumerate(keys)}
    received = len(keys)
    for side in (-1, 1):
        numbers["cells_row", side] = received
        received += edge_tiles
    for step in range(STEPS):
        for side in (-1, 1):
            numbers["row", step, side] = received
            received += edge_tiles
            for peer in range(peers):
                numbers["corner", step, side, peer] = received
                received += edge_tiles
    sent = len(keys)
    for side in (-1, 1):
        numbers["cells_out", side] = sent
        sent += members
    for step in range(STEPS):
        for side in (-1, 1):
            numbers["row_out", step, side] = sent
            sent += members
            for peer in range(peers):
                numbers["corner_out", step, side, peer] = sent
                sent += members
    return numbers, sent, received


def kernel(
    members,
    lat_count,
    lon_count,
    tile_rows,
    x_in,
    control_in,
    kappa_in,
    cells_in,
    counts_ref,
    innovations_in,
    precision_in,
    out_ref,
    x_ref,
    control_ref,
    kappa_ref,
    cells_ref,
    innovations_ref,
    precision_ref,
    load_sems,
    x_flat,
    alpha_o,
    alpha_h,
    kappa_o,
    kappa_h,
    wx_o,
    wx_h,
    work_o,
    work_h,
    next_o,
    next_h,
    forcing_o,
    forcing_h,
    pack_out,
    pack_in,
    packx_out,
    packx_in,
    edge_out,
    edge_in,
    terms,
    pieces,
    pulled_out,
    pulled_in,
    cells_all,
    rows_hot,
    cols_hot,
    send_sems,
    recv_sems,
):
    levels = SUBLANES
    rows = control_ref.shape[0] // levels
    slots = cells_ref.shape[1]
    groups = rows // GROUP
    edge_tiles = HALO // tile_rows
    peers = [1] if lon_count == 2 else [1, lon_count - 1]
    numbers, _, _ = copy_plan(members, len(peers), edge_tiles)
    weight = 1.0 / math.sqrt(members - 1)
    mem = lax.axis_index("mem")
    lat = lax.axis_index("lat")
    lon = lax.axis_index("lon")
    has = {-1: lat > 0, 0: None, 1: lat < lat_count - 1}

    def guarded(condition, run):
        if condition is None:
            run()
        else:
            pl.when(condition)(run)

    def device(mem_hop, lat_hop, lon_hop):
        return (
            lax.rem(mem + mem_hop, members),
            lat + lat_hop,
            lax.rem(lon + lon_hop, lon_count),
        )

    def far(peer):
        return len(peers) - 1 - peer

    def remote(src, dst, send_number, recv_number, target):
        return pltpu.make_async_remote_copy(
            src_ref=src,
            dst_ref=dst,
            send_sem=send_sems.at[send_number],
            recv_sem=recv_sems.at[recv_number],
            device_id=target,
            device_id_type=MESH,
        )

    pending = []

    def send(condition, src, dst, send_number, recv_number, target):
        guarded(condition, lambda: remote(src, dst, send_number, recv_number, target).start())
        pending.append((condition, src, send_number))

    def settle(name=None):
        kept = []
        for condition, src, number in pending:
            if name is None or number in (numbers[name, "row", -1], numbers[name, "row", 1]):
                guarded(
                    condition,
                    lambda: remote(src, src, number, 0, device(0, 0, peers[0])).wait_send(),
                )
            else:
                kept.append((condition, src, number))
        pending[:] = kept

    def await_in(condition, dst, recv_number):
        guarded(
            condition,
            lambda: remote(dst, dst, 0, recv_number, device(0, 0, peers[0])).wait_recv(),
        )

    loads = [
        pltpu.make_async_copy(src, dst, load_sems.at[number])
        for number, (src, dst) in enumerate(
            (
                (control_in, control_ref),
                (kappa_in, kappa_ref),
                (x_in, x_ref),
                (cells_in, cells_ref),
                (innovations_in, innovations_ref),
                (precision_in, precision_ref),
            )
        )
    ]
    for load in loads:
        load.start()

    barrier = pltpu.get_barrier_semaphore()
    for lat_hop in (0, -1, 1):
        def greet(lat_hop=lat_hop):
            for lon_hop in [0] + peers:
                for mem_hop in range(members if lon_hop == 0 else 1):
                    if (lat_hop, lon_hop, mem_hop) != (0, 0, 0):
                        pl.semaphore_signal(
                            barrier,
                            inc=1,
                            device_id=device(mem_hop, lat_hop, lon_hop),
                            device_id_type=MESH,
                        )
        guarded(has[lat_hop], greet)

    lane = lax.broadcasted_iota(jnp.int32, (1, SUBLANES, LANES), 2)
    lane2 = lane[0]

    for load in loads:
        load.wait()
    x_flat[...] = weight * x_ref[...].astype(jnp.float32)
    for r in range(rows):
        level_rows = pl.ds(r, levels, stride=rows)
        alpha_o[HALO + r] = control_ref[level_rows, :]
        kappa_o[HALO + r] = kappa_ref[level_rows, :]
        wx_o[HALO + r] = x_flat[level_rows, :]

    def packed(read, count):
        total = jnp.zeros((SUBLANES, LANES), jnp.float32)
        for j in range(count):
            shifted = pltpu.roll(read(j), (HALO + SLOT * j) % LANES, 1)
            total = jnp.where(lane2 // SLOT == j, shifted, total)
        return total

    def unpacked(read, j):
        shift = (LANES - HALO - SLOT * j) % LANES
        parts = [pltpu.roll(read(peer), shift, 1) if shift else read(peer) for peer in range(len(peers))]
        if len(parts) == 1:
            return parts[0]
        return jnp.where(lane2 < LANES // 2, parts[0], parts[1])

    for g in range(groups):
        base = HALO + g * GROUP
        pack_out[g, 0] = packed(lambda j: alpha_o[base + j], GROUP)
        pack_out[g, 1] = packed(lambda j: kappa_o[base + j], GROUP)
        packx_out[g] = packed(lambda j: wx_o[base + j], GROUP)

    zero_rows = jnp.zeros((HALO, SUBLANES, LANES), jnp.float32)
    for side in (-1, 1):
        start = 0 if side < 0 else HALO + rows
        group = 0 if side < 0 else groups + 1
        tile = 0 if side < 0 else edge_tiles + members

        def clear(start=start, group=group, tile=tile):
            for ref in (alpha_o, kappa_o, wx_o):
                ref[start : start + HALO] = zero_rows
            cells_all[tile : tile + edge_tiles] = jnp.zeros((edge_tiles, 1, slots), jnp.int32)
            for step in range(STEPS):
                pulled_in[step, tile : tile + edge_tiles] = jnp.zeros(
                    (edge_tiles, 1, slots), jnp.float32
                )
            for peer in range(len(peers)):
                pack_in[peer, group] = jnp.zeros((2, SUBLANES, LANES), jnp.float32)
                packx_in[peer, group] = jnp.zeros((SUBLANES, LANES), jnp.float32)
                for step in range(STEPS):
                    edge_in[step, peer, tile : tile + edge_tiles] = jnp.zeros(
                        (edge_tiles, SUBLANES, LANES), jnp.float32
                    )

        guarded(jnp.logical_not(has[side]), clear)

    greeted = len(peers) + members
    lat_near = 1 + (lat > 0).astype(jnp.int32) + (lat < lat_count - 1).astype(jnp.int32)
    pl.semaphore_wait(barrier, greeted * lat_near - 1)

    def row_copies(name, field, width, skip=0):
        for side in (-1, 1):
            source = HALO + skip if side < 0 else HALO + rows - width - skip
            target = HALO + rows + skip if side < 0 else HALO - width - skip
            send(
                has[side],
                field.at[pl.ds(source, width)],
                field.at[pl.ds(target, width)],
                numbers[name, "row", side],
                numbers[name, "row", -side],
                device(0, side, 0),
            )

    def row_waits(name, field, width, skip=0):
        for side in (-1, 1):
            start = HALO - width - skip if side < 0 else HALO + rows + skip
            await_in(has[side], field.at[pl.ds(start, width)], numbers[name, "row", side])

    def pack_copies(name, source, target):
        for side in (0, -1, 1):
            for peer, hop in enumerate(peers):
                if side == 0:
                    src, dst = source, target.at[far(peer), pl.ds(1, groups)]
                elif side < 0:
                    src, dst = source.at[0], target.at[far(peer), groups + 1]
                else:
                    src, dst = source.at[groups - 1], target.at[far(peer), 0]
                send(
                    has[side],
                    src,
                    dst,
                    numbers[name, side, peer],
                    numbers[name, -side, far(peer)],
                    device(0, side, hop),
                )

    def pack_waits(name, target):
        for side in (0, -1, 1):
            for peer in range(len(peers)):
                if side == 0:
                    dst = target.at[peer, pl.ds(1, groups)]
                else:
                    dst = target.at[peer, 0 if side < 0 else groups + 1]
                await_in(has[side], dst, numbers[name, side, peer])

    pack_copies("pack", pack_out, pack_in)
    row_copies("alpha", alpha_o, SWEEPS)
    row_copies("kappa", kappa_o, SWEEPS)
    pack_copies("packx", packx_out, packx_in)
    row_copies("kappa_far", kappa_o, HALO - SWEEPS, SWEEPS)
    row_copies("x", wx_o, HALO)

    def to_group(step, source, target, name):
        for hop in range(1, members):
            send(
                None,
                source,
                target.at[edge_tiles + mem],
                numbers[name + (hop,)],
                numbers[name + (hop,)],
                device(hop, 0, 0),
            )
        outs, ins = ("cells_out", "cells_row") if step is None else ("row_out", "row")
        key = () if step is None else (step,)
        for side in (-1, 1):
            near = mem - (0 if side < 0 else members - edge_tiles)
            inside = near < edge_tiles if side < 0 else near >= 0
            for hop in range(members):
                send(
                    jnp.logical_and(has[side], inside),
                    source,
                    target.at[near + (edge_tiles + members if side < 0 else 0)],
                    numbers[(outs,) + key + (side,)] + hop,
                    numbers[(ins,) + key + (-side,)] + near,
                    device(hop, side, 0),
                )

    def others():
        for hop in range(1, members):
            yield None, hop, edge_tiles + lax.rem(mem + members - hop, members)
        for side in (-1, 1):
            for i in range(edge_tiles):
                yield side, i, i + (0 if side < 0 else edge_tiles + members)

    to_group(None, cells_ref, cells_all, ("cells",))

    spots = tile_rows * levels

    def hot(spot, cells):
        column = lax.rem(cells, LANES)
        tile_row = lax.rem(lax.div(cells, LANES), tile_rows)
        level = lax.div(cells, LANES * tile_rows)
        place = tile_row * levels + level
        rows_hot[spot] = (
            lax.broadcasted_iota(jnp.int32, (spots, slots), 0) == place
        ).astype(jnp.float32).astype(jnp.bfloat16)
        cols_hot[spot] = (
            lax.broadcasted_iota(jnp.int32, (LANES, slots), 0) == column
        ).astype(jnp.float32).astype(jnp.bfloat16)

    def spread(spot, pulled):
        tile = jnp.zeros((spots, LANES), jnp.float32)
        for half in halves(pulled):
            tile = tile + lax.dot_general(
                rows_hot[spot] * half,
                cols_hot[spot],
                (((1,), (1,)), ((), ())),
                preferred_element_type=jnp.float32,
            )
        return tile.reshape(tile_rows, SUBLANES, LANES)

    mine = edge_tiles + mem
    hot(mine, cells_ref[...])
    live = (
        lax.broadcasted_iota(jnp.int32, (1, slots), 1) < counts_ref[0]
    ).astype(jnp.float32)
    masked_weight = precision_ref[...] * live
    innovations = innovations_ref[...]

    def halves(value):
        high = value.astype(jnp.bfloat16)
        return high, (value - high.astype(jnp.float32)).astype(jnp.bfloat16)

    first_lane, last_lane = lane == 0, lane == LANES - 1

    def sides(own, near):
        own_w, near_w = pltpu.roll(own, 1, 2), pltpu.roll(near, 1, 2)
        own_e, near_e = pltpu.roll(own, LANES - 1, 2), pltpu.roll(near, LANES - 1, 2)
        return (
            jnp.where(first_lane, near_w, own_w) + jnp.where(last_lane, near_e, own_e),
            jnp.where(first_lane, own_w, near_w) + jnp.where(last_lane, own_e, near_e),
        )

    def chunks(margin):
        first, last = HALO - margin, HALO + rows + margin
        return [(a, min(a + 8, last)) for a in range(first, last, 8)]

    def smooth_sweep(src, dst, margin, emit=None):
        for a, b in chunks(margin):
            own, near = src[0][a:b], src[1][a:b]
            beside = sides(own, near)
            for ref, value, both, kappa, out in (
                (src[0], own, beside[0], kappa_o, dst[0]),
                (src[1], near, beside[1], kappa_h, dst[1]),
            ):
                if emit is not None and ref is src[1]:
                    continue
                total = ref[a - 1 : b - 1] + ref[a + 1 : b + 1] + both
                value = value + kappa[a:b] * (total - 4.0 * value)
                if emit is None:
                    out[a:b] = value
                else:
                    emit(a, b, value)

    def adjoint_sweep(src, dst, margin, emit=None, near_too=True):
        for a, b in chunks(margin):
            scaled = [
                kappa[a - 1 : b + 1] * ref[a - 1 : b + 1]
                for ref, kappa in ((src[0], kappa_o), (src[1], kappa_h))
            ]
            beside = sides(scaled[0][1:-1], scaled[1][1:-1])
            for which in (0, 1):
                if which and not near_too:
                    continue
                t = scaled[which]
                value = src[which][a:b] + (t[:-2] + t[2:] + beside[which] - 4.0 * t[1:-1])
                if emit is None:
                    dst[which][a:b] = value
                else:
                    emit(which, a, b, value)

    work, following = (work_o, work_h), (next_o, next_h)

    row_waits("alpha", alpha_o, SWEEPS)
    row_waits("kappa", kappa_o, SWEEPS)
    pack_waits("pack", pack_in)
    for e in range(rows + 2 * HALO):
        g, j = divmod(e, GROUP)
        alpha_h[e] = unpacked(lambda peer: pack_in[peer, g, 0], j)
        kappa_h[e] = unpacked(lambda peer: pack_in[peer, g, 1], j)

    for step in range(STEPS):
        term = terms.at[step]

        def emit_term(a, b, value):
            term[a - HALO : b - HALO] = wx_o[a:b] * value

        smooth_sweep((alpha_o, alpha_h), work, SWEEPS - 1)
        src, dst = work, following
        for sweep in range(1, SWEEPS):
            last = sweep == SWEEPS - 1
            smooth_sweep(src, dst, SWEEPS - 1 - sweep, emit_term if last else None)
            src, dst = dst, src

        for hop in range(1, members):
            target = lax.rem(mem + hop, members)
            send(
                None,
                term.at[pl.ds(target * tile_rows, tile_rows)],
                pieces.at[step, hop],
                numbers["sum", step, hop],
                numbers["sum", step, hop],
                device(hop, 0, 0),
            )
        total = term[pl.ds(mem * tile_rows, tile_rows)]
        if step == 0:
            row_waits("kappa_far", kappa_o, HALO - SWEEPS, SWEEPS)
            row_waits("x", wx_o, HALO)
            pack_waits("packx", packx_in)
            for e in range(rows + 2 * HALO):
                g, j = divmod(e, GROUP)
                wx_h[e] = unpacked(lambda peer: packx_in[peer, g], j)
            for side, i, spot in others():
                if side is None:
                    await_in(None, cells_all.at[spot], numbers["cells", i])
                else:
                    await_in(has[side], cells_all.at[spot], numbers["cells_row", side] + i)
            for _, _, spot in others():
                hot(spot, cells_all[spot])
        for hop in range(1, members):
            await_in(None, pieces.at[step, hop], numbers["sum", step, hop])
            total = total + pieces[step, hop]

        flipped = jnp.transpose(total.reshape(spots, LANES))
        hot_rows, hot_cols = rows_hot[mine], cols_hot[mine]
        observed = jnp.zeros((LANES, slots), jnp.float32)
        for half in halves(flipped):
            observed = observed + jnp.dot(half, hot_rows, preferred_element_type=jnp.float32)
        observed = jnp.sum(
            observed * hot_cols.astype(jnp.float32), axis=0, keepdims=True
        )
        misfit = (observed - innovations) * masked_weight
        pulled = jnp.clip(misfit, -huber_edge, huber_edge) * masked_weight
        pulled_out[step] = pulled
        to_group(step, pulled_out.at[step], pulled_in.at[step], ("tile", step))
        tile = spread(mine, pulled)
        edge_out[step] = packed(lambda j: tile[j], tile_rows)

        force_o, edges = forcing_o.at[step], edge_in.at[step]
        for side in (-1, 1):
            near = mem - (0 if side < 0 else members - edge_tiles)
            inside = near < edge_tiles if side < 0 else near >= 0
            condition = jnp.logical_and(has[side], inside)
            spot = near + (edge_tiles + members if side < 0 else 0)
            for peer, lon_hop in enumerate(peers):
                for hop in range(members):
                    send(
                        condition,
                        edge_out.at[step],
                        edges.at[far(peer), spot],
                        numbers["corner_out", step, side, peer] + hop,
                        numbers["corner", step, -side, far(peer)] + near,
                        device(hop, side, lon_hop),
                    )
        for peer, lon_hop in enumerate(peers):
            for hop in range(members):
                send(
                    None,
                    edge_out.at[step],
                    edges.at[far(peer), edge_tiles + mem],
                    numbers["edge", step, peer, hop],
                    numbers["edge", step, far(peer), hop],
                    device(hop, 0, lon_hop),
                )
        force_o[pl.ds(HALO + mem * tile_rows, tile_rows)] = tile

        for side, i, spot in others():
            if side is None:
                await_in(None, pulled_in.at[step, spot], numbers["tile", step, i])
            else:
                await_in(has[side], pulled_in.at[step, spot], numbers["row", step, side] + i)
        for _, _, spot in others():
            force_o[pl.ds(spot * tile_rows, tile_rows)] = spread(spot, pulled_in[step, spot])
        for peer in range(len(peers)):
            for hop in range(members):
                source = lax.rem(mem + members - hop, members)
                await_in(
                    None, edges.at[peer, edge_tiles + source], numbers["edge", step, peer, hop]
                )
        for side in (-1, 1):
            for i in range(edge_tiles):
                spot = i + (0 if side < 0 else edge_tiles + members)
                for peer in range(len(peers)):
                    await_in(
                        has[side],
                        edges.at[peer, spot],
                        numbers["corner", step, side, peer] + i,
                    )

        margin = HALO - step * SWEEPS
        for e in range(HALO - margin, HALO + rows + margin):
            t, j = divmod(e, tile_rows)
            forcing_h[e] = unpacked(lambda peer: edges[peer, t], j)
        for a, b in chunks(margin):
            work_o[a:b] = wx_o[a:b] * force_o[a:b]
            work_h[a:b] = wx_h[a:b] * forcing_h[a:b]

        final = step == STEPS - 1
        inside_top = (lat > 0).astype(jnp.float32)
        inside_bottom = (lat < lat_count - 1).astype(jnp.float32)

        def emit_alpha(which, a, b, value):
            held = (alpha_o, alpha_h)[which]
            old = held[a:b]
            if final:
                fresh = ((1.0 - step_length) / step_length) * old - value
                for r in range(a, b):
                    out_ref[pl.ds(r - HALO, levels, stride=rows), :] = fresh[r - a]
                return
            fresh = old - step_length * (old + value)
            for r in range(a, b):
                row = fresh[r - a]
                if r < HALO:
                    row = row * inside_top
                elif r >= HALO + rows:
                    row = row * inside_bottom
                held[r] = row

        if step == 0:
            settle("alpha")
        src, dst = work, following
        for sweep in range(SWEEPS):
            last = sweep == SWEEPS - 1
            adjoint_sweep(
                src, dst, margin - 1 - sweep, emit_alpha if last else None, not (last and final)
            )
            src, dst = dst, src

    settle()


def fused(members, lat_count, lon_count, tile_rows, x, control, kappa, cells, counts, innov, prec):
    _, levels, rows, columns = x.shape
    peers = 1 if lon_count == 2 else 2
    edge_tiles = HALO // tile_rows
    slots = cells.shape[1]
    groups = rows // GROUP
    _, sent, received = copy_plan(members, peers, edge_tiles)
    vregs = lambda *lead: pltpu.VMEM(lead + (SUBLANES, LANES), jnp.float32)
    deep = rows + 2 * HALO
    tiles = members + 2 * edge_tiles
    vmem = pl.BlockSpec(memory_space=pltpu.VMEM)
    place = pl.BlockSpec(memory_space=pltpu.HBM)
    in_hbm = lambda array: pltpu.with_memory_space_constraint(array, pltpu.HBM)
    flat = lambda dtype: pltpu.VMEM((levels * rows, columns), dtype)
    out = pl.pallas_call(
        functools.partial(kernel, members, lat_count, lon_count, tile_rows),
        out_shape=jax.ShapeDtypeStruct((levels * rows, columns), jnp.float32),
        in_specs=[place] * 4 + [pl.BlockSpec(memory_space=pltpu.SMEM)] + [place] * 2,
        out_specs=vmem,
        scratch_shapes=[
            flat(x.dtype),
            flat(jnp.float32),
            flat(jnp.float32),
            pltpu.VMEM(cells.shape, cells.dtype),
            pltpu.VMEM(innov.shape, innov.dtype),
            pltpu.VMEM(prec.shape, prec.dtype),
            pltpu.SemaphoreType.DMA((6,)),
            flat(jnp.float32),
        ]
        + [vregs(deep)] * 10
        + [
            vregs(STEPS, deep),
            vregs(deep),
            vregs(groups, 2),
            vregs(peers, groups + 2, 2),
            vregs(groups),
            vregs(peers, groups + 2),
            vregs(STEPS),
            vregs(STEPS, peers, tiles),
            vregs(STEPS, rows),
            vregs(STEPS, members, tile_rows),
            pltpu.VMEM((STEPS, 1, slots), jnp.float32),
            pltpu.VMEM((STEPS, tiles, 1, slots), jnp.float32),
            pltpu.VMEM((tiles, 1, slots), jnp.int32),
            pltpu.VMEM((tiles, tile_rows * levels, slots), jnp.bfloat16),
            pltpu.VMEM((tiles, LANES, slots), jnp.bfloat16),
            pltpu.SemaphoreType.DMA((sent,)),
            pltpu.SemaphoreType.DMA((received,)),
        ],
        compiler_params=pltpu.CompilerParams(
            collective_id=0, has_side_effects=True, vmem_limit_bytes=24 * 2**20
        ),
    )(
        in_hbm(x.reshape(levels * rows, columns)),
        in_hbm(control.reshape(levels * rows, columns)),
        in_hbm(kappa.reshape(levels * rows, columns)),
        in_hbm(cells),
        counts,
        in_hbm(innov),
        in_hbm(prec),
    )
    return (step_length * out).reshape(1, levels, rows, columns)


def fits(members, lat_count, lon_count, x, cells):
    _, levels, rows, columns = x.shape
    tile_rows = rows // members
    return (
        levels == SUBLANES
        and columns == LANES
        and rows % members == 0
        and rows % GROUP == 0
        and rows >= 2 * HALO
        and HALO % tile_rows == 0
        and tile_rows <= GROUP
        and HALO // tile_rows <= members
        and lon_count > 1
        and cells.shape[0] == 1
    )


def picks_plan(members):

    keys = []
    for field in ("alpha", "kappa", "kappa_far", "x"):
        keys += [(field, side) for side in (-1, 1)]
    for pack in ("pack", "packx"):
        keys += [(pack, side) for side in (-1, 0, 1)]
    keys += [("obs", hop, lon_hop) for hop in range(members) for lon_hop in (0, 1)]
    keys += [("obs_edge", side, lon_hop) for side in (-1, 1) for lon_hop in (0, 1)]
    for step in range(STEPS):
        keys += [
            ("pick", step, hop, side, lon_hop)
            for hop in range(members)
            for side in (-1, 0, 1)
            for lon_hop in (0, 1)
        ]
    received = {key: number for number, key in enumerate(keys)}
    keys = [key for key in keys if key[0] != "obs_edge"] + [
        ("obs_edge", side, lon_hop, hop)
        for side in (-1, 1)
        for lon_hop in (0, 1)
        for hop in range(members)
    ]
    sent = {key: number for number, key in enumerate(keys)}
    return sent, received


def picks_kernel(
    members,
    lat_count,
    x_in,
    control_in,
    kappa_in,
    cells_in,
    counts_ref,
    innovations_in,
    precision_in,
    out_ref,
    x_ref,
    control_ref,
    kappa_ref,
    cells_ref,
    innovations_ref,
    precision_ref,
    load_sems,
    x_flat,
    alpha_o,
    alpha_h,
    kappa_o,
    kappa_h,
    wx_o,
    wx_h,
    work_o,
    work_h,
    next_o,
    next_h,
    pack_out,
    pack_in,
    packx_out,
    packx_in,
    term,
    obs_out,
    obs_in,
    weights_all,
    values_all,
    picks_out,
    picks_in,
    rows_hot,
    cols_hot,
    send_sems,
    recv_sems,
):
    levels = SUBLANES
    rows = control_ref.shape[0] // levels
    slots = cells_ref.shape[1]
    groups = rows // GROUP
    tile_rows = rows // members
    spots = tile_rows * levels
    sent, received = picks_plan(members)
    weight = 1.0 / math.sqrt(members - 1)
    mem = lax.axis_index("mem")
    lat = lax.axis_index("lat")
    lon = lax.axis_index("lon")
    has = {-1: lat > 0, 0: None, 1: lat < lat_count - 1}
    first, last = members, members + 1
    start_of = {t: HALO + t * tile_rows for t in range(members)}
    start_of[first], start_of[last] = 0, HALO + rows

    def guarded(condition, run):
        if condition is None:
            run()
        else:
            pl.when(condition)(run)

    def both(one, other):
        return other if one is None else jnp.logical_and(one, other)

    def device(mem_hop, lat_hop, lon_hop):
        return (
            lax.rem(mem + mem_hop, members) if mem_hop else mem,
            lat + lat_hop if lat_hop else lat,
            1 - lon if lon_hop else lon,
        )

    def remote(src, dst, send_number, recv_number, target):
        return pltpu.make_async_remote_copy(
            src_ref=src,
            dst_ref=dst,
            send_sem=send_sems.at[send_number],
            recv_sem=recv_sems.at[recv_number],
            device_id=target,
            device_id_type=MESH,
        )

    pending = []

    def send(condition, copies):
        def run():
            for src, dst, send_key, recv_key, target in copies:
                remote(src, dst, sent[send_key], received[recv_key], target).start()

        guarded(condition, run)
        pending.append((condition, [(src, key) for src, _, key, _, _ in copies]))

    def settle(name=None):
        kept = []
        for condition, copies in pending:
            chosen = [c for c in copies if name is None or c[1][0] == name]
            others = [c for c in copies if not (name is None or c[1][0] == name)]

            def run(chosen=chosen):
                for src, key in chosen:
                    remote(src, src, sent[key], 0, device(0, 0, 1)).wait_send()

            if chosen:
                guarded(condition, run)
            if others:
                kept.append((condition, others))
        pending[:] = kept

    def await_in(condition, arrivals):
        def run():
            for dst, key in arrivals:
                remote(dst, dst, 0, received[key], device(0, 0, 1)).wait_recv()

        guarded(condition, run)

    loads = [
        pltpu.make_async_copy(src, dst, load_sems.at[number])
        for number, (src, dst) in enumerate(
            (
                (control_in, control_ref),
                (kappa_in, kappa_ref),
                (x_in, x_ref),
                (cells_in, cells_ref),
                (innovations_in, innovations_ref),
                (precision_in, precision_ref),
            )
        )
    ]
    for load in loads:
        load.start()

    barrier = pltpu.get_barrier_semaphore()

    def greet(*hops):
        pl.semaphore_signal(barrier, inc=1, device_id=device(*hops), device_id_type=MESH)

    for side in (-1, 1):

        def greet_side(side=side):
            for lon_hop in (1, 0):
                greet(0, side, lon_hop)

        guarded(has[side], greet_side)
    greet(0, 0, 1)
    for hop in range(1, members):
        greet(hop, 0, 0)

    lane = lax.broadcasted_iota(jnp.int32, (1, SUBLANES, LANES), 2)
    lane2 = lane[0]

    def packed(read, count):
        total = jnp.zeros((SUBLANES, LANES), jnp.float32)
        for j in range(count):
            shifted = pltpu.roll(read(j), (HALO + SLOT * j) % LANES, 1)
            total = jnp.where(lane2 // SLOT == j, shifted, total)
        return total

    def unpacked(value, j):
        shift = (LANES - HALO - SLOT * j) % LANES
        return pltpu.roll(value, shift, 1) if shift else value

    def lay_out(source, target):
        for r in range(rows):
            value = source[pl.ds(r, levels, stride=rows), :]
            target[HALO + r] = value

    loads[0].wait()
    lay_out(control_ref, alpha_o)
    for g in range(groups):
        pack_out[g, 0] = packed(lambda j: alpha_o[HALO + g * GROUP + j], GROUP)
    loads[1].wait()
    lay_out(kappa_ref, kappa_o)
    for g in range(groups):
        pack_out[g, 1] = packed(lambda j: kappa_o[HALO + g * GROUP + j], GROUP)

    near_lat = (lat > 0).astype(jnp.int32) + (lat < lat_count - 1).astype(jnp.int32)
    pl.semaphore_wait(barrier, members + 2 * near_lat)

    def row_copy(name, field, width, side, skip=0):
        source = HALO + skip if side < 0 else HALO + rows - width - skip
        target = HALO + rows + skip if side < 0 else HALO - width - skip
        return (
            field.at[pl.ds(source, width)],
            field.at[pl.ds(target, width)],
            (name, side),
            (name, -side),
            device(0, side, 0),
        )

    def row_arrival(name, field, width, side, skip=0):
        start = HALO - width - skip if side < 0 else HALO + rows + skip
        return field.at[pl.ds(start, width)], (name, side)

    def pack_copy(name, source, target, side):
        if side == 0:
            src, dst = source, target.at[pl.ds(1, groups)]
        elif side < 0:
            src, dst = source.at[0], target.at[groups + 1]
        else:
            src, dst = source.at[groups - 1], target.at[0]
        return src, dst, (name, side), (name, -side), device(0, side, 1)

    def pack_arrival(name, target, side):
        if side == 0:
            return target.at[pl.ds(1, groups)], (name, side)
        return target.at[0 if side < 0 else groups + 1], (name, side)

    for side in (-1, 1):
        send(has[side], [pack_copy("pack", pack_out, pack_in, side)])
    send(None, [pack_copy("pack", pack_out, pack_in, 0)])
    for side in (-1, 1):
        send(
            has[side],
            [
                row_copy("alpha", alpha_o, SWEEPS, side),
                row_copy("kappa", kappa_o, SWEEPS, side),
            ],
        )

    for load in loads[3:]:
        load.wait()
    cells = cells_ref[...]
    column = lax.rem(cells, LANES)
    tile_row = lax.rem(lax.div(cells, LANES), tile_rows)
    level = lax.div(cells, LANES * tile_rows)
    live = (
        lax.broadcasted_iota(jnp.int32, (1, slots), 1) < counts_ref[0]
    ).astype(jnp.float32)
    my_obs = jnp.concatenate(
        [
            column.astype(jnp.float32),
            (tile_row * levels + level).astype(jnp.float32),
            precision_ref[...] * live,
            innovations_ref[...],
        ],
        axis=0,
    )
    obs_out[...] = my_obs
    obs_in[0, mem] = my_obs
    send(
        None,
        [
            (obs_out, obs_in.at[0, mem], ("obs", hop, 0), ("obs", hop, 0), device(hop, 0, 0))
            for hop in range(1, members)
        ]
        + [(obs_out, obs_in.at[1, mem], ("obs", 0, 1), ("obs", 0, 1), device(0, 0, 1))],
    )
    outer = {-1: mem == 0, 1: mem == members - 1}

    def obs_edge_copies(side, hops):
        return [
            (
                obs_out,
                obs_in.at[lon_hop, last if side < 0 else first],
                ("obs_edge", side, lon_hop, hop),
                ("obs_edge", -side, lon_hop),
                device(hop, side, lon_hop),
            )
            for lon_hop in (1, 0)
            for hop in hops
        ]

    for side in (-1, 1):
        send(both(has[side], outer[side]), obs_edge_copies(side, [0]))

    loads[2].wait()
    x_flat[...] = weight * x_ref[...].astype(jnp.float32)
    lay_out(x_flat, wx_o)
    for g in range(groups):
        packx_out[g] = packed(lambda j: wx_o[HALO + g * GROUP + j], GROUP)
    for side in (-1, 1):
        send(
            has[side],
            [
                pack_copy("packx", packx_out, packx_in, side),
                row_copy("kappa_far", kappa_o, HALO - SWEEPS, side, SWEEPS),
                row_copy("x", wx_o, HALO, side),
            ],
        )
    send(None, [pack_copy("packx", packx_out, packx_in, 0)])

    zero_rows = jnp.zeros((HALO, SUBLANES, LANES), jnp.float32)
    for side in (-1, 1):

        def clear(side=side):
            start = 0 if side < 0 else HALO + rows
            group = 0 if side < 0 else groups + 1
            tile = first if side < 0 else last
            for ref in (alpha_o, kappa_o, wx_o):
                ref[start : start + HALO] = zero_rows
            pack_in[group] = jnp.zeros((2, SUBLANES, LANES), jnp.float32)
            packx_in[group] = jnp.zeros((SUBLANES, LANES), jnp.float32)
            for lon_hop in (0, 1):
                obs_in[lon_hop, tile] = jnp.zeros((4, slots), jnp.float32)
                for step in range(STEPS):
                    for hop in range(members):
                        picks_in[step, hop, lon_hop, tile : tile + 1] = jnp.zeros(
                            (1, slots), jnp.float32
                        )

        guarded(jnp.logical_not(has[side]), clear)

    lane_of = lax.broadcasted_iota(jnp.int32, (LANES, slots), 0).astype(jnp.float32)
    spot_of = lax.broadcasted_iota(jnp.int32, (spots, slots), 0).astype(jnp.float32)

    def hot(lon_hop, tile):
        place = obs_in.at[lon_hop, tile]
        rows_hot[lon_hop, tile] = (
            (spot_of == place[1:2, :]).astype(jnp.float32).astype(jnp.bfloat16)
        )
        cols = (lane_of == place[0:1, :]).astype(jnp.float32).astype(jnp.bfloat16)
        cols_hot[lon_hop, tile] = cols
        weights_all[lon_hop, tile : tile + 1, :] = place[2:3, :]
        values_all[lon_hop, tile : tile + 1, :] = place[3:4, :]

    def halves(value):
        high = value.astype(jnp.bfloat16)
        return high, (value - high.astype(jnp.float32)).astype(jnp.bfloat16)

    first_lane, last_lane = lane == 0, lane == LANES - 1

    def sides(own, near):
        own_w, near_w = pltpu.roll(own, 1, 2), pltpu.roll(near, 1, 2)
        own_e, near_e = pltpu.roll(own, LANES - 1, 2), pltpu.roll(near, LANES - 1, 2)
        return (
            jnp.where(first_lane, near_w, own_w) + jnp.where(last_lane, near_e, own_e),
            jnp.where(first_lane, own_w, near_w) + jnp.where(last_lane, own_e, near_e),
        )

    def chunks(margin):
        begin, end = HALO - margin, HALO + rows + margin
        return [(a, min(a + 8, end)) for a in range(begin, end, 8)]

    def smooth_sweep(src, dst, margin, emit=None):
        for a, b in chunks(margin):
            own, near = src[0][a:b], src[1][a:b]
            beside = sides(own, near)
            for ref, value, ends, kappa, out in (
                (src[0], own, beside[0], kappa_o, dst[0]),
                (src[1], near, beside[1], kappa_h, dst[1]),
            ):
                if emit is not None and ref is src[1]:
                    continue
                total = ref[a - 1 : b - 1] + ref[a + 1 : b + 1] + ends
                value = value + kappa[a:b] * (total - 4.0 * value)
                if emit is None:
                    out[a:b] = value
                else:
                    emit(a, b, value)

    def adjoint_sweep(src, dst, margin, emit=None, near_too=True):
        for a, b in chunks(margin):
            scaled = [
                kappa[a - 1 : b + 1] * ref[a - 1 : b + 1]
                for ref, kappa in ((src[0], kappa_o), (src[1], kappa_h))
            ]
            beside = sides(scaled[0][1:-1], scaled[1][1:-1])
            for which in (0, 1):
                if which and not near_too:
                    continue
                t = scaled[which]
                value = src[which][a:b] + (t[:-2] + t[2:] + beside[which] - 4.0 * t[1:-1])
                if emit is None:
                    dst[which][a:b] = value
                else:
                    emit(which, a, b, value)

    work, following = (work_o, work_h), (next_o, next_h)

    for hop in range(1, members):
        await_in(None, [(obs_in.at[0, lax.rem(mem + members - hop, members)], ("obs", hop, 0))])
    for tile in range(members):
        hot(0, tile)

    for side in (-1, 1):
        await_in(
            has[side],
            [
                row_arrival("alpha", alpha_o, SWEEPS, side),
                row_arrival("kappa", kappa_o, SWEEPS, side),
                pack_arrival("pack", pack_in, side),
            ],
        )
    await_in(None, [pack_arrival("pack", pack_in, 0)])

    send(
        None,
        [
            (obs_out, obs_in.at[1, mem], ("obs", hop, 1), ("obs", hop, 1), device(hop, 0, 1))
            for hop in range(1, members)
        ],
    )
    for side in (-1, 1):
        send(both(has[side], outer[side]), obs_edge_copies(side, range(1, members)))

    for e in range(HALO - SWEEPS, rows + HALO + SWEEPS):
        g, j = divmod(e, GROUP)
        alpha_h[e] = unpacked(pack_in[g, 0], j)
        kappa_h[e] = unpacked(pack_in[g, 1], j)

    for step in range(STEPS):

        def emit_term(a, b, value):
            term[a - HALO : b - HALO] = wx_o[a:b] * value

        smooth_sweep((alpha_o, alpha_h), work, SWEEPS - 1)
        src, dst = work, following
        for sweep in range(1, SWEEPS):
            smooth_sweep(
                src, dst, SWEEPS - 1 - sweep, emit_term if sweep == SWEEPS - 1 else None
            )
            src, dst = dst, src

        for tile in range(members):
            flat = term[tile * tile_rows : (tile + 1) * tile_rows].reshape(spots, LANES)
            high, low = halves(flat)
            cols = cols_hot[0, tile]
            picked = jnp.dot(high, cols, preferred_element_type=jnp.float32) + jnp.dot(
                low, cols, preferred_element_type=jnp.float32
            )
            picks = jnp.sum(
                picked * rows_hot[0, tile].astype(jnp.float32), axis=0, keepdims=True
            )
            picks_out[step, tile : tile + 1, :] = picks

        def pick_copy(hop, side, lon_hop):
            target = picks_in.at[step, hop, lon_hop]
            if side == 0:
                src, dst = picks_out.at[step], target.at[pl.ds(0, members)]
            elif side < 0:
                src, dst = picks_out.at[step, pl.ds(0, 1)], target.at[pl.ds(last, 1)]
            else:
                src = picks_out.at[step, pl.ds(members - 1, 1)]
                dst = target.at[pl.ds(first, 1)]
            return (
                src,
                dst,
                ("pick", step, hop, side, lon_hop),
                ("pick", step, hop, -side, lon_hop),
                device(hop, side, lon_hop),
            )

        for side in (-1, 1):
            send(
                has[side],
                [pick_copy(hop, side, lon_hop) for lon_hop in (1, 0) for hop in range(members)],
            )
        send(None, [pick_copy(hop, 0, 1) for hop in range(members)])
        send(None, [pick_copy(hop, 0, 0) for hop in range(1, members)])

        if step == 0:
            for side in (-1, 1):
                await_in(
                    has[side],
                    [
                        row_arrival("kappa_far", kappa_o, HALO - SWEEPS, side, SWEEPS),
                        row_arrival("x", wx_o, HALO, side),
                        pack_arrival("packx", packx_in, side),
                    ],
                )
            await_in(None, [pack_arrival("packx", packx_in, 0)])
            for e in range(rows + 2 * HALO):
                g, j = divmod(e, GROUP)
                wx_h[e] = unpacked(packx_in[g], j)
                if not HALO - SWEEPS <= e < rows + HALO + SWEEPS:
                    kappa_h[e] = unpacked(pack_in[g, 1], j)
            for side, tile in ((-1, first), (1, last)):
                for lon_hop in (0, 1):
                    await_in(
                        has[side], [(obs_in.at[lon_hop, tile], ("obs_edge", side, lon_hop))]
                    )
            for hop in range(members):
                source = lax.rem(mem + members - hop, members)
                await_in(None, [(obs_in.at[1, source], ("obs", hop, 1))])
            for lon_hop in (0, 1):
                for tile in range(members + 2):
                    if (lon_hop, tile) not in [(0, t) for t in range(members)]:
                        hot(lon_hop, tile)
        if step == STEPS - 1:
            settle()

        def pulled_rows(lon_hop, a, b, observed=None):
            total = observed
            for hop in range(members):
                if hop == 0 and observed is not None:
                    continue
                piece = picks_in[step, hop, lon_hop, a:b, :]
                total = piece if total is None else total + piece
            masked_weight = weights_all[lon_hop, a:b, :]
            misfit = (total - values_all[lon_hop, a:b, :]) * masked_weight
            return halves(jnp.clip(misfit, -huber_edge, huber_edge) * masked_weight)

        def spread(lon_hop, tile, pulled, at):
            hot_rows = rows_hot[lon_hop, tile]
            left = jnp.concatenate(
                [hot_rows * half[at : at + 1, :] for half in pulled], axis=0
            )
            field = lax.dot_general(
                left,
                cols_hot[lon_hop, tile],
                (((1,), (1,)), ((), ())),
                preferred_element_type=jnp.float32,
            )
            field = (field[:spots] + field[spots:]).reshape(tile_rows, SUBLANES, LANES)
            a = start_of[tile]
            b = a + tile_rows
            (work_o, work_h)[lon_hop][a:b] = (wx_o, wx_h)[lon_hop][a:b] * field

        for lon_hop in (0, 1):
            await_in(
                None,
                [
                    (
                        picks_in.at[step, hop, lon_hop, pl.ds(0, members)],
                        ("pick", step, hop, 0, lon_hop),
                    )
                    for hop in range(members)
                    if (hop, lon_hop) != (0, 0)
                ],
            )
            pulled = pulled_rows(
                lon_hop, 0, members, picks_out[step] if lon_hop == 0 else None
            )
            for tile in range(members):
                spread(lon_hop, tile, pulled, tile)
        for side, tile in ((-1, first), (1, last)):
            await_in(
                has[side],
                [
                    (
                        picks_in.at[step, hop, lon_hop, pl.ds(tile, 1)],
                        ("pick", step, hop, side, lon_hop),
                    )
                    for hop in range(members)
                    for lon_hop in (0, 1)
                ],
            )
        for lon_hop in (0, 1):
            pulled = pulled_rows(lon_hop, first, last + 1)
            for tile in (first, last):
                spread(lon_hop, tile, pulled, tile - first)

        margin = HALO - step * SWEEPS
        final = step == STEPS - 1
        inside_top = (lat > 0).astype(jnp.float32)
        inside_bottom = (lat < lat_count - 1).astype(jnp.float32)

        def emit_alpha(which, a, b, value):
            held = (alpha_o, alpha_h)[which]
            old = held[a:b]
            if final:
                fresh = ((1.0 - step_length) / step_length) * old - value
                for r in range(a, b):
                    out_ref[pl.ds(r - HALO, levels, stride=rows), :] = fresh[r - a]
                return
            fresh = old - step_length * (old + value)
            for r in range(a, b):
                row = fresh[r - a]
                if r < HALO:
                    row = row * inside_top
                elif r >= HALO + rows:
                    row = row * inside_bottom
                held[r] = row

        if step == 0:
            settle("alpha")
        src, dst = work, following
        for sweep in range(SWEEPS):
            ends = sweep == SWEEPS - 1
            adjoint_sweep(
                src, dst, margin - 1 - sweep, emit_alpha if ends else None, not (ends and final)
            )
            src, dst = dst, src


def fused_picks(members, lat_count, x, control, kappa, cells, counts, innov, prec):
    _, levels, rows, columns = x.shape
    slots = cells.shape[1]
    groups = rows // GROUP
    spots = rows // members * levels
    sent, received = picks_plan(members)
    vregs = lambda *lead: pltpu.VMEM(lead + (SUBLANES, LANES), jnp.float32)
    floats = lambda *shape: pltpu.VMEM(shape, jnp.float32)
    deep = rows + 2 * HALO
    tiles = members + 2
    place = pl.BlockSpec(memory_space=pltpu.HBM)
    in_hbm = lambda array: pltpu.with_memory_space_constraint(array, pltpu.HBM)
    flat = lambda dtype: pltpu.VMEM((levels * rows, columns), dtype)
    out = pl.pallas_call(
        functools.partial(picks_kernel, members, lat_count),
        out_shape=jax.ShapeDtypeStruct((levels * rows, columns), jnp.float32),
        in_specs=[place] * 4 + [pl.BlockSpec(memory_space=pltpu.SMEM)] + [place] * 2,
        out_specs=pl.BlockSpec(memory_space=pltpu.VMEM),
        scratch_shapes=[
            flat(x.dtype),
            flat(jnp.float32),
            flat(jnp.float32),
            pltpu.VMEM(cells.shape, cells.dtype),
            floats(*innov.shape),
            floats(*prec.shape),
            pltpu.SemaphoreType.DMA((6,)),
            flat(jnp.float32),
        ]
        + [vregs(deep)] * 10
        + [
            vregs(groups, 2),
            vregs(groups + 2, 2),
            vregs(groups),
            vregs(groups + 2),
            vregs(rows),
            floats(4, slots),
            floats(2, tiles, 4, slots),
            floats(2, tiles, slots),
            floats(2, tiles, slots),
            floats(STEPS, members, slots),
            floats(STEPS, members, 2, tiles, slots),
            pltpu.VMEM((2, tiles, spots, slots), jnp.bfloat16),
            pltpu.VMEM((2, tiles, LANES, slots), jnp.bfloat16),
            pltpu.SemaphoreType.DMA((len(sent),)),
            pltpu.SemaphoreType.DMA((len(received),)),
        ],
        compiler_params=pltpu.CompilerParams(
            collective_id=1, has_side_effects=True, vmem_limit_bytes=24 * 2**20
        ),
    )(
        in_hbm(x.reshape(levels * rows, columns)),
        in_hbm(control.reshape(levels * rows, columns)),
        in_hbm(kappa.reshape(levels * rows, columns)),
        in_hbm(cells),
        counts,
        in_hbm(innov),
        in_hbm(prec),
    )
    return (step_length * out).reshape(1, levels, rows, columns)


def fits_picks(members, lat_count, lon_count, x, cells):
    return (
        fits(members, lat_count, lon_count, x, cells)
        and lon_count == 2
        and members <= 4
        and x.shape[2] // members == HALO == GROUP
        and cells.shape[1] % LANES == 0
    )


def on_device(members, lat_count, lon_count, x, control, kappa, cells, counts, innov, prec):
    if not fits(members, lat_count, lon_count, x, cells):
        return per_device(x, control, kappa, cells, counts, innov, prec)
    if fits_picks(members, lat_count, lon_count, x, cells):
        return fused_picks(members, lat_count, x, control, kappa, cells, counts, innov, prec)
    tile_rows = x.shape[2] // members
    return fused(
        members, lat_count, lon_count, tile_rows, x, control, kappa, cells, counts, innov, prec
    )


def solution(mesh):
    return jax.shard_map(
        functools.partial(
            on_device, mesh.shape["mem"], mesh.shape["lat"], mesh.shape["lon"]
        ),
        mesh=mesh,
        in_specs=(
            P("mem", None, "lat", "lon"),
            P("mem", None, "lat", "lon"),
            P(None, "lat", "lon"),
            P(("mem", "lat", "lon"), None),
            P(("mem", "lat", "lon")),
            P(("mem", "lat", "lon"), None),
            P(("mem", "lat", "lon"), None),
        ),
        out_specs=P("mem", None, "lat", "lon"),
        check_vma=False,
    )
```

```python
import functools
import math

import jax
import jax.numpy as jnp
from jax import lax
from jax.experimental import pallas as pl
from jax.experimental.pallas import tpu as pltpu
from jax.sharding import PartitionSpec as P

SWEEPS = 4
STEPS = 2


huber_edge = 1.5
step_length = 0.5


def with_halo(cells, sides, width):
    for axis, dim in sides:
        count = lax.axis_size(axis)
        head = lax.slice_in_dim(cells, 0, width, axis=dim)
        tail = lax.slice_in_dim(cells, cells.shape[dim] - width, cells.shape[dim], axis=dim)
        cells = jnp.concatenate(
            [
                lax.ppermute(tail, axis, [(i, (i + 1) % count) for i in range(count)]),
                cells,
                lax.ppermute(head, axis, [((i + 1) % count, i) for i in range(count)]),
            ],
            axis=dim,
        )
    return cells


def inside_rows(lat_rows, margin):
    first_row = lax.axis_index("lat") * lat_rows - margin
    global_rows = first_row + jnp.arange(lat_rows + 2 * margin, dtype=jnp.int32)
    total_rows = lat_rows * lax.axis_size("lat")
    return ((global_rows >= 0) & (global_rows < total_rows)).astype(jnp.float32)[None, :, None]


def stencil(padded):
    center = padded[:, 1:-1, 1:-1]
    laplace_term = (
        padded[:, :-2, 1:-1]
        + padded[:, 2:, 1:-1]
        + padded[:, 1:-1, :-2]
        + padded[:, 1:-1, 2:]
        - 4.0 * center
    )
    return (laplace_term, center)


def smooth_deep(state_field, kappa_rim):
    lat_rows = state_field.shape[1]
    padded = with_halo(state_field, (("lat", 1), ("lon", 2)), SWEEPS)
    padded = padded * inside_rows(lat_rows, SWEEPS)
    for sweep_index in range(SWEEPS):
        offset = sweep_index + 1
        local_kappa = kappa_rim[
            :, offset : kappa_rim.shape[1] - offset, offset : kappa_rim.shape[2] - offset
        ]
        laplace_term, center = stencil(padded)
        padded = (center + local_kappa * laplace_term) * inside_rows(lat_rows, SWEEPS - offset)
    return padded


def adjoint_deep(state_field, kappa_rim):
    lat_rows = state_field.shape[1]
    padded = with_halo(state_field, (("lat", 1), ("lon", 2)), SWEEPS)
    padded = padded * inside_rows(lat_rows, SWEEPS)
    for sweep_index in range(SWEEPS):
        local_kappa = kappa_rim[
            :,
            sweep_index : kappa_rim.shape[1] - sweep_index,
            sweep_index : kappa_rim.shape[2] - sweep_index,
        ]
        laplace_term, center = stencil(local_kappa * padded)
        padded = (padded[:, 1:-1, 1:-1] + laplace_term) * inside_rows(
            lat_rows, SWEEPS - sweep_index - 1
        )
    return padded


def per_device(
    perturbations, control, diffusivity, obs_cells, obs_counts, innovations, obs_precision
):
    members = lax.axis_size("mem")
    weight = 1.0 / math.sqrt(members - 1)
    member_x = perturbations[0]
    alpha_now = control[0]
    live_slots = (
        jnp.arange(obs_cells.shape[1], dtype=jnp.int32)[None, :] < obs_counts[:, None]
    ).astype(jnp.float32)
    masked_weight = obs_precision * live_slots
    kappa_rim = with_halo(diffusivity, (("lat", 1), ("lon", 2)), SWEEPS)
    for step_index in range(STEPS):
        smoothed = smooth_deep(alpha_now, kappa_rim)
        member_term = member_x.astype(jnp.float32) * smoothed
        owned_piece = lax.psum_scatter(member_term, "mem", scatter_dimension=1, tiled=True)
        increment = weight * owned_piece
        tile_cells = obs_cells[0]
        observed = increment.reshape(-1)[tile_cells]
        misfit = (observed - innovations[0]) * masked_weight[0]
        pulled = jnp.clip(misfit, -huber_edge, huber_edge) * masked_weight[0]
        tile_field = (
            jnp.zeros((increment.size,), jnp.float32)
            .at[tile_cells]
            .add(pulled)
            .reshape(increment.shape)
        )
        forcing = lax.all_gather(tile_field, "mem", axis=1, tiled=True)
        source = weight * member_x.astype(jnp.float32) * forcing
        gradient = alpha_now + adjoint_deep(source, kappa_rim)
        alpha_now = alpha_now - step_length * gradient
    return alpha_now[None]


LANES = 128
SUBLANES = 8
HALO = STEPS * SWEEPS
SLOT = 2 * HALO
GROUP = LANES // SLOT
MESH = pl.DeviceIdType.MESH


def copy_plan(members, peers, edge_tiles):
    keys = []
    for field in ("alpha", "kappa", "kappa_far", "x"):
        keys += [(field, "row", side) for side in (-1, 1)]
    for pack in ("pack", "packx"):
        keys += [(pack, side, peer) for side in (-1, 0, 1) for peer in range(peers)]
    keys += [("cells", hop) for hop in range(1, members)]
    for step in range(STEPS):
        keys += [("sum", step, hop) for hop in range(1, members)]
        keys += [("tile", step, hop) for hop in range(1, members)]
        keys += [("edge", step, peer, hop) for peer in range(peers) for hop in range(members)]
    numbers = {key: number for number, key in enumerate(keys)}
    received = len(keys)
    for side in (-1, 1):
        numbers["cells_row", side] = received
        received += edge_tiles
    for step in range(STEPS):
        for side in (-1, 1):
            numbers["row", step, side] = received
            received += edge_tiles
            for peer in range(peers):
                numbers["corner", step, side, peer] = received
                received += edge_tiles
    sent = len(keys)
    for side in (-1, 1):
        numbers["cells_out", side] = sent
        sent += members
    for step in range(STEPS):
        for side in (-1, 1):
            numbers["row_out", step, side] = sent
            sent += members
            for peer in range(peers):
                numbers["corner_out", step, side, peer] = sent
                sent += members
    return numbers, sent, received


def kernel(
    members,
    lat_count,
    lon_count,
    tile_rows,
    x_in,
    control_in,
    kappa_in,
    cells_in,
    counts_ref,
    innovations_in,
    precision_in,
    out_ref,
    x_ref,
    control_ref,
    kappa_ref,
    cells_ref,
    innovations_ref,
    precision_ref,
    load_sems,
    x_flat,
    alpha_o,
    alpha_h,
    kappa_o,
    kappa_h,
    wx_o,
    wx_h,
    work_o,
    work_h,
    next_o,
    next_h,
    forcing_o,
    forcing_h,
    pack_out,
    pack_in,
    packx_out,
    packx_in,
    edge_out,
    edge_in,
    terms,
    pieces,
    pulled_out,
    pulled_in,
    cells_all,
    rows_hot,
    cols_hot,
    send_sems,
    recv_sems,
):
    levels = SUBLANES
    rows = control_ref.shape[0] // levels
    slots = cells_ref.shape[1]
    groups = rows // GROUP
    edge_tiles = HALO // tile_rows
    peers = [1] if lon_count == 2 else [1, lon_count - 1]
    numbers, _, _ = copy_plan(members, len(peers), edge_tiles)
    weight = 1.0 / math.sqrt(members - 1)
    mem = lax.axis_index("mem")
    lat = lax.axis_index("lat")
    lon = lax.axis_index("lon")
    has = {-1: lat > 0, 0: None, 1: lat < lat_count - 1}

    def guarded(condition, run):
        if condition is None:
            run()
        else:
            pl.when(condition)(run)

    def device(mem_hop, lat_hop, lon_hop):
        return (
            lax.rem(mem + mem_hop, members),
            lat + lat_hop,
            lax.rem(lon + lon_hop, lon_count),
        )

    def far(peer):
        return len(peers) - 1 - peer

    def remote(src, dst, send_number, recv_number, target):
        return pltpu.make_async_remote_copy(
            src_ref=src,
            dst_ref=dst,
            send_sem=send_sems.at[send_number],
            recv_sem=recv_sems.at[recv_number],
            device_id=target,
            device_id_type=MESH,
        )

    pending = []

    def send(condition, src, dst, send_number, recv_number, target):
        guarded(condition, lambda: remote(src, dst, send_number, recv_number, target).start())
        pending.append((condition, src, send_number))

    def settle(name=None):
        kept = []
        for condition, src, number in pending:
            if name is None or number in (numbers[name, "row", -1], numbers[name, "row", 1]):
                guarded(
                    condition,
                    lambda: remote(src, src, number, 0, device(0, 0, peers[0])).wait_send(),
                )
            else:
                kept.append((condition, src, number))
        pending[:] = kept

    def await_in(condition, dst, recv_number):
        guarded(
            condition,
            lambda: remote(dst, dst, 0, recv_number, device(0, 0, peers[0])).wait_recv(),
        )

    loads = [
        pltpu.make_async_copy(src, dst, load_sems.at[number])
        for number, (src, dst) in enumerate(
            (
                (control_in, control_ref),
                (kappa_in, kappa_ref),
                (x_in, x_ref),
                (cells_in, cells_ref),
                (innovations_in, innovations_ref),
                (precision_in, precision_ref),
            )
        )
    ]
    for load in loads:
        load.start()

    barrier = pltpu.get_barrier_semaphore()
    for lat_hop in (0, -1, 1):
        def greet(lat_hop=lat_hop):
            for lon_hop in [0] + peers:
                for mem_hop in range(members if lon_hop == 0 else 1):
                    if (lat_hop, lon_hop, mem_hop) != (0, 0, 0):
                        pl.semaphore_signal(
                            barrier,
                            inc=1,
                            device_id=device(mem_hop, lat_hop, lon_hop),
                            device_id_type=MESH,
                        )
        guarded(has[lat_hop], greet)

    lane = lax.broadcasted_iota(jnp.int32, (1, SUBLANES, LANES), 2)
    lane2 = lane[0]

    for load in loads:
        load.wait()
    x_flat[...] = weight * x_ref[...].astype(jnp.float32)
    for r in range(rows):
        level_rows = pl.ds(r, levels, stride=rows)
        alpha_o[HALO + r] = control_ref[level_rows, :]
        kappa_o[HALO + r] = kappa_ref[level_rows, :]
        wx_o[HALO + r] = x_flat[level_rows, :]

    def packed(read, count):
        total = jnp.zeros((SUBLANES, LANES), jnp.float32)
        for j in range(count):
            shifted = pltpu.roll(read(j), (HALO + SLOT * j) % LANES, 1)
            total = jnp.where(lane2 // SLOT == j, shifted, total)
        return total

    def unpacked(read, j):
        shift = (LANES - HALO - SLOT * j) % LANES
        parts = [pltpu.roll(read(peer), shift, 1) if shift else read(peer) for peer in range(len(peers))]
        if len(parts) == 1:
            return parts[0]
        return jnp.where(lane2 < LANES // 2, parts[0], parts[1])

    for g in range(groups):
        base = HALO + g * GROUP
        pack_out[g, 0] = packed(lambda j: alpha_o[base + j], GROUP)
        pack_out[g, 1] = packed(lambda j: kappa_o[base + j], GROUP)
        packx_out[g] = packed(lambda j: wx_o[base + j], GROUP)

    zero_rows = jnp.zeros((HALO, SUBLANES, LANES), jnp.float32)
    for side in (-1, 1):
        start = 0 if side < 0 else HALO + rows
        group = 0 if side < 0 else groups + 1
        tile = 0 if side < 0 else edge_tiles + members

        def clear(start=start, group=group, tile=tile):
            for ref in (alpha_o, kappa_o, wx_o):
                ref[start : start + HALO] = zero_rows
            cells_all[tile : tile + edge_tiles] = jnp.zeros((edge_tiles, 1, slots), jnp.int32)
            for step in range(STEPS):
                pulled_in[step, tile : tile + edge_tiles] = jnp.zeros(
                    (edge_tiles, 1, slots), jnp.float32
                )
            for peer in range(len(peers)):
                pack_in[peer, group] = jnp.zeros((2, SUBLANES, LANES), jnp.float32)
                packx_in[peer, group] = jnp.zeros((SUBLANES, LANES), jnp.float32)
                for step in range(STEPS):
                    edge_in[step, peer, tile : tile + edge_tiles] = jnp.zeros(
                        (edge_tiles, SUBLANES, LANES), jnp.float32
                    )

        guarded(jnp.logical_not(has[side]), clear)

    greeted = len(peers) + members
    lat_near = 1 + (lat > 0).astype(jnp.int32) + (lat < lat_count - 1).astype(jnp.int32)
    pl.semaphore_wait(barrier, greeted * lat_near - 1)

    def row_copies(name, field, width, skip=0):
        for side in (-1, 1):
            source = HALO + skip if side < 0 else HALO + rows - width - skip
            target = HALO + rows + skip if side < 0 else HALO - width - skip
            send(
                has[side],
                field.at[pl.ds(source, width)],
                field.at[pl.ds(target, width)],
                numbers[name, "row", side],
                numbers[name, "row", -side],
                device(0, side, 0),
            )

    def row_waits(name, field, width, skip=0):
        for side in (-1, 1):
            start = HALO - width - skip if side < 0 else HALO + rows + skip
            await_in(has[side], field.at[pl.ds(start, width)], numbers[name, "row", side])

    def pack_copies(name, source, target):
        for side in (0, -1, 1):
            for peer, hop in enumerate(peers):
                if side == 0:
                    src, dst = source, target.at[far(peer), pl.ds(1, groups)]
                elif side < 0:
                    src, dst = source.at[0], target.at[far(peer), groups + 1]
                else:
                    src, dst = source.at[groups - 1], target.at[far(peer), 0]
                send(
                    has[side],
                    src,
                    dst,
                    numbers[name, side, peer],
                    numbers[name, -side, far(peer)],
                    device(0, side, hop),
                )

    def pack_waits(name, target):
        for side in (0, -1, 1):
            for peer in range(len(peers)):
                if side == 0:
                    dst = target.at[peer, pl.ds(1, groups)]
                else:
                    dst = target.at[peer, 0 if side < 0 else groups + 1]
                await_in(has[side], dst, numbers[name, side, peer])

    pack_copies("pack", pack_out, pack_in)
    row_copies("alpha", alpha_o, SWEEPS)
    row_copies("kappa", kappa_o, SWEEPS)
    pack_copies("packx", packx_out, packx_in)
    row_copies("kappa_far", kappa_o, HALO - SWEEPS, SWEEPS)
    row_copies("x", wx_o, HALO)

    def to_group(step, source, target, name):
        for hop in range(1, members):
            send(
                None,
                source,
                target.at[edge_tiles + mem],
                numbers[name + (hop,)],
                numbers[name + (hop,)],
                device(hop, 0, 0),
            )
        outs, ins = ("cells_out", "cells_row") if step is None else ("row_out", "row")
        key = () if step is None else (step,)
        for side in (-1, 1):
            near = mem - (0 if side < 0 else members - edge_tiles)
            inside = near < edge_tiles if side < 0 else near >= 0
            for hop in range(members):
                send(
                    jnp.logical_and(has[side], inside),
                    source,
                    target.at[near + (edge_tiles + members if side < 0 else 0)],
                    numbers[(outs,) + key + (side,)] + hop,
                    numbers[(ins,) + key + (-side,)] + near,
                    device(hop, side, 0),
                )

    def others():
        for hop in range(1, members):
            yield None, hop, edge_tiles + lax.rem(mem + members - hop, members)
        for side in (-1, 1):
            for i in range(edge_tiles):
                yield side, i, i + (0 if side < 0 else edge_tiles + members)

    to_group(None, cells_ref, cells_all, ("cells",))

    spots = tile_rows * levels

    def hot(spot, cells):
        column = lax.rem(cells, LANES)
        tile_row = lax.rem(lax.div(cells, LANES), tile_rows)
        level = lax.div(cells, LANES * tile_rows)
        place = tile_row * levels + level
        rows_hot[spot] = (
            lax.broadcasted_iota(jnp.int32, (spots, slots), 0) == place
        ).astype(jnp.float32).astype(jnp.bfloat16)
        cols_hot[spot] = (
            lax.broadcasted_iota(jnp.int32, (LANES, slots), 0) == column
        ).astype(jnp.float32).astype(jnp.bfloat16)

    def spread(spot, pulled):
        tile = jnp.zeros((spots, LANES), jnp.float32)
        for half in halves(pulled):
            tile = tile + lax.dot_general(
                rows_hot[spot] * half,
                cols_hot[spot],
                (((1,), (1,)), ((), ())),
                preferred_element_type=jnp.float32,
            )
        return tile.reshape(tile_rows, SUBLANES, LANES)

    mine = edge_tiles + mem
    hot(mine, cells_ref[...])
    live = (
        lax.broadcasted_iota(jnp.int32, (1, slots), 1) < counts_ref[0]
    ).astype(jnp.float32)
    masked_weight = precision_ref[...] * live
    innovations = innovations_ref[...]

    def halves(value):
        high = value.astype(jnp.bfloat16)
        return high, (value - high.astype(jnp.float32)).astype(jnp.bfloat16)

    first_lane, last_lane = lane == 0, lane == LANES - 1

    def sides(own, near):
        own_w, near_w = pltpu.roll(own, 1, 2), pltpu.roll(near, 1, 2)
        own_e, near_e = pltpu.roll(own, LANES - 1, 2), pltpu.roll(near, LANES - 1, 2)
        return (
            jnp.where(first_lane, near_w, own_w) + jnp.where(last_lane, near_e, own_e),
            jnp.where(first_lane, own_w, near_w) + jnp.where(last_lane, own_e, near_e),
        )

    def chunks(margin):
        first, last = HALO - margin, HALO + rows + margin
        return [(a, min(a + 8, last)) for a in range(first, last, 8)]

    def smooth_sweep(src, dst, margin, emit=None):
        for a, b in chunks(margin):
            own, near = src[0][a:b], src[1][a:b]
            beside = sides(own, near)
            for ref, value, both, kappa, out in (
                (src[0], own, beside[0], kappa_o, dst[0]),
                (src[1], near, beside[1], kappa_h, dst[1]),
            ):
                if emit is not None and ref is src[1]:
                    continue
                total = ref[a - 1 : b - 1] + ref[a + 1 : b + 1] + both
                value = value + kappa[a:b] * (total - 4.0 * value)
                if emit is None:
                    out[a:b] = value
                else:
                    emit(a, b, value)

    def adjoint_sweep(src, dst, margin, emit=None, near_too=True):
        for a, b in chunks(margin):
            scaled = [
                kappa[a - 1 : b + 1] * ref[a - 1 : b + 1]
                for ref, kappa in ((src[0], kappa_o), (src[1], kappa_h))
            ]
            beside = sides(scaled[0][1:-1], scaled[1][1:-1])
            for which in (0, 1):
                if which and not near_too:
                    continue
                t = scaled[which]
                value = src[which][a:b] + (t[:-2] + t[2:] + beside[which] - 4.0 * t[1:-1])
                if emit is None:
                    dst[which][a:b] = value
                else:
                    emit(which, a, b, value)

    work, following = (work_o, work_h), (next_o, next_h)

    row_waits("alpha", alpha_o, SWEEPS)
    row_waits("kappa", kappa_o, SWEEPS)
    pack_waits("pack", pack_in)
    for e in range(rows + 2 * HALO):
        g, j = divmod(e, GROUP)
        alpha_h[e] = unpacked(lambda peer: pack_in[peer, g, 0], j)
        kappa_h[e] = unpacked(lambda peer: pack_in[peer, g, 1], j)

    for step in range(STEPS):
        term = terms.at[step]

        def emit_term(a, b, value):
            term[a - HALO : b - HALO] = wx_o[a:b] * value

        smooth_sweep((alpha_o, alpha_h), work, SWEEPS - 1)
        src, dst = work, following
        for sweep in range(1, SWEEPS):
            last = sweep == SWEEPS - 1
            smooth_sweep(src, dst, SWEEPS - 1 - sweep, emit_term if last else None)
            src, dst = dst, src

        for hop in range(1, members):
            target = lax.rem(mem + hop, members)
            send(
                None,
                term.at[pl.ds(target * tile_rows, tile_rows)],
                pieces.at[step, hop],
                numbers["sum", step, hop],
                numbers["sum", step, hop],
                device(hop, 0, 0),
            )
        total = term[pl.ds(mem * tile_rows, tile_rows)]
        if step == 0:
            row_waits("kappa_far", kappa_o, HALO - SWEEPS, SWEEPS)
            row_waits("x", wx_o, HALO)
            pack_waits("packx", packx_in)
            for e in range(rows + 2 * HALO):
                g, j = divmod(e, GROUP)
                wx_h[e] = unpacked(lambda peer: packx_in[peer, g], j)
            for side, i, spot in others():
                if side is None:
                    await_in(None, cells_all.at[spot], numbers["cells", i])
                else:
                    await_in(has[side], cells_all.at[spot], numbers["cells_row", side] + i)
            for _, _, spot in others():
                hot(spot, cells_all[spot])
        for hop in range(1, members):
            await_in(None, pieces.at[step, hop], numbers["sum", step, hop])
            total = total + pieces[step, hop]

        flipped = jnp.transpose(total.reshape(spots, LANES))
        hot_rows, hot_cols = rows_hot[mine], cols_hot[mine]
        observed = jnp.zeros((LANES, slots), jnp.float32)
        for half in halves(flipped):
            observed = observed + jnp.dot(half, hot_rows, preferred_element_type=jnp.float32)
        observed = jnp.sum(
            observed * hot_cols.astype(jnp.float32), axis=0, keepdims=True
        )
        misfit = (observed - innovations) * masked_weight
        pulled = jnp.clip(misfit, -huber_edge, huber_edge) * masked_weight
        pulled_out[step] = pulled
        to_group(step, pulled_out.at[step], pulled_in.at[step], ("tile", step))
        tile = spread(mine, pulled)
        edge_out[step] = packed(lambda j: tile[j], tile_rows)

        force_o, edges = forcing_o.at[step], edge_in.at[step]
        for side in (-1, 1):
            near = mem - (0 if side < 0 else members - edge_tiles)
            inside = near < edge_tiles if side < 0 else near >= 0
            condition = jnp.logical_and(has[side], inside)
            spot = near + (edge_tiles + members if side < 0 else 0)
            for peer, lon_hop in enumerate(peers):
                for hop in range(members):
                    send(
                        condition,
                        edge_out.at[step],
                        edges.at[far(peer), spot],
                        numbers["corner_out", step, side, peer] + hop,
                        numbers["corner", step, -side, far(peer)] + near,
                        device(hop, side, lon_hop),
                    )
        for peer, lon_hop in enumerate(peers):
            for hop in range(members):
                send(
                    None,
                    edge_out.at[step],
                    edges.at[far(peer), edge_tiles + mem],
                    numbers["edge", step, peer, hop],
                    numbers["edge", step, far(peer), hop],
                    device(hop, 0, lon_hop),
                )
        force_o[pl.ds(HALO + mem * tile_rows, tile_rows)] = tile

        for side, i, spot in others():
            if side is None:
                await_in(None, pulled_in.at[step, spot], numbers["tile", step, i])
            else:
                await_in(has[side], pulled_in.at[step, spot], numbers["row", step, side] + i)
        for _, _, spot in others():
            force_o[pl.ds(spot * tile_rows, tile_rows)] = spread(spot, pulled_in[step, spot])
        for peer in range(len(peers)):
            for hop in range(members):
                source = lax.rem(mem + members - hop, members)
                await_in(
                    None, edges.at[peer, edge_tiles + source], numbers["edge", step, peer, hop]
                )
        for side in (-1, 1):
            for i in range(edge_tiles):
                spot = i + (0 if side < 0 else edge_tiles + members)
                for peer in range(len(peers)):
                    await_in(
                        has[side],
                        edges.at[peer, spot],
                        numbers["corner", step, side, peer] + i,
                    )

        margin = HALO - step * SWEEPS
        for e in range(HALO - margin, HALO + rows + margin):
            t, j = divmod(e, tile_rows)
            forcing_h[e] = unpacked(lambda peer: edges[peer, t], j)
        for a, b in chunks(margin):
            work_o[a:b] = wx_o[a:b] * force_o[a:b]
            work_h[a:b] = wx_h[a:b] * forcing_h[a:b]

        final = step == STEPS - 1
        inside_top = (lat > 0).astype(jnp.float32)
        inside_bottom = (lat < lat_count - 1).astype(jnp.float32)

        def emit_alpha(which, a, b, value):
            held = (alpha_o, alpha_h)[which]
            old = held[a:b]
            if final:
                fresh = ((1.0 - step_length) / step_length) * old - value
                for r in range(a, b):
                    out_ref[pl.ds(r - HALO, levels, stride=rows), :] = fresh[r - a]
                return
            fresh = old - step_length * (old + value)
            for r in range(a, b):
                row = fresh[r - a]
                if r < HALO:
                    row = row * inside_top
                elif r >= HALO + rows:
                    row = row * inside_bottom
                held[r] = row

        if step == 0:
            settle("alpha")
        src, dst = work, following
        for sweep in range(SWEEPS):
            last = sweep == SWEEPS - 1
            adjoint_sweep(
                src, dst, margin - 1 - sweep, emit_alpha if last else None, not (last and final)
            )
            src, dst = dst, src

    settle()


def fused(members, lat_count, lon_count, tile_rows, x, control, kappa, cells, counts, innov, prec):
    _, levels, rows, columns = x.shape
    peers = 1 if lon_count == 2 else 2
    edge_tiles = HALO // tile_rows
    slots = cells.shape[1]
    groups = rows // GROUP
    _, sent, received = copy_plan(members, peers, edge_tiles)
    vregs = lambda *lead: pltpu.VMEM(lead + (SUBLANES, LANES), jnp.float32)
    deep = rows + 2 * HALO
    tiles = members + 2 * edge_tiles
    vmem = pl.BlockSpec(memory_space=pltpu.VMEM)
    place = pl.BlockSpec(memory_space=pltpu.HBM)
    in_hbm = lambda array: pltpu.with_memory_space_constraint(array, pltpu.HBM)
    flat = lambda dtype: pltpu.VMEM((levels * rows, columns), dtype)
    out = pl.pallas_call(
        functools.partial(kernel, members, lat_count, lon_count, tile_rows),
        out_shape=jax.ShapeDtypeStruct((levels * rows, columns), jnp.float32),
        in_specs=[place] * 4 + [pl.BlockSpec(memory_space=pltpu.SMEM)] + [place] * 2,
        out_specs=vmem,
        scratch_shapes=[
            flat(x.dtype),
            flat(jnp.float32),
            flat(jnp.float32),
            pltpu.VMEM(cells.shape, cells.dtype),
            pltpu.VMEM(innov.shape, innov.dtype),
            pltpu.VMEM(prec.shape, prec.dtype),
            pltpu.SemaphoreType.DMA((6,)),
            flat(jnp.float32),
        ]
        + [vregs(deep)] * 10
        + [
            vregs(STEPS, deep),
            vregs(deep),
            vregs(groups, 2),
            vregs(peers, groups + 2, 2),
            vregs(groups),
            vregs(peers, groups + 2),
            vregs(STEPS),
            vregs(STEPS, peers, tiles),
            vregs(STEPS, rows),
            vregs(STEPS, members, tile_rows),
            pltpu.VMEM((STEPS, 1, slots), jnp.float32),
            pltpu.VMEM((STEPS, tiles, 1, slots), jnp.float32),
            pltpu.VMEM((tiles, 1, slots), jnp.int32),
            pltpu.VMEM((tiles, tile_rows * levels, slots), jnp.bfloat16),
            pltpu.VMEM((tiles, LANES, slots), jnp.bfloat16),
            pltpu.SemaphoreType.DMA((sent,)),
            pltpu.SemaphoreType.DMA((received,)),
        ],
        compiler_params=pltpu.CompilerParams(
            collective_id=0, has_side_effects=True, vmem_limit_bytes=24 * 2**20
        ),
    )(
        in_hbm(x.reshape(levels * rows, columns)),
        in_hbm(control.reshape(levels * rows, columns)),
        in_hbm(kappa.reshape(levels * rows, columns)),
        in_hbm(cells),
        counts,
        in_hbm(innov),
        in_hbm(prec),
    )
    return (step_length * out).reshape(1, levels, rows, columns)


def fits(members, lat_count, lon_count, x, cells):
    _, levels, rows, columns = x.shape
    tile_rows = rows // members
    return (
        levels == SUBLANES
        and columns == LANES
        and rows % members == 0
        and rows % GROUP == 0
        and rows >= 2 * HALO
        and HALO % tile_rows == 0
        and tile_rows <= GROUP
        and HALO // tile_rows <= members
        and lon_count > 1
        and cells.shape[0] == 1
    )


def picks_plan(members):

    keys = []
    for field in ("alpha", "kappa", "kappa_far", "x"):
        keys += [(field, side) for side in (-1, 1)]
    keys += [("pack", 0), ("packx", 0)]
    keys += [(name, side) for name in ("corner", "far") for side in (-1, 1)]
    keys += [("obs", hop) for hop in range(1, members)] + [("obs_lon",)]
    keys += [("obs_edge", side, lon_hop) for side in (-1, 1) for lon_hop in (0, 1)]
    for step in range(STEPS):
        keys += [
            ("pick", step, hop, side, lon_hop)
            for hop in range(members)
            for side in (-1, 0, 1)
            for lon_hop in (0, 1)
        ]
    return {key: number for number, key in enumerate(keys)}


def picks_kernel(
    members,
    lat_count,
    x_in,
    control_in,
    kappa_in,
    cells_in,
    counts_ref,
    innovations_in,
    precision_in,
    out_ref,
    x_ref,
    cells_ref,
    innovations_ref,
    precision_ref,
    load_sems,
    x_flat,
    alpha_n,
    kappa_n,
    wx_n,
    alpha_o,
    kappa_o,
    wx_o,
    damp_o,
    work_o,
    next_o,
    alpha_d,
    kappa_d,
    wx_d,
    damp_d,
    work_d,
    next_d,
    near_d,
    edge_alpha,
    edge_kappa,
    edge_x,
    pack_out,
    packx_out,
    pack_in,
    packx_in,
    corner_out,
    corner_in,
    far_out,
    far_in,
    term,
    obs_out,
    obs_in,
    weights_all,
    values_all,
    picks_out,
    picks_in,
    rows_hot,
    cols_hot,
    rows_near,
    cols_near,
    send_sems,
    recv_sems,
):
    levels = SUBLANES
    rows = x_ref.shape[0] // levels
    slots = cells_ref.shape[1]
    blocks_count = members + 2
    tile_rows = rows // members
    spots = tile_rows * levels
    numbers = picks_plan(members)
    weight = 1.0 / math.sqrt(members - 1)
    mem = lax.axis_index("mem")
    lat = lax.axis_index("lat")
    lon = lax.axis_index("lon")
    has = {-1: lat > 0, 0: None, 1: lat < lat_count - 1}
    first, last = members, members + 1
    start_of = {t: HALO + t * tile_rows for t in range(members)}
    start_of[first], start_of[last] = 0, HALO + rows

    def guarded(condition, run):
        if condition is None:
            run()
        else:
            pl.when(condition)(run)

    def both(one, other):
        return other if one is None else jnp.logical_and(one, other)

    def device(mem_hop, lat_hop, lon_hop):
        return (
            lax.rem(mem + mem_hop, members) if mem_hop else mem,
            lat + lat_hop if lat_hop else lat,
            1 - lon if lon_hop else lon,
        )

    def remote(src, dst, send_number, recv_number, target):
        return pltpu.make_async_remote_copy(
            src_ref=src,
            dst_ref=dst,
            send_sem=send_sems.at[send_number],
            recv_sem=recv_sems.at[recv_number],
            device_id=target,
            device_id_type=MESH,
        )

    pending = []

    def send(condition, copies):
        def run():
            for src, dst, send_key, recv_key, target in copies:
                remote(src, dst, numbers[send_key], numbers[recv_key], target).start()

        guarded(condition, run)
        pending.append((condition, [(src, key) for src, _, key, _, _ in copies]))

    def settle(name=None):
        kept = []
        for condition, copies in pending:
            chosen = [c for c in copies if name is None or c[1][0] == name]
            others = [c for c in copies if not (name is None or c[1][0] == name)]

            def run(chosen=chosen):
                for src, key in chosen:
                    remote(src, src, numbers[key], 0, device(0, 0, 1)).wait_send()

            if chosen:
                guarded(condition, run)
            if others:
                kept.append((condition, others))
        pending[:] = kept

    def await_in(condition, arrivals):
        def run():
            for dst, key in arrivals:
                remote(dst, dst, 0, numbers[key], device(0, 0, 1)).wait_recv()

        guarded(condition, run)

    def rows_in(source, target, first_sem):
        return [
            pltpu.make_async_copy(
                source.at[pl.ds(level * rows, rows)],
                target.at[pl.ds(0, rows), level],
                load_sems.at[first_sem + level],
            )
            for level in range(levels)
        ]

    alpha_loads = rows_in(control_in, alpha_n, 0)
    kappa_loads = rows_in(kappa_in, kappa_n, levels)
    loads = [
        pltpu.make_async_copy(src, dst, load_sems.at[2 * levels + number])
        for number, (src, dst) in enumerate(
            (
                (x_in, x_ref),
                (cells_in, cells_ref),
                (innovations_in, innovations_ref),
                (precision_in, precision_ref),
            )
        )
    ]
    for load in alpha_loads + kappa_loads + loads:
        load.start()

    barrier = pltpu.get_barrier_semaphore()

    def greet(*hops):
        pl.semaphore_signal(barrier, inc=1, device_id=device(*hops), device_id_type=MESH)

    for side in (-1, 1):

        def greet_side(side=side):
            for lon_hop in (1, 0):
                greet(0, side, lon_hop)

        guarded(has[side], greet_side)
    greet(0, 0, 1)
    for hop in range(1, members):
        greet(hop, 0, 0)

    lane = lax.broadcasted_iota(jnp.int32, (1, SUBLANES, LANES), 2)
    slot = lax.rem(lax.div(lane[0] + HALO, SLOT), LANES // SLOT)
    half_turn = LANES // 2

    def turned(value, lanes, axis=1):
        lanes %= LANES
        return pltpu.roll(value, lanes, axis) if lanes else value

    def into_frames(source, target):
        for r in range(rows):
            block = r // GROUP + 1
            target[HALO + r] = turned(source[r], SLOT * block)

    def by_slot(rows_of, i):
        total = rows_of[GROUP + i]
        for block in range(2, members + 1):
            total = jnp.where(slot == block, rows_of[GROUP * block + i], total)
        return total

    low_slots = (slot >= 1) & (slot <= members)
    up_frame = SLOT * (blocks_count - 1)

    for load in alpha_loads:
        load.wait()
    into_frames(alpha_n, alpha_o)
    for r in range(SWEEPS):
        edge_alpha[r] = turned(alpha_n[r], up_frame)
    for load in kappa_loads:
        load.wait()
    into_frames(kappa_n, kappa_o)
    for r in range(HALO):
        edge_kappa[r] = turned(kappa_n[r], up_frame)
    for i in range(GROUP):
        pack_out[i] = jnp.where(
            low_slots, by_slot(alpha_o, i), turned(by_slot(kappa_o, i), half_turn)
        )

    def gathered(rows_of, wanted):
        total = None
        for place, row in enumerate(wanted):
            shifted = turned(rows_of(row), SLOT * place - SLOT * (row // GROUP))
            total = shifted if total is None else jnp.where(slot % len(wanted) == place, shifted, total)
        return total

    def edge_rows(side, begin, end):
        block = 1 if side < 0 else members
        return [GROUP * block + i for i in range(begin, end)]

    for side in (-1, 1):
        begin = 0 if side < 0 else GROUP - SWEEPS
        corner_out[max(side, 0)] = gathered(
            lambda row: pack_out[row % GROUP], edge_rows(side, begin, begin + SWEEPS)
        )

    near_lat = (lat > 0).astype(jnp.int32) + (lat < lat_count - 1).astype(jnp.int32)
    pl.semaphore_wait(barrier, members + 2 * near_lat)

    def row_copy(name, side, natural, edge, field, width, skip=0):
        if side < 0:
            src, dst = edge.at[pl.ds(skip, width)], field.at[pl.ds(HALO + rows + skip, width)]
        else:
            src = natural.at[pl.ds(rows - width - skip, width)]
            dst = field.at[pl.ds(HALO - width - skip, width)]
        return src, dst, (name, side), (name, -side), device(0, side, 0)

    def row_arrival(name, field, width, side, skip=0):
        start = HALO - width - skip if side < 0 else HALO + rows + skip
        return field.at[pl.ds(start, width)], (name, side)

    def side_copy(name, source, target, side):
        at, to = max(side, 0), max(-side, 0)
        return source.at[at], target.at[to], (name, side), (name, -side), device(0, side, 1)

    def side_arrival(name, target, side):
        return target.at[max(side, 0)], (name, side)

    def whole_copy(name, source, target):
        return source, target, (name, 0), (name, 0), device(0, 0, 1)

    for side in (-1, 1):
        send(has[side], [side_copy("corner", corner_out, corner_in, side)])
    send(None, [whole_copy("pack", pack_out, pack_in)])
    for side in (-1, 1):
        send(
            has[side],
            [
                row_copy("alpha", side, alpha_n, edge_alpha, alpha_o, SWEEPS),
                row_copy("kappa", side, kappa_n, edge_kappa, kappa_o, SWEEPS),
            ],
        )

    for load in loads[1:]:
        load.wait()
    cells = cells_ref[...]
    column = lax.rem(cells, LANES)
    tile_row = lax.rem(lax.div(cells, LANES), tile_rows)
    level = lax.div(cells, LANES * tile_rows)
    live = (
        lax.broadcasted_iota(jnp.int32, (1, slots), 1) < counts_ref[0]
    ).astype(jnp.float32)
    my_obs = jnp.concatenate(
        [
            column.astype(jnp.float32),
            (tile_row * levels + level).astype(jnp.float32),
            precision_ref[...] * live,
            innovations_ref[...],
        ],
        axis=0,
    )
    obs_out[...] = my_obs
    obs_in[0, mem] = my_obs
    send(
        None,
        [
            (obs_out, obs_in.at[0, mem], ("obs", hop), ("obs", hop), device(hop, 0, 0))
            for hop in range(1, members)
        ],
    )

    loads[0].wait()
    x_flat[...] = weight * x_ref[...].astype(jnp.float32)
    for r in range(rows):
        wx_n[r] = x_flat[pl.ds(r, levels, stride=rows), :]
    into_frames(wx_n, wx_o)
    for r in range(HALO):
        edge_x[r] = turned(wx_n[r], up_frame)
    for i in range(GROUP // 2):
        packx_out[i] = jnp.where(
            low_slots, by_slot(wx_o, i), turned(by_slot(wx_o, i + GROUP // 2), half_turn)
        )
    for side in (-1, 1):
        begin = SWEEPS if side < 0 else 0
        far_out[max(side, 0), 0] = gathered(lambda row: wx_o[row], edge_rows(side, 0, GROUP))
        far_out[max(side, 0), 1] = gathered(
            lambda row: kappa_o[row], edge_rows(side, begin, begin + GROUP - SWEEPS)
        )
    for side in (-1, 1):
        send(
            has[side],
            [
                side_copy("far", far_out, far_in, side),
                row_copy(
                    "kappa_far", side, kappa_n, edge_kappa, kappa_o, HALO - SWEEPS, SWEEPS
                ),
                row_copy("x", side, wx_n, edge_x, wx_o, HALO),
            ],
        )
    send(None, [whole_copy("packx", packx_out, packx_in)])

    zero_rows = jnp.zeros((HALO, SUBLANES, LANES), jnp.float32)
    for side in (-1, 1):

        def clear(side=side):
            start = 0 if side < 0 else HALO + rows
            tile = first if side < 0 else last
            for ref in (alpha_o, kappa_o, wx_o):
                ref[start : start + HALO] = zero_rows
            corner_in[max(side, 0)] = zero_rows[0]
            far_in[max(side, 0)] = zero_rows[:2]
            for lon_hop in (0, 1):
                obs_in[lon_hop, tile] = jnp.zeros((4, slots), jnp.float32)
                for step in range(STEPS):
                    for hop in range(members):
                        picks_in[step, hop, lon_hop, tile : tile + 1] = jnp.zeros(
                            (1, slots), jnp.float32
                        )

        guarded(jnp.logical_not(has[side]), clear)

    lane_of = lax.broadcasted_iota(jnp.int32, (LANES, slots), 0).astype(jnp.float32)
    spot_of = lax.broadcasted_iota(jnp.int32, (spots, slots), 0).astype(jnp.float32)

    def hot(lon_hop, tile):
        place = obs_in.at[lon_hop, tile]
        column = place[0:1, :]
        in_frame = column + float(SLOT * (start_of[tile] // GROUP))
        in_frame = jnp.where(in_frame >= LANES, in_frame - LANES, in_frame)
        row_ones = (spot_of == place[1:2, :]).astype(jnp.float32).astype(jnp.bfloat16)
        if lon_hop:
            inside = (column >= HALO) & (column < LANES - HALO)
            in_frame = jnp.where(inside, -1.0, in_frame)
        column_ones = (lane_of == in_frame).astype(jnp.float32).astype(jnp.bfloat16)
        if lon_hop:
            rows_near[:, tile * slots : (tile + 1) * slots] = row_ones
            cols_near[:, tile * slots : (tile + 1) * slots] = column_ones
        else:
            rows_hot[tile] = row_ones
            cols_hot[tile] = column_ones
        weights_all[lon_hop, tile : tile + 1, :] = place[2:3, :]
        values_all[lon_hop, tile : tile + 1, :] = place[3:4, :]

    def halves(value):
        high = value.astype(jnp.bfloat16)
        return high, (value - high.astype(jnp.float32)).astype(jnp.bfloat16)

    def beside(own, deep, begin, end, deep_too):
        deep_w, deep_e = pltpu.roll(deep, 1, 2), pltpu.roll(deep, LANES - 1, 2)
        west, east = [deep_w[i] for i in range(GROUP)], [deep_e[i] for i in range(GROUP)]
        for block in range(blocks_count):
            a, b = max(begin, GROUP * block), min(end, GROUP * (block + 1))
            if a >= b:
                continue
            i, j = a - GROUP * block, b - GROUP * block
            around = own(a - 1, b + 1)
            middle = around[1:-1]
            up = [around[r] for r in range(b - a)]
            down = [around[r + 2] for r in range(b - a)]
            if i == 0:
                up[0] = turned(up[0], SLOT)
            if j == GROUP:
                down[-1] = turned(down[-1], -SLOT)
            own_w, own_e = pltpu.roll(middle, 1, 2), pltpu.roll(middle, LANES - 1, 2)
            at_w = lane == SLOT * block % LANES
            at_e = lane == (SLOT * block - 1) % LANES
            total = (
                jnp.where(at_w, deep_w[i:j], own_w)
                + jnp.where(at_e, deep_e[i:j], own_e)
                + (jnp.stack(up) + jnp.stack(down))
            )
            if deep_too:
                for r in range(i, j):
                    west[r] = jnp.where(at_w[0], own_w[r - i], west[r])
                    east[r] = jnp.where(at_e[0], own_e[r - i], east[r])
            yield block, a, b, total
        if deep_too:
            up = [turned(deep[GROUP - 1], SLOT)] + [deep[i] for i in range(GROUP - 1)]
            down = [deep[i] for i in range(1, GROUP)] + [turned(deep[0], -SLOT)]
            yield None, 0, GROUP, (
                jnp.stack(west) + jnp.stack(east) + (jnp.stack(up) + jnp.stack(down))
            )

    def smooth_sweep(src, dst, margin, emit=None):
        begin, end = HALO - margin, HALO + rows + margin
        own = lambda a, b: src[0][a:b]
        for block, a, b, total in beside(own, src[1][...], begin, end, emit is None):
            if block is None:
                dst[1][...] = damp_d[...] * src[1][...] + kappa_d[...] * total
                continue
            value = damp_o[a:b] * src[0][a:b] + kappa_o[a:b] * total
            if emit is None:
                dst[0][a:b] = value
            else:
                emit(a, b, value)

    def adjoint_sweep(src, dst, margin, emit=None, deep_too=True):
        begin, end = HALO - margin, HALO + rows + margin
        own = lambda a, b: kappa_o[a:b] * src[0][a:b]
        scaled = kappa_d[...] * src[1][...]
        for block, a, b, total in beside(own, scaled, begin, end, deep_too):
            if block is None:
                value = damp_d[...] * src[1][...] + total
            else:
                value = damp_o[a:b] * src[0][a:b] + total
            if emit is not None:
                emit(block, a, b, value)
            elif block is None:
                dst[1][...] = value
            else:
                dst[0][a:b] = value

    work, following = (work_o, work_d), (next_o, next_d)

    for hop in range(1, members):
        await_in(None, [(obs_in.at[0, lax.rem(mem + members - hop, members)], ("obs", hop))])
    for side in (-1, 1):
        tile, place = (0, last) if side < 0 else (members - 1, first)
        send(
            has[side],
            [
                (
                    obs_in.at[0, tile],
                    obs_in.at[lon_hop, place],
                    ("obs_edge", side, lon_hop),
                    ("obs_edge", -side, lon_hop),
                    device(0, side, lon_hop),
                )
                for lon_hop in (1, 0)
            ],
        )
    whole = pl.ds(0, members)
    send(
        None,
        [(obs_in.at[0, whole], obs_in.at[1, whole], ("obs_lon",), ("obs_lon",), device(0, 0, 1))],
    )
    for tile in range(members):
        hot(0, tile)

    for side in (-1, 1):
        await_in(
            has[side],
            [
                row_arrival("alpha", alpha_o, SWEEPS, side),
                row_arrival("kappa", kappa_o, SWEEPS, side),
                side_arrival("corner", corner_in, side),
            ],
        )
    await_in(None, [(pack_in, ("pack", 0))])

    def damp(begin, end):
        damp_o[begin:end] = 1.0 - 4.0 * kappa_o[begin:end]

    def at_block(value, place, block):
        return turned(value, SLOT * block - SLOT * place)

    for i in range(GROUP):
        part = pack_in[i]
        block = blocks_count - 1 if i < SWEEPS else 0
        ends = corner_in[0 if block == 0 else 1]
        at_end = slot == block
        alpha_d[i] = jnp.where(at_end, at_block(ends, i % SWEEPS, block), part)
        kappa_d[i] = jnp.where(
            at_end, at_block(ends, i % SWEEPS + SWEEPS, block), turned(part, half_turn)
        )
    damp(HALO - SWEEPS, HALO + rows + SWEEPS)
    damp_d[...] = 1.0 - 4.0 * kappa_d[...]

    for step in range(STEPS):

        def emit_term(a, b, value):
            term[a - HALO : b - HALO] = wx_o[a:b] * value

        smooth_sweep((alpha_o, alpha_d), work, SWEEPS - 1)
        src, dst = work, following
        for sweep in range(1, SWEEPS):
            smooth_sweep(
                src, dst, SWEEPS - 1 - sweep, emit_term if sweep == SWEEPS - 1 else None
            )
            src, dst = dst, src

        for tile in range(members):
            flat = term[tile * tile_rows : (tile + 1) * tile_rows].reshape(spots, LANES)
            high, low = halves(flat)
            cols = cols_hot[tile]
            picked = jnp.dot(high, cols, preferred_element_type=jnp.float32) + jnp.dot(
                low, cols, preferred_element_type=jnp.float32
            )
            picks = jnp.sum(
                picked * rows_hot[tile].astype(jnp.float32), axis=0, keepdims=True
            )
            picks_out[step, tile : tile + 1, :] = picks

        def pick_copy(hop, side, lon_hop):
            target = picks_in.at[step, hop, lon_hop]
            if side == 0:
                src, dst = picks_out.at[step], target.at[pl.ds(0, members)]
            elif side < 0:
                src, dst = picks_out.at[step, pl.ds(0, 1)], target.at[pl.ds(last, 1)]
            else:
                src = picks_out.at[step, pl.ds(members - 1, 1)]
                dst = target.at[pl.ds(first, 1)]
            return (
                src,
                dst,
                ("pick", step, hop, side, lon_hop),
                ("pick", step, hop, -side, lon_hop),
                device(hop, side, lon_hop),
            )

        for side in (-1, 1):
            send(
                has[side],
                [pick_copy(hop, side, lon_hop) for lon_hop in (1, 0) for hop in range(members)],
            )
        send(None, [pick_copy(hop, 0, 1) for hop in range(members)])
        send(None, [pick_copy(hop, 0, 0) for hop in range(1, members)])

        if step == 0:
            for side in (-1, 1):
                await_in(
                    has[side],
                    [
                        row_arrival("kappa_far", kappa_o, HALO - SWEEPS, side, SWEEPS),
                        row_arrival("x", wx_o, HALO, side),
                        side_arrival("far", far_in, side),
                    ],
                )
            await_in(None, [(packx_in, ("packx", 0))])
            for i in range(GROUP):
                part = packx_in[i % (GROUP // 2)]
                value = part if i < GROUP // 2 else turned(part, half_turn)
                for block, index in ((0, 0), (blocks_count - 1, 1)):
                    value = jnp.where(slot == block, at_block(far_in[index, 0], i, block), value)
                wx_d[i] = value
                block = 0 if i < SWEEPS else blocks_count - 1
                ends = at_block(far_in[0 if block == 0 else 1, 1], i % SWEEPS, block)
                kappa_d[i] = jnp.where(slot == block, ends, kappa_d[i])
            damp(0, HALO - SWEEPS)
            damp(HALO + rows + SWEEPS, rows + 2 * HALO)
            damp_d[...] = 1.0 - 4.0 * kappa_d[...]
            for side, tile in ((-1, first), (1, last)):
                for lon_hop in (0, 1):
                    await_in(
                        has[side], [(obs_in.at[lon_hop, tile], ("obs_edge", side, lon_hop))]
                    )
            await_in(None, [(obs_in.at[1, whole], ("obs_lon",))])
            for lon_hop in (0, 1):
                for tile in range(members + 2):
                    if (lon_hop, tile) not in [(0, t) for t in range(members)]:
                        hot(lon_hop, tile)
        if step == STEPS - 1:
            settle()

        def pulled_rows(lon_hop, a, b, observed=None):
            total = observed
            for hop in range(members):
                if hop == 0 and observed is not None:
                    continue
                piece = picks_in[step, hop, lon_hop, a:b, :]
                total = piece if total is None else total + piece
            masked_weight = weights_all[lon_hop, a:b, :]
            misfit = (total - values_all[lon_hop, a:b, :]) * masked_weight
            return jnp.clip(misfit, -huber_edge, huber_edge) * masked_weight

        def placed(rows_of, cols_of, pulled):
            left = jnp.concatenate([rows_of * half for half in halves(pulled)], axis=0)
            field = lax.dot_general(
                left, cols_of, (((1,), (1,)), ((), ())), preferred_element_type=jnp.float32
            )
            return (field[:spots] + field[spots:]).reshape(tile_rows, SUBLANES, LANES)

        def spread(tile, pulled):
            a = start_of[tile]
            b = a + tile_rows
            work_o[a:b] = wx_o[a:b] * placed(rows_hot[tile], cols_hot[tile], pulled)

        def arrivals(lon_hop, side):
            tile, count = {-1: (first, 1), 0: (0, members), 1: (last, 1)}[side]
            return [
                (
                    picks_in.at[step, hop, lon_hop, pl.ds(tile, count)],
                    ("pick", step, hop, side, lon_hop),
                )
                for hop in range(members)
                if (hop, lon_hop, side) != (0, 0, 0)
            ]

        await_in(None, arrivals(0, 0))
        pulled = pulled_rows(0, 0, members, picks_out[step])
        for tile in range(members):
            spread(tile, pulled[tile : tile + 1])
        def placed_near(a, b):
            pulled = pulled_rows(1, a, b)
            pulled = jnp.concatenate([pulled[t : t + 1] for t in range(b - a)], axis=1)
            part = slice(a * slots, b * slots)
            return placed(rows_near[:, part], cols_near[:, part], pulled)

        await_in(None, arrivals(1, 0))
        near_d[...] = placed_near(0, members)
        for side in (-1, 1):
            await_in(has[side], arrivals(0, side) + arrivals(1, side))
        pulled = pulled_rows(0, first, last + 1)
        for tile in (first, last):
            spread(tile, pulled[tile - first : tile - first + 1])
        work_d[...] = wx_d[...] * (near_d[...] + placed_near(first, last + 1))

        margin = HALO - step * SWEEPS
        final = step == STEPS - 1
        inside_top = (lat > 0).astype(jnp.float32)
        inside_bottom = (lat < lat_count - 1).astype(jnp.float32)

        def emit_alpha(block, a, b, value):
            held = alpha_d if block is None else alpha_o
            old = held[a:b]
            if final:
                fresh = ((1.0 - step_length) / step_length) * old - value
                fresh = turned(fresh, -SLOT * block, 2)
                for r in range(a, b):
                    out_ref[pl.ds(r - HALO, levels, stride=rows), :] = fresh[r - a]
                return
            fresh = old - step_length * (old + value)
            if block is None:
                fresh = fresh * jnp.where(
                    slot == 0,
                    inside_top,
                    jnp.where(slot == blocks_count - 1, inside_bottom, 1.0),
                )
            elif block == 0:
                fresh = fresh * inside_top
            elif block == blocks_count - 1:
                fresh = fresh * inside_bottom
            held[a:b] = fresh

        src, dst = work, following
        for sweep in range(SWEEPS):
            ends = sweep == SWEEPS - 1
            adjoint_sweep(
                src, dst, margin - 1 - sweep, emit_alpha if ends else None, not (ends and final)
            )
            src, dst = dst, src


def fused_picks(members, lat_count, x, control, kappa, cells, counts, innov, prec):
    _, levels, rows, columns = x.shape
    slots = cells.shape[1]
    spots = rows // members * levels
    count = len(picks_plan(members))
    vregs = lambda *lead: pltpu.VMEM(lead + (SUBLANES, LANES), jnp.float32)
    floats = lambda *shape: pltpu.VMEM(shape, jnp.float32)
    deep = rows + 2 * HALO
    tiles = members + 2
    place = pl.BlockSpec(memory_space=pltpu.HBM)
    in_hbm = lambda array: pltpu.with_memory_space_constraint(array, pltpu.HBM)
    flat = lambda dtype: pltpu.VMEM((levels * rows, columns), dtype)
    out = pl.pallas_call(
        functools.partial(picks_kernel, members, lat_count),
        out_shape=jax.ShapeDtypeStruct((levels * rows, columns), jnp.float32),
        in_specs=[place] * 4 + [pl.BlockSpec(memory_space=pltpu.SMEM)] + [place] * 2,
        out_specs=pl.BlockSpec(memory_space=pltpu.VMEM),
        scratch_shapes=[
            flat(x.dtype),
            pltpu.VMEM(cells.shape, cells.dtype),
            floats(*innov.shape),
            floats(*prec.shape),
            pltpu.SemaphoreType.DMA((2 * levels + 4,)),
            flat(jnp.float32),
        ]
        + [vregs(rows)] * 3
        + [vregs(deep)] * 6
        + [vregs(GROUP)] * 7
        + [vregs(SWEEPS), vregs(HALO), vregs(HALO)]
        + [vregs(GROUP), vregs(GROUP // 2)] * 2
        + [vregs(2)] * 2
        + [vregs(2, 2)] * 2
        + [
            vregs(rows),
            floats(4, slots),
            floats(2, tiles, 4, slots),
            floats(2, tiles, slots),
            floats(2, tiles, slots),
            floats(STEPS, members, slots),
            floats(STEPS, members, 2, tiles, slots),
            pltpu.VMEM((tiles, spots, slots), jnp.bfloat16),
            pltpu.VMEM((tiles, LANES, slots), jnp.bfloat16),
            pltpu.VMEM((spots, tiles * slots), jnp.bfloat16),
            pltpu.VMEM((LANES, tiles * slots), jnp.bfloat16),
            pltpu.SemaphoreType.DMA((count,)),
            pltpu.SemaphoreType.DMA((count,)),
        ],
        compiler_params=pltpu.CompilerParams(
            collective_id=1, has_side_effects=True, vmem_limit_bytes=24 * 2**20
        ),
    )(
        in_hbm(x.reshape(levels * rows, columns)),
        in_hbm(control.reshape(levels * rows, columns)),
        in_hbm(kappa.reshape(levels * rows, columns)),
        in_hbm(cells),
        counts,
        in_hbm(innov),
        in_hbm(prec),
    )
    return (step_length * out).reshape(1, levels, rows, columns)


def fits_picks(members, lat_count, lon_count, x, cells):
    return (
        fits(members, lat_count, lon_count, x, cells)
        and lon_count == 2
        and 2 <= members
        and (members + 2) * SLOT <= LANES
        and x.shape[2] // members == HALO == GROUP == 2 * SWEEPS
        and cells.shape[1] % LANES == 0
    )


def on_device(members, lat_count, lon_count, x, control, kappa, cells, counts, innov, prec):
    if not fits(members, lat_count, lon_count, x, cells):
        return per_device(x, control, kappa, cells, counts, innov, prec)
    if fits_picks(members, lat_count, lon_count, x, cells):
        return fused_picks(members, lat_count, x, control, kappa, cells, counts, innov, prec)
    tile_rows = x.shape[2] // members
    return fused(
        members, lat_count, lon_count, tile_rows, x, control, kappa, cells, counts, innov, prec
    )


def solution(mesh):
    return jax.shard_map(
        functools.partial(
            on_device, mesh.shape["mem"], mesh.shape["lat"], mesh.shape["lon"]
        ),
        mesh=mesh,
        in_specs=(
            P("mem", None, "lat", "lon"),
            P("mem", None, "lat", "lon"),
            P(None, "lat", "lon"),
            P(("mem", "lat", "lon"), None),
            P(("mem", "lat", "lon")),
            P(("mem", "lat", "lon"), None),
            P(("mem", "lat", "lon"), None),
        ),
        out_specs=P("mem", None, "lat", "lon"),
        check_vma=False,
    )
```

```python
import functools
import math

import jax
import jax.numpy as jnp
from jax import lax
from jax.experimental import pallas as pl
from jax.experimental.pallas import tpu as pltpu
from jax.sharding import PartitionSpec as P

SWEEPS = 4
STEPS = 2


huber_edge = 1.5
step_length = 0.5


def with_halo(cells, sides, width):
    for axis, dim in sides:
        count = lax.axis_size(axis)
        head = lax.slice_in_dim(cells, 0, width, axis=dim)
        tail = lax.slice_in_dim(cells, cells.shape[dim] - width, cells.shape[dim], axis=dim)
        cells = jnp.concatenate(
            [
                lax.ppermute(tail, axis, [(i, (i + 1) % count) for i in range(count)]),
                cells,
                lax.ppermute(head, axis, [((i + 1) % count, i) for i in range(count)]),
            ],
            axis=dim,
        )
    return cells


def inside_rows(lat_rows, margin):
    first_row = lax.axis_index("lat") * lat_rows - margin
    global_rows = first_row + jnp.arange(lat_rows + 2 * margin, dtype=jnp.int32)
    total_rows = lat_rows * lax.axis_size("lat")
    return ((global_rows >= 0) & (global_rows < total_rows)).astype(jnp.float32)[None, :, None]


def stencil(padded):
    center = padded[:, 1:-1, 1:-1]
    laplace_term = (
        padded[:, :-2, 1:-1]
        + padded[:, 2:, 1:-1]
        + padded[:, 1:-1, :-2]
        + padded[:, 1:-1, 2:]
        - 4.0 * center
    )
    return (laplace_term, center)


def smooth_deep(state_field, kappa_rim):
    lat_rows = state_field.shape[1]
    padded = with_halo(state_field, (("lat", 1), ("lon", 2)), SWEEPS)
    padded = padded * inside_rows(lat_rows, SWEEPS)
    for sweep_index in range(SWEEPS):
        offset = sweep_index + 1
        local_kappa = kappa_rim[
            :, offset : kappa_rim.shape[1] - offset, offset : kappa_rim.shape[2] - offset
        ]
        laplace_term, center = stencil(padded)
        padded = (center + local_kappa * laplace_term) * inside_rows(lat_rows, SWEEPS - offset)
    return padded


def adjoint_deep(state_field, kappa_rim):
    lat_rows = state_field.shape[1]
    padded = with_halo(state_field, (("lat", 1), ("lon", 2)), SWEEPS)
    padded = padded * inside_rows(lat_rows, SWEEPS)
    for sweep_index in range(SWEEPS):
        local_kappa = kappa_rim[
            :,
            sweep_index : kappa_rim.shape[1] - sweep_index,
            sweep_index : kappa_rim.shape[2] - sweep_index,
        ]
        laplace_term, center = stencil(local_kappa * padded)
        padded = (padded[:, 1:-1, 1:-1] + laplace_term) * inside_rows(
            lat_rows, SWEEPS - sweep_index - 1
        )
    return padded


def per_device(
    perturbations, control, diffusivity, obs_cells, obs_counts, innovations, obs_precision
):
    members = lax.axis_size("mem")
    weight = 1.0 / math.sqrt(members - 1)
    member_x = perturbations[0]
    alpha_now = control[0]
    live_slots = (
        jnp.arange(obs_cells.shape[1], dtype=jnp.int32)[None, :] < obs_counts[:, None]
    ).astype(jnp.float32)
    masked_weight = obs_precision * live_slots
    kappa_rim = with_halo(diffusivity, (("lat", 1), ("lon", 2)), SWEEPS)
    for step_index in range(STEPS):
        smoothed = smooth_deep(alpha_now, kappa_rim)
        member_term = member_x.astype(jnp.float32) * smoothed
        owned_piece = lax.psum_scatter(member_term, "mem", scatter_dimension=1, tiled=True)
        increment = weight * owned_piece
        tile_cells = obs_cells[0]
        observed = increment.reshape(-1)[tile_cells]
        misfit = (observed - innovations[0]) * masked_weight[0]
        pulled = jnp.clip(misfit, -huber_edge, huber_edge) * masked_weight[0]
        tile_field = (
            jnp.zeros((increment.size,), jnp.float32)
            .at[tile_cells]
            .add(pulled)
            .reshape(increment.shape)
        )
        forcing = lax.all_gather(tile_field, "mem", axis=1, tiled=True)
        source = weight * member_x.astype(jnp.float32) * forcing
        gradient = alpha_now + adjoint_deep(source, kappa_rim)
        alpha_now = alpha_now - step_length * gradient
    return alpha_now[None]


LANES = 128
SUBLANES = 8
HALO = STEPS * SWEEPS
SLOT = 2 * HALO
GROUP = LANES // SLOT
MESH = pl.DeviceIdType.MESH


def copy_plan(members, peers, edge_tiles):
    keys = []
    for field in ("alpha", "kappa", "kappa_far", "x"):
        keys += [(field, "row", side) for side in (-1, 1)]
    for pack in ("pack", "packx"):
        keys += [(pack, side, peer) for side in (-1, 0, 1) for peer in range(peers)]
    keys += [("cells", hop) for hop in range(1, members)]
    for step in range(STEPS):
        keys += [("sum", step, hop) for hop in range(1, members)]
        keys += [("tile", step, hop) for hop in range(1, members)]
        keys += [("edge", step, peer, hop) for peer in range(peers) for hop in range(members)]
    numbers = {key: number for number, key in enumerate(keys)}
    received = len(keys)
    for side in (-1, 1):
        numbers["cells_row", side] = received
        received += edge_tiles
    for step in range(STEPS):
        for side in (-1, 1):
            numbers["row", step, side] = received
            received += edge_tiles
            for peer in range(peers):
                numbers["corner", step, side, peer] = received
                received += edge_tiles
    sent = len(keys)
    for side in (-1, 1):
        numbers["cells_out", side] = sent
        sent += members
    for step in range(STEPS):
        for side in (-1, 1):
            numbers["row_out", step, side] = sent
            sent += members
            for peer in range(peers):
                numbers["corner_out", step, side, peer] = sent
                sent += members
    return numbers, sent, received


def kernel(
    members,
    lat_count,
    lon_count,
    tile_rows,
    x_in,
    control_in,
    kappa_in,
    cells_in,
    counts_ref,
    innovations_in,
    precision_in,
    out_ref,
    x_ref,
    control_ref,
    kappa_ref,
    cells_ref,
    innovations_ref,
    precision_ref,
    load_sems,
    x_flat,
    alpha_o,
    alpha_h,
    kappa_o,
    kappa_h,
    wx_o,
    wx_h,
    work_o,
    work_h,
    next_o,
    next_h,
    forcing_o,
    forcing_h,
    pack_out,
    pack_in,
    packx_out,
    packx_in,
    edge_out,
    edge_in,
    terms,
    pieces,
    pulled_out,
    pulled_in,
    cells_all,
    rows_hot,
    cols_hot,
    send_sems,
    recv_sems,
):
    levels = SUBLANES
    rows = control_ref.shape[0] // levels
    slots = cells_ref.shape[1]
    groups = rows // GROUP
    edge_tiles = HALO // tile_rows
    peers = [1] if lon_count == 2 else [1, lon_count - 1]
    numbers, _, _ = copy_plan(members, len(peers), edge_tiles)
    weight = 1.0 / math.sqrt(members - 1)
    mem = lax.axis_index("mem")
    lat = lax.axis_index("lat")
    lon = lax.axis_index("lon")
    has = {-1: lat > 0, 0: None, 1: lat < lat_count - 1}

    def guarded(condition, run):
        if condition is None:
            run()
        else:
            pl.when(condition)(run)

    def device(mem_hop, lat_hop, lon_hop):
        return (
            lax.rem(mem + mem_hop, members),
            lat + lat_hop,
            lax.rem(lon + lon_hop, lon_count),
        )

    def far(peer):
        return len(peers) - 1 - peer

    def remote(src, dst, send_number, recv_number, target):
        return pltpu.make_async_remote_copy(
            src_ref=src,
            dst_ref=dst,
            send_sem=send_sems.at[send_number],
            recv_sem=recv_sems.at[recv_number],
            device_id=target,
            device_id_type=MESH,
        )

    pending = []

    def send(condition, src, dst, send_number, recv_number, target):
        guarded(condition, lambda: remote(src, dst, send_number, recv_number, target).start())
        pending.append((condition, src, send_number))

    def settle(name=None):
        kept = []
        for condition, src, number in pending:
            if name is None or number in (numbers[name, "row", -1], numbers[name, "row", 1]):
                guarded(
                    condition,
                    lambda: remote(src, src, number, 0, device(0, 0, peers[0])).wait_send(),
                )
            else:
                kept.append((condition, src, number))
        pending[:] = kept

    def await_in(condition, dst, recv_number):
        guarded(
            condition,
            lambda: remote(dst, dst, 0, recv_number, device(0, 0, peers[0])).wait_recv(),
        )

    loads = [
        pltpu.make_async_copy(src, dst, load_sems.at[number])
        for number, (src, dst) in enumerate(
            (
                (control_in, control_ref),
                (kappa_in, kappa_ref),
                (x_in, x_ref),
                (cells_in, cells_ref),
                (innovations_in, innovations_ref),
                (precision_in, precision_ref),
            )
        )
    ]
    for load in loads:
        load.start()

    barrier = pltpu.get_barrier_semaphore()
    for lat_hop in (0, -1, 1):
        def greet(lat_hop=lat_hop):
            for lon_hop in [0] + peers:
                for mem_hop in range(members if lon_hop == 0 else 1):
                    if (lat_hop, lon_hop, mem_hop) != (0, 0, 0):
                        pl.semaphore_signal(
                            barrier,
                            inc=1,
                            device_id=device(mem_hop, lat_hop, lon_hop),
                            device_id_type=MESH,
                        )
        guarded(has[lat_hop], greet)

    lane = lax.broadcasted_iota(jnp.int32, (1, SUBLANES, LANES), 2)
    lane2 = lane[0]

    for load in loads:
        load.wait()
    x_flat[...] = weight * x_ref[...].astype(jnp.float32)
    for r in range(rows):
        level_rows = pl.ds(r, levels, stride=rows)
        alpha_o[HALO + r] = control_ref[level_rows, :]
        kappa_o[HALO + r] = kappa_ref[level_rows, :]
        wx_o[HALO + r] = x_flat[level_rows, :]

    def packed(read, count):
        total = jnp.zeros((SUBLANES, LANES), jnp.float32)
        for j in range(count):
            shifted = pltpu.roll(read(j), (HALO + SLOT * j) % LANES, 1)
            total = jnp.where(lane2 // SLOT == j, shifted, total)
        return total

    def unpacked(read, j):
        shift = (LANES - HALO - SLOT * j) % LANES
        parts = [pltpu.roll(read(peer), shift, 1) if shift else read(peer) for peer in range(len(peers))]
        if len(parts) == 1:
            return parts[0]
        return jnp.where(lane2 < LANES // 2, parts[0], parts[1])

    for g in range(groups):
        base = HALO + g * GROUP
        pack_out[g, 0] = packed(lambda j: alpha_o[base + j], GROUP)
        pack_out[g, 1] = packed(lambda j: kappa_o[base + j], GROUP)
        packx_out[g] = packed(lambda j: wx_o[base + j], GROUP)

    zero_rows = jnp.zeros((HALO, SUBLANES, LANES), jnp.float32)
    for side in (-1, 1):
        start = 0 if side < 0 else HALO + rows
        group = 0 if side < 0 else groups + 1
        tile = 0 if side < 0 else edge_tiles + members

        def clear(start=start, group=group, tile=tile):
            for ref in (alpha_o, kappa_o, wx_o):
                ref[start : start + HALO] = zero_rows
            cells_all[tile : tile + edge_tiles] = jnp.zeros((edge_tiles, 1, slots), jnp.int32)
            for step in range(STEPS):
                pulled_in[step, tile : tile + edge_tiles] = jnp.zeros(
                    (edge_tiles, 1, slots), jnp.float32
                )
            for peer in range(len(peers)):
                pack_in[peer, group] = jnp.zeros((2, SUBLANES, LANES), jnp.float32)
                packx_in[peer, group] = jnp.zeros((SUBLANES, LANES), jnp.float32)
                for step in range(STEPS):
                    edge_in[step, peer, tile : tile + edge_tiles] = jnp.zeros(
                        (edge_tiles, SUBLANES, LANES), jnp.float32
                    )

        guarded(jnp.logical_not(has[side]), clear)

    greeted = len(peers) + members
    lat_near = 1 + (lat > 0).astype(jnp.int32) + (lat < lat_count - 1).astype(jnp.int32)
    pl.semaphore_wait(barrier, greeted * lat_near - 1)

    def row_copies(name, field, width, skip=0):
        for side in (-1, 1):
            source = HALO + skip if side < 0 else HALO + rows - width - skip
            target = HALO + rows + skip if side < 0 else HALO - width - skip
            send(
                has[side],
                field.at[pl.ds(source, width)],
                field.at[pl.ds(target, width)],
                numbers[name, "row", side],
                numbers[name, "row", -side],
                device(0, side, 0),
            )

    def row_waits(name, field, width, skip=0):
        for side in (-1, 1):
            start = HALO - width - skip if side < 0 else HALO + rows + skip
            await_in(has[side], field.at[pl.ds(start, width)], numbers[name, "row", side])

    def pack_copies(name, source, target):
        for side in (0, -1, 1):
            for peer, hop in enumerate(peers):
                if side == 0:
                    src, dst = source, target.at[far(peer), pl.ds(1, groups)]
                elif side < 0:
                    src, dst = source.at[0], target.at[far(peer), groups + 1]
                else:
                    src, dst = source.at[groups - 1], target.at[far(peer), 0]
                send(
                    has[side],
                    src,
                    dst,
                    numbers[name, side, peer],
                    numbers[name, -side, far(peer)],
                    device(0, side, hop),
                )

    def pack_waits(name, target):
        for side in (0, -1, 1):
            for peer in range(len(peers)):
                if side == 0:
                    dst = target.at[peer, pl.ds(1, groups)]
                else:
                    dst = target.at[peer, 0 if side < 0 else groups + 1]
                await_in(has[side], dst, numbers[name, side, peer])

    pack_copies("pack", pack_out, pack_in)
    row_copies("alpha", alpha_o, SWEEPS)
    row_copies("kappa", kappa_o, SWEEPS)
    pack_copies("packx", packx_out, packx_in)
    row_copies("kappa_far", kappa_o, HALO - SWEEPS, SWEEPS)
    row_copies("x", wx_o, HALO)

    def to_group(step, source, target, name):
        for hop in range(1, members):
            send(
                None,
                source,
                target.at[edge_tiles + mem],
                numbers[name + (hop,)],
                numbers[name + (hop,)],
                device(hop, 0, 0),
            )
        outs, ins = ("cells_out", "cells_row") if step is None else ("row_out", "row")
        key = () if step is None else (step,)
        for side in (-1, 1):
            near = mem - (0 if side < 0 else members - edge_tiles)
            inside = near < edge_tiles if side < 0 else near >= 0
            for hop in range(members):
                send(
                    jnp.logical_and(has[side], inside),
                    source,
                    target.at[near + (edge_tiles + members if side < 0 else 0)],
                    numbers[(outs,) + key + (side,)] + hop,
                    numbers[(ins,) + key + (-side,)] + near,
                    device(hop, side, 0),
                )

    def others():
        for hop in range(1, members):
            yield None, hop, edge_tiles + lax.rem(mem + members - hop, members)
        for side in (-1, 1):
            for i in range(edge_tiles):
                yield side, i, i + (0 if side < 0 else edge_tiles + members)

    to_group(None, cells_ref, cells_all, ("cells",))

    spots = tile_rows * levels

    def hot(spot, cells):
        column = lax.rem(cells, LANES)
        tile_row = lax.rem(lax.div(cells, LANES), tile_rows)
        level = lax.div(cells, LANES * tile_rows)
        place = tile_row * levels + level
        rows_hot[spot] = (
            lax.broadcasted_iota(jnp.int32, (spots, slots), 0) == place
        ).astype(jnp.float32).astype(jnp.bfloat16)
        cols_hot[spot] = (
            lax.broadcasted_iota(jnp.int32, (LANES, slots), 0) == column
        ).astype(jnp.float32).astype(jnp.bfloat16)

    def spread(spot, pulled):
        tile = jnp.zeros((spots, LANES), jnp.float32)
        for half in halves(pulled):
            tile = tile + lax.dot_general(
                rows_hot[spot] * half,
                cols_hot[spot],
                (((1,), (1,)), ((), ())),
                preferred_element_type=jnp.float32,
            )
        return tile.reshape(tile_rows, SUBLANES, LANES)

    mine = edge_tiles + mem
    hot(mine, cells_ref[...])
    live = (
        lax.broadcasted_iota(jnp.int32, (1, slots), 1) < counts_ref[0]
    ).astype(jnp.float32)
    masked_weight = precision_ref[...] * live
    innovations = innovations_ref[...]

    def halves(value):
        high = value.astype(jnp.bfloat16)
        return high, (value - high.astype(jnp.float32)).astype(jnp.bfloat16)

    first_lane, last_lane = lane == 0, lane == LANES - 1

    def sides(own, near):
        own_w, near_w = pltpu.roll(own, 1, 2), pltpu.roll(near, 1, 2)
        own_e, near_e = pltpu.roll(own, LANES - 1, 2), pltpu.roll(near, LANES - 1, 2)
        return (
            jnp.where(first_lane, near_w, own_w) + jnp.where(last_lane, near_e, own_e),
            jnp.where(first_lane, own_w, near_w) + jnp.where(last_lane, own_e, near_e),
        )

    def chunks(margin):
        first, last = HALO - margin, HALO + rows + margin
        return [(a, min(a + 8, last)) for a in range(first, last, 8)]

    def smooth_sweep(src, dst, margin, emit=None):
        for a, b in chunks(margin):
            own, near = src[0][a:b], src[1][a:b]
            beside = sides(own, near)
            for ref, value, both, kappa, out in (
                (src[0], own, beside[0], kappa_o, dst[0]),
                (src[1], near, beside[1], kappa_h, dst[1]),
            ):
                if emit is not None and ref is src[1]:
                    continue
                total = ref[a - 1 : b - 1] + ref[a + 1 : b + 1] + both
                value = value + kappa[a:b] * (total - 4.0 * value)
                if emit is None:
                    out[a:b] = value
                else:
                    emit(a, b, value)

    def adjoint_sweep(src, dst, margin, emit=None, near_too=True):
        for a, b in chunks(margin):
            scaled = [
                kappa[a - 1 : b + 1] * ref[a - 1 : b + 1]
                for ref, kappa in ((src[0], kappa_o), (src[1], kappa_h))
            ]
            beside = sides(scaled[0][1:-1], scaled[1][1:-1])
            for which in (0, 1):
                if which and not near_too:
                    continue
                t = scaled[which]
                value = src[which][a:b] + (t[:-2] + t[2:] + beside[which] - 4.0 * t[1:-1])
                if emit is None:
                    dst[which][a:b] = value
                else:
                    emit(which, a, b, value)

    work, following = (work_o, work_h), (next_o, next_h)

    row_waits("alpha", alpha_o, SWEEPS)
    row_waits("kappa", kappa_o, SWEEPS)
    pack_waits("pack", pack_in)
    for e in range(rows + 2 * HALO):
        g, j = divmod(e, GROUP)
        alpha_h[e] = unpacked(lambda peer: pack_in[peer, g, 0], j)
        kappa_h[e] = unpacked(lambda peer: pack_in[peer, g, 1], j)

    for step in range(STEPS):
        term = terms.at[step]

        def emit_term(a, b, value):
            term[a - HALO : b - HALO] = wx_o[a:b] * value

        smooth_sweep((alpha_o, alpha_h), work, SWEEPS - 1)
        src, dst = work, following
        for sweep in range(1, SWEEPS):
            last = sweep == SWEEPS - 1
            smooth_sweep(src, dst, SWEEPS - 1 - sweep, emit_term if last else None)
            src, dst = dst, src

        for hop in range(1, members):
            target = lax.rem(mem + hop, members)
            send(
                None,
                term.at[pl.ds(target * tile_rows, tile_rows)],
                pieces.at[step, hop],
                numbers["sum", step, hop],
                numbers["sum", step, hop],
                device(hop, 0, 0),
            )
        total = term[pl.ds(mem * tile_rows, tile_rows)]
        if step == 0:
            row_waits("kappa_far", kappa_o, HALO - SWEEPS, SWEEPS)
            row_waits("x", wx_o, HALO)
            pack_waits("packx", packx_in)
            for e in range(rows + 2 * HALO):
                g, j = divmod(e, GROUP)
                wx_h[e] = unpacked(lambda peer: packx_in[peer, g], j)
            for side, i, spot in others():
                if side is None:
                    await_in(None, cells_all.at[spot], numbers["cells", i])
                else:
                    await_in(has[side], cells_all.at[spot], numbers["cells_row", side] + i)
            for _, _, spot in others():
                hot(spot, cells_all[spot])
        for hop in range(1, members):
            await_in(None, pieces.at[step, hop], numbers["sum", step, hop])
            total = total + pieces[step, hop]

        flipped = jnp.transpose(total.reshape(spots, LANES))
        hot_rows, hot_cols = rows_hot[mine], cols_hot[mine]
        observed = jnp.zeros((LANES, slots), jnp.float32)
        for half in halves(flipped):
            observed = observed + jnp.dot(half, hot_rows, preferred_element_type=jnp.float32)
        observed = jnp.sum(
            observed * hot_cols.astype(jnp.float32), axis=0, keepdims=True
        )
        misfit = (observed - innovations) * masked_weight
        pulled = jnp.clip(misfit, -huber_edge, huber_edge) * masked_weight
        pulled_out[step] = pulled
        to_group(step, pulled_out.at[step], pulled_in.at[step], ("tile", step))
        tile = spread(mine, pulled)
        edge_out[step] = packed(lambda j: tile[j], tile_rows)

        force_o, edges = forcing_o.at[step], edge_in.at[step]
        for side in (-1, 1):
            near = mem - (0 if side < 0 else members - edge_tiles)
            inside = near < edge_tiles if side < 0 else near >= 0
            condition = jnp.logical_and(has[side], inside)
            spot = near + (edge_tiles + members if side < 0 else 0)
            for peer, lon_hop in enumerate(peers):
                for hop in range(members):
                    send(
                        condition,
                        edge_out.at[step],
                        edges.at[far(peer), spot],
                        numbers["corner_out", step, side, peer] + hop,
                        numbers["corner", step, -side, far(peer)] + near,
                        device(hop, side, lon_hop),
                    )
        for peer, lon_hop in enumerate(peers):
            for hop in range(members):
                send(
                    None,
                    edge_out.at[step],
                    edges.at[far(peer), edge_tiles + mem],
                    numbers["edge", step, peer, hop],
                    numbers["edge", step, far(peer), hop],
                    device(hop, 0, lon_hop),
                )
        force_o[pl.ds(HALO + mem * tile_rows, tile_rows)] = tile

        for side, i, spot in others():
            if side is None:
                await_in(None, pulled_in.at[step, spot], numbers["tile", step, i])
            else:
                await_in(has[side], pulled_in.at[step, spot], numbers["row", step, side] + i)
        for _, _, spot in others():
            force_o[pl.ds(spot * tile_rows, tile_rows)] = spread(spot, pulled_in[step, spot])
        for peer in range(len(peers)):
            for hop in range(members):
                source = lax.rem(mem + members - hop, members)
                await_in(
                    None, edges.at[peer, edge_tiles + source], numbers["edge", step, peer, hop]
                )
        for side in (-1, 1):
            for i in range(edge_tiles):
                spot = i + (0 if side < 0 else edge_tiles + members)
                for peer in range(len(peers)):
                    await_in(
                        has[side],
                        edges.at[peer, spot],
                        numbers["corner", step, side, peer] + i,
                    )

        margin = HALO - step * SWEEPS
        for e in range(HALO - margin, HALO + rows + margin):
            t, j = divmod(e, tile_rows)
            forcing_h[e] = unpacked(lambda peer: edges[peer, t], j)
        for a, b in chunks(margin):
            work_o[a:b] = wx_o[a:b] * force_o[a:b]
            work_h[a:b] = wx_h[a:b] * forcing_h[a:b]

        final = step == STEPS - 1
        inside_top = (lat > 0).astype(jnp.float32)
        inside_bottom = (lat < lat_count - 1).astype(jnp.float32)

        def emit_alpha(which, a, b, value):
            held = (alpha_o, alpha_h)[which]
            old = held[a:b]
            if final:
                fresh = ((1.0 - step_length) / step_length) * old - value
                for r in range(a, b):
                    out_ref[pl.ds(r - HALO, levels, stride=rows), :] = fresh[r - a]
                return
            fresh = old - step_length * (old + value)
            for r in range(a, b):
                row = fresh[r - a]
                if r < HALO:
                    row = row * inside_top
                elif r >= HALO + rows:
                    row = row * inside_bottom
                held[r] = row

        if step == 0:
            settle("alpha")
        src, dst = work, following
        for sweep in range(SWEEPS):
            last = sweep == SWEEPS - 1
            adjoint_sweep(
                src, dst, margin - 1 - sweep, emit_alpha if last else None, not (last and final)
            )
            src, dst = dst, src

    settle()


def fused(members, lat_count, lon_count, tile_rows, x, control, kappa, cells, counts, innov, prec):
    _, levels, rows, columns = x.shape
    peers = 1 if lon_count == 2 else 2
    edge_tiles = HALO // tile_rows
    slots = cells.shape[1]
    groups = rows // GROUP
    _, sent, received = copy_plan(members, peers, edge_tiles)
    vregs = lambda *lead: pltpu.VMEM(lead + (SUBLANES, LANES), jnp.float32)
    deep = rows + 2 * HALO
    tiles = members + 2 * edge_tiles
    vmem = pl.BlockSpec(memory_space=pltpu.VMEM)
    place = pl.BlockSpec(memory_space=pltpu.HBM)
    in_hbm = lambda array: pltpu.with_memory_space_constraint(array, pltpu.HBM)
    flat = lambda dtype: pltpu.VMEM((levels * rows, columns), dtype)
    out = pl.pallas_call(
        functools.partial(kernel, members, lat_count, lon_count, tile_rows),
        out_shape=jax.ShapeDtypeStruct((levels * rows, columns), jnp.float32),
        in_specs=[place] * 4 + [pl.BlockSpec(memory_space=pltpu.SMEM)] + [place] * 2,
        out_specs=vmem,
        scratch_shapes=[
            flat(x.dtype),
            flat(jnp.float32),
            flat(jnp.float32),
            pltpu.VMEM(cells.shape, cells.dtype),
            pltpu.VMEM(innov.shape, innov.dtype),
            pltpu.VMEM(prec.shape, prec.dtype),
            pltpu.SemaphoreType.DMA((6,)),
            flat(jnp.float32),
        ]
        + [vregs(deep)] * 10
        + [
            vregs(STEPS, deep),
            vregs(deep),
            vregs(groups, 2),
            vregs(peers, groups + 2, 2),
            vregs(groups),
            vregs(peers, groups + 2),
            vregs(STEPS),
            vregs(STEPS, peers, tiles),
            vregs(STEPS, rows),
            vregs(STEPS, members, tile_rows),
            pltpu.VMEM((STEPS, 1, slots), jnp.float32),
            pltpu.VMEM((STEPS, tiles, 1, slots), jnp.float32),
            pltpu.VMEM((tiles, 1, slots), jnp.int32),
            pltpu.VMEM((tiles, tile_rows * levels, slots), jnp.bfloat16),
            pltpu.VMEM((tiles, LANES, slots), jnp.bfloat16),
            pltpu.SemaphoreType.DMA((sent,)),
            pltpu.SemaphoreType.DMA((received,)),
        ],
        compiler_params=pltpu.CompilerParams(
            collective_id=0, has_side_effects=True, vmem_limit_bytes=24 * 2**20
        ),
    )(
        in_hbm(x.reshape(levels * rows, columns)),
        in_hbm(control.reshape(levels * rows, columns)),
        in_hbm(kappa.reshape(levels * rows, columns)),
        in_hbm(cells),
        counts,
        in_hbm(innov),
        in_hbm(prec),
    )
    return (step_length * out).reshape(1, levels, rows, columns)


def fits(members, lat_count, lon_count, x, cells):
    _, levels, rows, columns = x.shape
    tile_rows = rows // members
    return (
        levels == SUBLANES
        and columns == LANES
        and rows % members == 0
        and rows % GROUP == 0
        and rows >= 2 * HALO
        and HALO % tile_rows == 0
        and tile_rows <= GROUP
        and HALO // tile_rows <= members
        and lon_count > 1
        and cells.shape[0] == 1
    )


def picks_plan(members):

    keys = []
    for field in ("alpha", "kappa", "kappa_far", "x"):
        keys += [(field, side) for side in (-1, 1)]
    keys += [("pack", 0), ("packx", 0)]
    keys += [(name, side) for name in ("corner", "far") for side in (-1, 1)]
    keys += [("obs", hop) for hop in range(1, members)] + [("obs_lon",)]
    keys += [("obs_edge", side, lon_hop) for side in (-1, 1) for lon_hop in (0, 1)]
    for step in range(STEPS):
        keys += [
            ("pick", step, hop, side, lon_hop)
            for hop in range(members)
            for side in (-1, 0, 1)
            for lon_hop in (0, 1)
        ]
    return {key: number for number, key in enumerate(keys)}


def picks_kernel(
    members,
    lat_count,
    x_in,
    control_in,
    kappa_in,
    cells_in,
    counts_ref,
    innovations_in,
    precision_in,
    out_ref,
    x_ref,
    cells_ref,
    innovations_ref,
    precision_ref,
    load_sems,
    x_flat,
    alpha_n,
    kappa_n,
    wx_n,
    alpha_o,
    kappa_o,
    wx_o,
    damp_o,
    work_o,
    next_o,
    path_o,
    alpha_d,
    kappa_d,
    wx_d,
    damp_d,
    work_d,
    next_d,
    path_d,
    near_d,
    edge_alpha,
    edge_kappa,
    edge_x,
    pack_out,
    packx_out,
    pack_in,
    packx_in,
    corner_out,
    corner_in,
    far_out,
    far_in,
    term,
    obs_out,
    obs_in,
    weights_all,
    values_all,
    picks_out,
    picks_in,
    rows_hot,
    cols_hot,
    rows_near,
    cols_near,
    send_sems,
    recv_sems,
):
    levels = SUBLANES
    rows = x_ref.shape[0] // levels
    slots = cells_ref.shape[1]
    blocks_count = members + 2
    tile_rows = rows // members
    spots = tile_rows * levels
    numbers = picks_plan(members)
    weight = 1.0 / math.sqrt(members - 1)
    mem = lax.axis_index("mem")
    lat = lax.axis_index("lat")
    lon = lax.axis_index("lon")
    has = {-1: lat > 0, 0: None, 1: lat < lat_count - 1}
    first, last = members, members + 1
    start_of = {t: HALO + t * tile_rows for t in range(members)}
    start_of[first], start_of[last] = 0, HALO + rows

    def guarded(condition, run):
        if condition is None:
            run()
        else:
            pl.when(condition)(run)

    def both(one, other):
        return other if one is None else jnp.logical_and(one, other)

    def device(mem_hop, lat_hop, lon_hop):
        return (
            lax.rem(mem + mem_hop, members) if mem_hop else mem,
            lat + lat_hop if lat_hop else lat,
            1 - lon if lon_hop else lon,
        )

    def remote(src, dst, send_number, recv_number, target):
        return pltpu.make_async_remote_copy(
            src_ref=src,
            dst_ref=dst,
            send_sem=send_sems.at[send_number],
            recv_sem=recv_sems.at[recv_number],
            device_id=target,
            device_id_type=MESH,
        )

    pending = []

    def send(condition, copies):
        def run():
            for src, dst, send_key, recv_key, target in copies:
                remote(src, dst, numbers[send_key], numbers[recv_key], target).start()

        guarded(condition, run)
        pending.append((condition, [(src, key) for src, _, key, _, _ in copies]))

    def settle(name=None):
        kept = []
        for condition, copies in pending:
            chosen = [c for c in copies if name is None or c[1][0] == name]
            others = [c for c in copies if not (name is None or c[1][0] == name)]

            def run(chosen=chosen):
                for src, key in chosen:
                    remote(src, src, numbers[key], 0, device(0, 0, 1)).wait_send()

            if chosen:
                guarded(condition, run)
            if others:
                kept.append((condition, others))
        pending[:] = kept

    def await_in(condition, arrivals):
        def run():
            for dst, key in arrivals:
                remote(dst, dst, 0, numbers[key], device(0, 0, 1)).wait_recv()

        guarded(condition, run)

    def rows_in(source, target, first_sem):
        return [
            pltpu.make_async_copy(
                source.at[pl.ds(level * rows, rows)],
                target.at[pl.ds(0, rows), level],
                load_sems.at[first_sem + level],
            )
            for level in range(levels)
        ]

    alpha_loads = rows_in(control_in, alpha_n, 0)
    kappa_loads = rows_in(kappa_in, kappa_n, levels)
    loads = [
        pltpu.make_async_copy(src, dst, load_sems.at[2 * levels + number])
        for number, (src, dst) in enumerate(
            (
                (x_in, x_ref),
                (cells_in, cells_ref),
                (innovations_in, innovations_ref),
                (precision_in, precision_ref),
            )
        )
    ]
    barrier = pltpu.get_barrier_semaphore()

    def greet(*hops):
        pl.semaphore_signal(barrier, inc=1, device_id=device(*hops), device_id_type=MESH)

    for side in (-1, 1):

        def greet_side(side=side):
            for lon_hop in (1, 0):
                greet(0, side, lon_hop)

        guarded(has[side], greet_side)
    greet(0, 0, 1)
    for hop in range(1, members):
        greet(hop, 0, 0)

    for load in alpha_loads + kappa_loads + loads:
        load.start()

    lane = lax.broadcasted_iota(jnp.int32, (1, SUBLANES, LANES), 2)
    slot = lax.rem(lax.div(lane[0] + HALO, SLOT), LANES // SLOT)
    half_turn = LANES // 2

    def turned(value, lanes, axis=1):
        lanes %= LANES
        return pltpu.roll(value, lanes, axis) if lanes else value

    def into_frames(source, target):
        for r in range(rows):
            block = r // GROUP + 1
            target[HALO + r] = turned(source[r], SLOT * block)

    def by_slot(rows_of, i):
        total = rows_of[GROUP + i]
        for block in range(2, members + 1):
            total = jnp.where(slot == block, rows_of[GROUP * block + i], total)
        return total

    low_slots = (slot >= 1) & (slot <= members)
    up_frame = SLOT * (blocks_count - 1)

    for load in alpha_loads:
        load.wait()
    into_frames(alpha_n, alpha_o)
    for r in range(SWEEPS):
        edge_alpha[r] = turned(alpha_n[r], up_frame)
    for load in kappa_loads:
        load.wait()
    into_frames(kappa_n, kappa_o)
    for r in range(HALO):
        edge_kappa[r] = turned(kappa_n[r], up_frame)
    for i in range(GROUP):
        pack_out[i] = jnp.where(
            low_slots, by_slot(alpha_o, i), turned(by_slot(kappa_o, i), half_turn)
        )

    def gathered(rows_of, wanted):
        total = None
        for place, row in enumerate(wanted):
            shifted = turned(rows_of(row), SLOT * place - SLOT * (row // GROUP))
            total = shifted if total is None else jnp.where(slot % len(wanted) == place, shifted, total)
        return total

    def edge_rows(side, begin, end):
        block = 1 if side < 0 else members
        return [GROUP * block + i for i in range(begin, end)]

    for side in (-1, 1):
        begin = 0 if side < 0 else GROUP - SWEEPS
        corner_out[max(side, 0)] = gathered(
            lambda row: pack_out[row % GROUP], edge_rows(side, begin, begin + SWEEPS)
        )

    for load in loads[1:]:
        load.wait()
    cells = cells_ref[...]
    column = lax.rem(cells, LANES)
    tile_row = lax.rem(lax.div(cells, LANES), tile_rows)
    level = lax.div(cells, LANES * tile_rows)
    live = (
        lax.broadcasted_iota(jnp.int32, (1, slots), 1) < counts_ref[0]
    ).astype(jnp.float32)
    my_obs = jnp.concatenate(
        [
            column.astype(jnp.float32),
            (tile_row * levels + level).astype(jnp.float32),
            precision_ref[...] * live,
            innovations_ref[...],
        ],
        axis=0,
    )
    obs_out[...] = my_obs
    obs_in[0, mem] = my_obs
    near_lat = (lat > 0).astype(jnp.int32) + (lat < lat_count - 1).astype(jnp.int32)
    pl.semaphore_wait(barrier, members + 2 * near_lat)

    def row_copy(name, side, natural, edge, field, width, skip=0):
        if side < 0:
            src, dst = edge.at[pl.ds(skip, width)], field.at[pl.ds(HALO + rows + skip, width)]
        else:
            src = natural.at[pl.ds(rows - width - skip, width)]
            dst = field.at[pl.ds(HALO - width - skip, width)]
        return src, dst, (name, side), (name, -side), device(0, side, 0)

    def row_arrival(name, field, width, side, skip=0):
        start = HALO - width - skip if side < 0 else HALO + rows + skip
        return field.at[pl.ds(start, width)], (name, side)

    def side_copy(name, source, target, side):
        at, to = max(side, 0), max(-side, 0)
        return source.at[at], target.at[to], (name, side), (name, -side), device(0, side, 1)

    def side_arrival(name, target, side):
        return target.at[max(side, 0)], (name, side)

    def whole_copy(name, source, target):
        return source, target, (name, 0), (name, 0), device(0, 0, 1)

    for side in (-1, 1):
        send(has[side], [side_copy("corner", corner_out, corner_in, side)])
    send(None, [whole_copy("pack", pack_out, pack_in)])
    send(
        None,
        [
            (obs_out, obs_in.at[0, mem], ("obs", hop), ("obs", hop), device(hop, 0, 0))
            for hop in range(1, members)
        ],
    )

    for side in (-1, 1):
        send(
            has[side],
            [
                row_copy("alpha", side, alpha_n, edge_alpha, alpha_o, SWEEPS),
                row_copy("kappa", side, kappa_n, edge_kappa, kappa_o, SWEEPS),
            ],
        )

    loads[0].wait()
    x_flat[...] = weight * x_ref[...].astype(jnp.float32)
    for r in range(rows):
        wx_n[r] = x_flat[pl.ds(r, levels, stride=rows), :]
    into_frames(wx_n, wx_o)
    for r in range(HALO):
        edge_x[r] = turned(wx_n[r], up_frame)
    for i in range(GROUP // 2):
        packx_out[i] = jnp.where(
            low_slots, by_slot(wx_o, i), turned(by_slot(wx_o, i + GROUP // 2), half_turn)
        )
    for side in (-1, 1):
        begin = SWEEPS if side < 0 else 0
        far_out[max(side, 0), 0] = gathered(lambda row: wx_o[row], edge_rows(side, 0, GROUP))
        far_out[max(side, 0), 1] = gathered(
            lambda row: kappa_o[row], edge_rows(side, begin, begin + GROUP - SWEEPS)
        )
    for side in (-1, 1):
        send(
            has[side],
            [
                side_copy("far", far_out, far_in, side),
                row_copy(
                    "kappa_far", side, kappa_n, edge_kappa, kappa_o, HALO - SWEEPS, SWEEPS
                ),
                row_copy("x", side, wx_n, edge_x, wx_o, HALO),
            ],
        )
    send(None, [whole_copy("packx", packx_out, packx_in)])

    zero_rows = jnp.zeros((HALO, SUBLANES, LANES), jnp.float32)
    for side in (-1, 1):

        def clear(side=side):
            start = 0 if side < 0 else HALO + rows
            tile = first if side < 0 else last
            for ref in (alpha_o, kappa_o, wx_o):
                ref[start : start + HALO] = zero_rows
            corner_in[max(side, 0)] = zero_rows[0]
            far_in[max(side, 0)] = zero_rows[:2]
            for lon_hop in (0, 1):
                obs_in[lon_hop, tile] = jnp.zeros((4, slots), jnp.float32)
                for step in range(STEPS):
                    for hop in range(members):
                        picks_in[step, hop, lon_hop, tile : tile + 1] = jnp.zeros(
                            (1, slots), jnp.float32
                        )

        guarded(jnp.logical_not(has[side]), clear)

    lane_of = lax.broadcasted_iota(jnp.int32, (LANES, slots), 0).astype(jnp.float32)
    spot_of = lax.broadcasted_iota(jnp.int32, (spots, slots), 0).astype(jnp.float32)

    def hot(lon_hop, tile):
        place = obs_in.at[lon_hop, tile]
        column = place[0:1, :]
        in_frame = column + float(SLOT * (start_of[tile] // GROUP))
        in_frame = jnp.where(in_frame >= LANES, in_frame - LANES, in_frame)
        row_ones = (spot_of == place[1:2, :]).astype(jnp.float32).astype(jnp.bfloat16)
        if lon_hop:
            inside = (column >= HALO) & (column < LANES - HALO)
            in_frame = jnp.where(inside, -1.0, in_frame)
        column_ones = (lane_of == in_frame).astype(jnp.float32).astype(jnp.bfloat16)
        if lon_hop:
            rows_near[:, tile * slots : (tile + 1) * slots] = row_ones
            cols_near[:, tile * slots : (tile + 1) * slots] = column_ones
        else:
            rows_hot[tile] = row_ones
            cols_hot[tile] = column_ones
        weights_all[lon_hop, tile : tile + 1, :] = place[2:3, :]
        values_all[lon_hop, tile : tile + 1, :] = place[3:4, :]

    def halves(value):
        high = value.astype(jnp.bfloat16)
        return high, (value - high.astype(jnp.float32)).astype(jnp.bfloat16)

    def beside(own, deep, begin, end, deep_too):
        deep_w, deep_e = pltpu.roll(deep, 1, 2), pltpu.roll(deep, LANES - 1, 2)
        west, east = [deep_w[i] for i in range(GROUP)], [deep_e[i] for i in range(GROUP)]
        for block in range(blocks_count):
            a, b = max(begin, GROUP * block), min(end, GROUP * (block + 1))
            if a >= b:
                continue
            i, j = a - GROUP * block, b - GROUP * block
            around = own(a - 1, b + 1)
            middle = around[1:-1]
            up = [around[r] for r in range(b - a)]
            down = [around[r + 2] for r in range(b - a)]
            if i == 0:
                up[0] = turned(up[0], SLOT)
            if j == GROUP:
                down[-1] = turned(down[-1], -SLOT)
            own_w, own_e = pltpu.roll(middle, 1, 2), pltpu.roll(middle, LANES - 1, 2)
            at_w = lane == SLOT * block % LANES
            at_e = lane == (SLOT * block - 1) % LANES
            total = (
                jnp.where(at_w, deep_w[i:j], own_w)
                + jnp.where(at_e, deep_e[i:j], own_e)
                + (jnp.stack(up) + jnp.stack(down))
            )
            if deep_too:
                for r in range(i, j):
                    west[r] = jnp.where(at_w[0], own_w[r - i], west[r])
                    east[r] = jnp.where(at_e[0], own_e[r - i], east[r])
            yield block, a, b, total
        if deep_too:
            up = [turned(deep[GROUP - 1], SLOT)] + [deep[i] for i in range(GROUP - 1)]
            down = [deep[i] for i in range(1, GROUP)] + [turned(deep[0], -SLOT)]
            yield None, 0, GROUP, (
                jnp.stack(west) + jnp.stack(east) + (jnp.stack(up) + jnp.stack(down))
            )

    def smooth_sweep(src, dst, margin, emit=None):
        begin, end = HALO - margin, HALO + rows + margin
        own = lambda a, b: src[0][a:b]
        for block, a, b, total in beside(own, src[1][...], begin, end, emit is None):
            if block is None:
                dst[1][...] = damp_d[...] * src[1][...] + kappa_d[...] * total
                continue
            value = damp_o[a:b] * src[0][a:b] + kappa_o[a:b] * total
            if emit is None:
                dst[0][a:b] = value
            else:
                emit(a, b, value)

    path = [(path_o.at[n], path_d.at[n]) for n in range(SWEEPS)]

    def path_sum(which, part):
        total = path[0][which][part]
        for n in range(1, SWEEPS):
            total = total + path[n][which][part]
        return total

    def adjoint(margin, emit, deep_too):
        for n in range(SWEEPS - 1):
            smooth_sweep(path[n], path[n + 1], margin - 1 - n)
        margin -= SWEEPS
        begin, end = HALO - margin, HALO + rows + margin
        own = lambda a, b: path_sum(0, slice(a, b))
        deep = path_sum(1, slice(None))
        for block, a, b, total in beside(own, deep, begin, end, deep_too):
            if block is None:
                emit(block, a, b, work_d[...] + (total - 4.0 * deep))
            else:
                emit(block, a, b, work_o[a:b] + (total - 4.0 * own(a, b)))

    work, following = (work_o, work_d), (next_o, next_d)

    for hop in range(1, members):
        await_in(None, [(obs_in.at[0, lax.rem(mem + members - hop, members)], ("obs", hop))])
    for side in (-1, 1):
        tile, place = (0, last) if side < 0 else (members - 1, first)
        send(
            has[side],
            [
                (
                    obs_in.at[0, tile],
                    obs_in.at[lon_hop, place],
                    ("obs_edge", side, lon_hop),
                    ("obs_edge", -side, lon_hop),
                    device(0, side, lon_hop),
                )
                for lon_hop in (1, 0)
            ],
        )
    whole = pl.ds(0, members)
    send(
        None,
        [(obs_in.at[0, whole], obs_in.at[1, whole], ("obs_lon",), ("obs_lon",), device(0, 0, 1))],
    )
    for tile in range(members):
        hot(0, tile)

    for side in (-1, 1):
        await_in(
            has[side],
            [
                row_arrival("alpha", alpha_o, SWEEPS, side),
                row_arrival("kappa", kappa_o, SWEEPS, side),
                side_arrival("corner", corner_in, side),
            ],
        )
    await_in(None, [(pack_in, ("pack", 0))])

    def damp(begin, end):
        damp_o[begin:end] = 1.0 - 4.0 * kappa_o[begin:end]

    def at_block(value, place, block):
        return turned(value, SLOT * block - SLOT * place)

    for i in range(GROUP):
        part = pack_in[i]
        block = blocks_count - 1 if i < SWEEPS else 0
        ends = corner_in[0 if block == 0 else 1]
        at_end = slot == block
        alpha_d[i] = jnp.where(at_end, at_block(ends, i % SWEEPS, block), part)
        kappa_d[i] = jnp.where(
            at_end, at_block(ends, i % SWEEPS + SWEEPS, block), turned(part, half_turn)
        )
    damp(HALO - SWEEPS, HALO + rows + SWEEPS)
    damp_d[...] = 1.0 - 4.0 * kappa_d[...]

    for step in range(STEPS):

        def emit_term(a, b, value):
            term[a - HALO : b - HALO] = wx_o[a:b] * value

        smooth_sweep((alpha_o, alpha_d), work, SWEEPS - 1)
        src, dst = work, following
        for sweep in range(1, SWEEPS):
            smooth_sweep(
                src, dst, SWEEPS - 1 - sweep, emit_term if sweep == SWEEPS - 1 else None
            )
            src, dst = dst, src

        for tile in range(members):
            flat = term[tile * tile_rows : (tile + 1) * tile_rows].reshape(spots, LANES)
            high, low = halves(flat)
            cols = cols_hot[tile]
            picked = jnp.dot(high, cols, preferred_element_type=jnp.float32) + jnp.dot(
                low, cols, preferred_element_type=jnp.float32
            )
            picks = jnp.sum(
                picked * rows_hot[tile].astype(jnp.float32), axis=0, keepdims=True
            )
            picks_out[step, tile : tile + 1, :] = picks

        def pick_copy(hop, side, lon_hop):
            target = picks_in.at[step, hop, lon_hop]
            if side == 0:
                src, dst = picks_out.at[step], target.at[pl.ds(0, members)]
            elif side < 0:
                src, dst = picks_out.at[step, pl.ds(0, 1)], target.at[pl.ds(last, 1)]
            else:
                src = picks_out.at[step, pl.ds(members - 1, 1)]
                dst = target.at[pl.ds(first, 1)]
            return (
                src,
                dst,
                ("pick", step, hop, side, lon_hop),
                ("pick", step, hop, -side, lon_hop),
                device(hop, side, lon_hop),
            )

        for side in (-1, 1):
            send(
                has[side],
                [pick_copy(hop, side, lon_hop) for lon_hop in (1, 0) for hop in range(members)],
            )
        send(None, [pick_copy(hop, 0, 1) for hop in range(members)])
        send(None, [pick_copy(hop, 0, 0) for hop in range(1, members)])

        if step == 0:
            for side in (-1, 1):
                await_in(
                    has[side],
                    [
                        row_arrival("kappa_far", kappa_o, HALO - SWEEPS, side, SWEEPS),
                        row_arrival("x", wx_o, HALO, side),
                        side_arrival("far", far_in, side),
                    ],
                )
            await_in(None, [(packx_in, ("packx", 0))])
            for i in range(GROUP):
                part = packx_in[i % (GROUP // 2)]
                value = part if i < GROUP // 2 else turned(part, half_turn)
                for block, index in ((0, 0), (blocks_count - 1, 1)):
                    value = jnp.where(slot == block, at_block(far_in[index, 0], i, block), value)
                wx_d[i] = value
                block = 0 if i < SWEEPS else blocks_count - 1
                ends = at_block(far_in[0 if block == 0 else 1, 1], i % SWEEPS, block)
                kappa_d[i] = jnp.where(slot == block, ends, kappa_d[i])
            damp(0, HALO - SWEEPS)
            damp(HALO + rows + SWEEPS, rows + 2 * HALO)
            damp_d[...] = 1.0 - 4.0 * kappa_d[...]
            for side, tile in ((-1, first), (1, last)):
                for lon_hop in (0, 1):
                    await_in(
                        has[side], [(obs_in.at[lon_hop, tile], ("obs_edge", side, lon_hop))]
                    )
            await_in(None, [(obs_in.at[1, whole], ("obs_lon",))])
            for lon_hop in (0, 1):
                for tile in range(members + 2):
                    if (lon_hop, tile) not in [(0, t) for t in range(members)]:
                        hot(lon_hop, tile)
        if step == STEPS - 1:
            settle()

        def pulled_rows(lon_hop, a, b, observed=None):
            total = observed
            for hop in range(members):
                if hop == 0 and observed is not None:
                    continue
                piece = picks_in[step, hop, lon_hop, a:b, :]
                total = piece if total is None else total + piece
            masked_weight = weights_all[lon_hop, a:b, :]
            misfit = (total - values_all[lon_hop, a:b, :]) * masked_weight
            return jnp.clip(misfit, -huber_edge, huber_edge) * masked_weight

        def placed(rows_of, cols_of, pulled):
            left = jnp.concatenate([rows_of * half for half in halves(pulled)], axis=0)
            field = lax.dot_general(
                left, cols_of, (((1,), (1,)), ((), ())), preferred_element_type=jnp.float32
            )
            return (field[:spots] + field[spots:]).reshape(tile_rows, SUBLANES, LANES)

        def spread(tile, pulled):
            a = start_of[tile]
            b = a + tile_rows
            source = wx_o[a:b] * placed(rows_hot[tile], cols_hot[tile], pulled)
            work_o[a:b] = source
            path_o[0, a:b] = kappa_o[a:b] * source

        def arrivals(lon_hop, side):
            tile, count = {-1: (first, 1), 0: (0, members), 1: (last, 1)}[side]
            return [
                (
                    picks_in.at[step, hop, lon_hop, pl.ds(tile, count)],
                    ("pick", step, hop, side, lon_hop),
                )
                for hop in range(members)
                if (hop, lon_hop, side) != (0, 0, 0)
            ]

        await_in(None, arrivals(0, 0))
        pulled = pulled_rows(0, 0, members, picks_out[step])
        for tile in range(members):
            spread(tile, pulled[tile : tile + 1])
        def placed_near(a, b):
            pulled = pulled_rows(1, a, b)
            pulled = jnp.concatenate([pulled[t : t + 1] for t in range(b - a)], axis=1)
            part = slice(a * slots, b * slots)
            return placed(rows_near[:, part], cols_near[:, part], pulled)

        await_in(None, arrivals(1, 0))
        near_d[...] = placed_near(0, members)
        for side in (-1, 1):
            await_in(has[side], arrivals(0, side) + arrivals(1, side))
        pulled = pulled_rows(0, first, last + 1)
        for tile in (first, last):
            spread(tile, pulled[tile - first : tile - first + 1])
        source = wx_d[...] * (near_d[...] + placed_near(first, last + 1))
        work_d[...] = source
        path_d[0] = kappa_d[...] * source

        margin = HALO - step * SWEEPS
        final = step == STEPS - 1
        inside_top = (lat > 0).astype(jnp.float32)
        inside_bottom = (lat < lat_count - 1).astype(jnp.float32)

        def emit_alpha(block, a, b, value):
            held = alpha_d if block is None else alpha_o
            old = held[a:b]
            if final:
                fresh = ((1.0 - step_length) / step_length) * old - value
                fresh = turned(fresh, -SLOT * block, 2)
                for r in range(a, b):
                    out_ref[pl.ds(r - HALO, levels, stride=rows), :] = fresh[r - a]
                return
            fresh = old - step_length * (old + value)
            if block is None:
                fresh = fresh * jnp.where(
                    slot == 0,
                    inside_top,
                    jnp.where(slot == blocks_count - 1, inside_bottom, 1.0),
                )
            elif block == 0:
                fresh = fresh * inside_top
            elif block == blocks_count - 1:
                fresh = fresh * inside_bottom
            held[a:b] = fresh

        adjoint(margin, emit_alpha, not final)


def fused_picks(members, lat_count, x, control, kappa, cells, counts, innov, prec):
    _, levels, rows, columns = x.shape
    slots = cells.shape[1]
    spots = rows // members * levels
    count = len(picks_plan(members))
    vregs = lambda *lead: pltpu.VMEM(lead + (SUBLANES, LANES), jnp.float32)
    floats = lambda *shape: pltpu.VMEM(shape, jnp.float32)
    deep = rows + 2 * HALO
    tiles = members + 2
    place = pl.BlockSpec(memory_space=pltpu.HBM)
    in_hbm = lambda array: pltpu.with_memory_space_constraint(array, pltpu.HBM)
    flat = lambda dtype: pltpu.VMEM((levels * rows, columns), dtype)
    out = pl.pallas_call(
        functools.partial(picks_kernel, members, lat_count),
        out_shape=jax.ShapeDtypeStruct((levels * rows, columns), jnp.float32),
        in_specs=[place] * 4 + [pl.BlockSpec(memory_space=pltpu.SMEM)] + [place] * 2,
        out_specs=pl.BlockSpec(memory_space=pltpu.VMEM),
        scratch_shapes=[
            flat(x.dtype),
            pltpu.VMEM(cells.shape, cells.dtype),
            floats(*innov.shape),
            floats(*prec.shape),
            pltpu.SemaphoreType.DMA((2 * levels + 4,)),
            flat(jnp.float32),
        ]
        + [vregs(rows)] * 3
        + [vregs(deep)] * 6
        + [vregs(SWEEPS, deep)]
        + [vregs(GROUP)] * 6
        + [vregs(SWEEPS, GROUP), vregs(GROUP)]
        + [vregs(SWEEPS), vregs(HALO), vregs(HALO)]
        + [vregs(GROUP), vregs(GROUP // 2)] * 2
        + [vregs(2)] * 2
        + [vregs(2, 2)] * 2
        + [
            vregs(rows),
            floats(4, slots),
            floats(2, tiles, 4, slots),
            floats(2, tiles, slots),
            floats(2, tiles, slots),
            floats(STEPS, members, slots),
            floats(STEPS, members, 2, tiles, slots),
            pltpu.VMEM((tiles, spots, slots), jnp.bfloat16),
            pltpu.VMEM((tiles, LANES, slots), jnp.bfloat16),
            pltpu.VMEM((spots, tiles * slots), jnp.bfloat16),
            pltpu.VMEM((LANES, tiles * slots), jnp.bfloat16),
            pltpu.SemaphoreType.DMA((count,)),
            pltpu.SemaphoreType.DMA((count,)),
        ],
        compiler_params=pltpu.CompilerParams(
            collective_id=1, has_side_effects=True, vmem_limit_bytes=24 * 2**20
        ),
    )(
        in_hbm(x.reshape(levels * rows, columns)),
        in_hbm(control.reshape(levels * rows, columns)),
        in_hbm(kappa.reshape(levels * rows, columns)),
        in_hbm(cells),
        counts,
        in_hbm(innov),
        in_hbm(prec),
    )
    return (step_length * out).reshape(1, levels, rows, columns)


def fits_picks(members, lat_count, lon_count, x, cells):
    return (
        fits(members, lat_count, lon_count, x, cells)
        and lon_count == 2
        and 2 <= members
        and (members + 2) * SLOT <= LANES
        and x.shape[2] // members == HALO == GROUP == 2 * SWEEPS
        and cells.shape[1] % LANES == 0
    )


def on_device(members, lat_count, lon_count, x, control, kappa, cells, counts, innov, prec):
    if not fits(members, lat_count, lon_count, x, cells):
        return per_device(x, control, kappa, cells, counts, innov, prec)
    if fits_picks(members, lat_count, lon_count, x, cells):
        return fused_picks(members, lat_count, x, control, kappa, cells, counts, innov, prec)
    tile_rows = x.shape[2] // members
    return fused(
        members, lat_count, lon_count, tile_rows, x, control, kappa, cells, counts, innov, prec
    )


def solution(mesh):
    return jax.shard_map(
        functools.partial(
            on_device, mesh.shape["mem"], mesh.shape["lat"], mesh.shape["lon"]
        ),
        mesh=mesh,
        in_specs=(
            P("mem", None, "lat", "lon"),
            P("mem", None, "lat", "lon"),
            P(None, "lat", "lon"),
            P(("mem", "lat", "lon"), None),
            P(("mem", "lat", "lon")),
            P(("mem", "lat", "lon"), None),
            P(("mem", "lat", "lon"), None),
        ),
        out_specs=P("mem", None, "lat", "lon"),
        check_vma=False,
    )
```

```python
import functools
import math

import jax
import jax.numpy as jnp
from jax import lax
from jax.experimental import pallas as pl
from jax.experimental.pallas import tpu as pltpu
from jax.sharding import PartitionSpec as P

SWEEPS = 4
STEPS = 2


huber_edge = 1.5
step_length = 0.5


def with_halo(cells, sides, width):
    for axis, dim in sides:
        count = lax.axis_size(axis)
        head = lax.slice_in_dim(cells, 0, width, axis=dim)
        tail = lax.slice_in_dim(cells, cells.shape[dim] - width, cells.shape[dim], axis=dim)
        cells = jnp.concatenate(
            [
                lax.ppermute(tail, axis, [(i, (i + 1) % count) for i in range(count)]),
                cells,
                lax.ppermute(head, axis, [((i + 1) % count, i) for i in range(count)]),
            ],
            axis=dim,
        )
    return cells


def inside_rows(lat_rows, margin):
    first_row = lax.axis_index("lat") * lat_rows - margin
    global_rows = first_row + jnp.arange(lat_rows + 2 * margin, dtype=jnp.int32)
    total_rows = lat_rows * lax.axis_size("lat")
    return ((global_rows >= 0) & (global_rows < total_rows)).astype(jnp.float32)[None, :, None]


def stencil(padded):
    center = padded[:, 1:-1, 1:-1]
    laplace_term = (
        padded[:, :-2, 1:-1]
        + padded[:, 2:, 1:-1]
        + padded[:, 1:-1, :-2]
        + padded[:, 1:-1, 2:]
        - 4.0 * center
    )
    return (laplace_term, center)


def smooth_deep(state_field, kappa_rim):
    lat_rows = state_field.shape[1]
    padded = with_halo(state_field, (("lat", 1), ("lon", 2)), SWEEPS)
    padded = padded * inside_rows(lat_rows, SWEEPS)
    for sweep_index in range(SWEEPS):
        offset = sweep_index + 1
        local_kappa = kappa_rim[
            :, offset : kappa_rim.shape[1] - offset, offset : kappa_rim.shape[2] - offset
        ]
        laplace_term, center = stencil(padded)
        padded = (center + local_kappa * laplace_term) * inside_rows(lat_rows, SWEEPS - offset)
    return padded


def adjoint_deep(state_field, kappa_rim):
    lat_rows = state_field.shape[1]
    padded = with_halo(state_field, (("lat", 1), ("lon", 2)), SWEEPS)
    padded = padded * inside_rows(lat_rows, SWEEPS)
    for sweep_index in range(SWEEPS):
        local_kappa = kappa_rim[
            :,
            sweep_index : kappa_rim.shape[1] - sweep_index,
            sweep_index : kappa_rim.shape[2] - sweep_index,
        ]
        laplace_term, center = stencil(local_kappa * padded)
        padded = (padded[:, 1:-1, 1:-1] + laplace_term) * inside_rows(
            lat_rows, SWEEPS - sweep_index - 1
        )
    return padded


def per_device(
    perturbations, control, diffusivity, obs_cells, obs_counts, innovations, obs_precision
):
    members = lax.axis_size("mem")
    weight = 1.0 / math.sqrt(members - 1)
    member_x = perturbations[0]
    alpha_now = control[0]
    live_slots = (
        jnp.arange(obs_cells.shape[1], dtype=jnp.int32)[None, :] < obs_counts[:, None]
    ).astype(jnp.float32)
    masked_weight = obs_precision * live_slots
    kappa_rim = with_halo(diffusivity, (("lat", 1), ("lon", 2)), SWEEPS)
    for step_index in range(STEPS):
        smoothed = smooth_deep(alpha_now, kappa_rim)
        member_term = member_x.astype(jnp.float32) * smoothed
        owned_piece = lax.psum_scatter(member_term, "mem", scatter_dimension=1, tiled=True)
        increment = weight * owned_piece
        tile_cells = obs_cells[0]
        observed = increment.reshape(-1)[tile_cells]
        misfit = (observed - innovations[0]) * masked_weight[0]
        pulled = jnp.clip(misfit, -huber_edge, huber_edge) * masked_weight[0]
        tile_field = (
            jnp.zeros((increment.size,), jnp.float32)
            .at[tile_cells]
            .add(pulled)
            .reshape(increment.shape)
        )
        forcing = lax.all_gather(tile_field, "mem", axis=1, tiled=True)
        source = weight * member_x.astype(jnp.float32) * forcing
        gradient = alpha_now + adjoint_deep(source, kappa_rim)
        alpha_now = alpha_now - step_length * gradient
    return alpha_now[None]


LANES = 128
SUBLANES = 8
HALO = STEPS * SWEEPS
SLOT = 2 * HALO
GROUP = LANES // SLOT
MESH = pl.DeviceIdType.MESH


def copy_plan(members, peers, edge_tiles):
    keys = []
    for field in ("alpha", "kappa", "kappa_far", "x"):
        keys += [(field, "row", side) for side in (-1, 1)]
    for pack in ("pack", "packx"):
        keys += [(pack, side, peer) for side in (-1, 0, 1) for peer in range(peers)]
    keys += [("cells", hop) for hop in range(1, members)]
    for step in range(STEPS):
        keys += [("sum", step, hop) for hop in range(1, members)]
        keys += [("tile", step, hop) for hop in range(1, members)]
        keys += [("edge", step, peer, hop) for peer in range(peers) for hop in range(members)]
    numbers = {key: number for number, key in enumerate(keys)}
    received = len(keys)
    for side in (-1, 1):
        numbers["cells_row", side] = received
        received += edge_tiles
    for step in range(STEPS):
        for side in (-1, 1):
            numbers["row", step, side] = received
            received += edge_tiles
            for peer in range(peers):
                numbers["corner", step, side, peer] = received
                received += edge_tiles
    sent = len(keys)
    for side in (-1, 1):
        numbers["cells_out", side] = sent
        sent += members
    for step in range(STEPS):
        for side in (-1, 1):
            numbers["row_out", step, side] = sent
            sent += members
            for peer in range(peers):
                numbers["corner_out", step, side, peer] = sent
                sent += members
    return numbers, sent, received


def kernel(
    members,
    lat_count,
    lon_count,
    tile_rows,
    x_in,
    control_in,
    kappa_in,
    cells_in,
    counts_ref,
    innovations_in,
    precision_in,
    out_ref,
    x_ref,
    control_ref,
    kappa_ref,
    cells_ref,
    innovations_ref,
    precision_ref,
    load_sems,
    x_flat,
    alpha_o,
    alpha_h,
    kappa_o,
    kappa_h,
    wx_o,
    wx_h,
    work_o,
    work_h,
    next_o,
    next_h,
    forcing_o,
    forcing_h,
    pack_out,
    pack_in,
    packx_out,
    packx_in,
    edge_out,
    edge_in,
    terms,
    pieces,
    pulled_out,
    pulled_in,
    cells_all,
    rows_hot,
    cols_hot,
    send_sems,
    recv_sems,
):
    levels = SUBLANES
    rows = control_ref.shape[0] // levels
    slots = cells_ref.shape[1]
    groups = rows // GROUP
    edge_tiles = HALO // tile_rows
    peers = [1] if lon_count == 2 else [1, lon_count - 1]
    numbers, _, _ = copy_plan(members, len(peers), edge_tiles)
    weight = 1.0 / math.sqrt(members - 1)
    mem = lax.axis_index("mem")
    lat = lax.axis_index("lat")
    lon = lax.axis_index("lon")
    has = {-1: lat > 0, 0: None, 1: lat < lat_count - 1}

    def guarded(condition, run):
        if condition is None:
            run()
        else:
            pl.when(condition)(run)

    def device(mem_hop, lat_hop, lon_hop):
        return (
            lax.rem(mem + mem_hop, members),
            lat + lat_hop,
            lax.rem(lon + lon_hop, lon_count),
        )

    def far(peer):
        return len(peers) - 1 - peer

    def remote(src, dst, send_number, recv_number, target):
        return pltpu.make_async_remote_copy(
            src_ref=src,
            dst_ref=dst,
            send_sem=send_sems.at[send_number],
            recv_sem=recv_sems.at[recv_number],
            device_id=target,
            device_id_type=MESH,
        )

    pending = []

    def send(condition, src, dst, send_number, recv_number, target):
        guarded(condition, lambda: remote(src, dst, send_number, recv_number, target).start())
        pending.append((condition, src, send_number))

    def settle(name=None):
        kept = []
        for condition, src, number in pending:
            if name is None or number in (numbers[name, "row", -1], numbers[name, "row", 1]):
                guarded(
                    condition,
                    lambda: remote(src, src, number, 0, device(0, 0, peers[0])).wait_send(),
                )
            else:
                kept.append((condition, src, number))
        pending[:] = kept

    def await_in(condition, dst, recv_number):
        guarded(
            condition,
            lambda: remote(dst, dst, 0, recv_number, device(0, 0, peers[0])).wait_recv(),
        )

    loads = [
        pltpu.make_async_copy(src, dst, load_sems.at[number])
        for number, (src, dst) in enumerate(
            (
                (control_in, control_ref),
                (kappa_in, kappa_ref),
                (x_in, x_ref),
                (cells_in, cells_ref),
                (innovations_in, innovations_ref),
                (precision_in, precision_ref),
            )
        )
    ]
    for load in loads:
        load.start()

    barrier = pltpu.get_barrier_semaphore()
    for lat_hop in (0, -1, 1):
        def greet(lat_hop=lat_hop):
            for lon_hop in [0] + peers:
                for mem_hop in range(members if lon_hop == 0 else 1):
                    if (lat_hop, lon_hop, mem_hop) != (0, 0, 0):
                        pl.semaphore_signal(
                            barrier,
                            inc=1,
                            device_id=device(mem_hop, lat_hop, lon_hop),
                            device_id_type=MESH,
                        )
        guarded(has[lat_hop], greet)

    lane = lax.broadcasted_iota(jnp.int32, (1, SUBLANES, LANES), 2)
    lane2 = lane[0]

    for load in loads:
        load.wait()
    x_flat[...] = weight * x_ref[...].astype(jnp.float32)
    for r in range(rows):
        level_rows = pl.ds(r, levels, stride=rows)
        alpha_o[HALO + r] = control_ref[level_rows, :]
        kappa_o[HALO + r] = kappa_ref[level_rows, :]
        wx_o[HALO + r] = x_flat[level_rows, :]

    def packed(read, count):
        total = jnp.zeros((SUBLANES, LANES), jnp.float32)
        for j in range(count):
            shifted = pltpu.roll(read(j), (HALO + SLOT * j) % LANES, 1)
            total = jnp.where(lane2 // SLOT == j, shifted, total)
        return total

    def unpacked(read, j):
        shift = (LANES - HALO - SLOT * j) % LANES
        parts = [pltpu.roll(read(peer), shift, 1) if shift else read(peer) for peer in range(len(peers))]
        if len(parts) == 1:
            return parts[0]
        return jnp.where(lane2 < LANES // 2, parts[0], parts[1])

    for g in range(groups):
        base = HALO + g * GROUP
        pack_out[g, 0] = packed(lambda j: alpha_o[base + j], GROUP)
        pack_out[g, 1] = packed(lambda j: kappa_o[base + j], GROUP)
        packx_out[g] = packed(lambda j: wx_o[base + j], GROUP)

    zero_rows = jnp.zeros((HALO, SUBLANES, LANES), jnp.float32)
    for side in (-1, 1):
        start = 0 if side < 0 else HALO + rows
        group = 0 if side < 0 else groups + 1
        tile = 0 if side < 0 else edge_tiles + members

        def clear(start=start, group=group, tile=tile):
            for ref in (alpha_o, kappa_o, wx_o):
                ref[start : start + HALO] = zero_rows
            cells_all[tile : tile + edge_tiles] = jnp.zeros((edge_tiles, 1, slots), jnp.int32)
            for step in range(STEPS):
                pulled_in[step, tile : tile + edge_tiles] = jnp.zeros(
                    (edge_tiles, 1, slots), jnp.float32
                )
            for peer in range(len(peers)):
                pack_in[peer, group] = jnp.zeros((2, SUBLANES, LANES), jnp.float32)
                packx_in[peer, group] = jnp.zeros((SUBLANES, LANES), jnp.float32)
                for step in range(STEPS):
                    edge_in[step, peer, tile : tile + edge_tiles] = jnp.zeros(
                        (edge_tiles, SUBLANES, LANES), jnp.float32
                    )

        guarded(jnp.logical_not(has[side]), clear)

    greeted = len(peers) + members
    lat_near = 1 + (lat > 0).astype(jnp.int32) + (lat < lat_count - 1).astype(jnp.int32)
    pl.semaphore_wait(barrier, greeted * lat_near - 1)

    def row_copies(name, field, width, skip=0):
        for side in (-1, 1):
            source = HALO + skip if side < 0 else HALO + rows - width - skip
            target = HALO + rows + skip if side < 0 else HALO - width - skip
            send(
                has[side],
                field.at[pl.ds(source, width)],
                field.at[pl.ds(target, width)],
                numbers[name, "row", side],
                numbers[name, "row", -side],
                device(0, side, 0),
            )

    def row_waits(name, field, width, skip=0):
        for side in (-1, 1):
            start = HALO - width - skip if side < 0 else HALO + rows + skip
            await_in(has[side], field.at[pl.ds(start, width)], numbers[name, "row", side])

    def pack_copies(name, source, target):
        for side in (0, -1, 1):
            for peer, hop in enumerate(peers):
                if side == 0:
                    src, dst = source, target.at[far(peer), pl.ds(1, groups)]
                elif side < 0:
                    src, dst = source.at[0], target.at[far(peer), groups + 1]
                else:
                    src, dst = source.at[groups - 1], target.at[far(peer), 0]
                send(
                    has[side],
                    src,
                    dst,
                    numbers[name, side, peer],
                    numbers[name, -side, far(peer)],
                    device(0, side, hop),
                )

    def pack_waits(name, target):
        for side in (0, -1, 1):
            for peer in range(len(peers)):
                if side == 0:
                    dst = target.at[peer, pl.ds(1, groups)]
                else:
                    dst = target.at[peer, 0 if side < 0 else groups + 1]
                await_in(has[side], dst, numbers[name, side, peer])

    pack_copies("pack", pack_out, pack_in)
    row_copies("alpha", alpha_o, SWEEPS)
    row_copies("kappa", kappa_o, SWEEPS)
    pack_copies("packx", packx_out, packx_in)
    row_copies("kappa_far", kappa_o, HALO - SWEEPS, SWEEPS)
    row_copies("x", wx_o, HALO)

    def to_group(step, source, target, name):
        for hop in range(1, members):
            send(
                None,
                source,
                target.at[edge_tiles + mem],
                numbers[name + (hop,)],
                numbers[name + (hop,)],
                device(hop, 0, 0),
            )
        outs, ins = ("cells_out", "cells_row") if step is None else ("row_out", "row")
        key = () if step is None else (step,)
        for side in (-1, 1):
            near = mem - (0 if side < 0 else members - edge_tiles)
            inside = near < edge_tiles if side < 0 else near >= 0
            for hop in range(members):
                send(
                    jnp.logical_and(has[side], inside),
                    source,
                    target.at[near + (edge_tiles + members if side < 0 else 0)],
                    numbers[(outs,) + key + (side,)] + hop,
                    numbers[(ins,) + key + (-side,)] + near,
                    device(hop, side, 0),
                )

    def others():
        for hop in range(1, members):
            yield None, hop, edge_tiles + lax.rem(mem + members - hop, members)
        for side in (-1, 1):
            for i in range(edge_tiles):
                yield side, i, i + (0 if side < 0 else edge_tiles + members)

    to_group(None, cells_ref, cells_all, ("cells",))

    spots = tile_rows * levels

    def hot(spot, cells):
        column = lax.rem(cells, LANES)
        tile_row = lax.rem(lax.div(cells, LANES), tile_rows)
        level = lax.div(cells, LANES * tile_rows)
        place = tile_row * levels + level
        rows_hot[spot] = (
            lax.broadcasted_iota(jnp.int32, (spots, slots), 0) == place
        ).astype(jnp.float32).astype(jnp.bfloat16)
        cols_hot[spot] = (
            lax.broadcasted_iota(jnp.int32, (LANES, slots), 0) == column
        ).astype(jnp.float32).astype(jnp.bfloat16)

    def spread(spot, pulled):
        tile = jnp.zeros((spots, LANES), jnp.float32)
        for half in halves(pulled):
            tile = tile + lax.dot_general(
                rows_hot[spot] * half,
                cols_hot[spot],
                (((1,), (1,)), ((), ())),
                preferred_element_type=jnp.float32,
            )
        return tile.reshape(tile_rows, SUBLANES, LANES)

    mine = edge_tiles + mem
    hot(mine, cells_ref[...])
    live = (
        lax.broadcasted_iota(jnp.int32, (1, slots), 1) < counts_ref[0]
    ).astype(jnp.float32)
    masked_weight = precision_ref[...] * live
    innovations = innovations_ref[...]

    def halves(value):
        high = value.astype(jnp.bfloat16)
        return high, (value - high.astype(jnp.float32)).astype(jnp.bfloat16)

    first_lane, last_lane = lane == 0, lane == LANES - 1

    def sides(own, near):
        own_w, near_w = pltpu.roll(own, 1, 2), pltpu.roll(near, 1, 2)
        own_e, near_e = pltpu.roll(own, LANES - 1, 2), pltpu.roll(near, LANES - 1, 2)
        return (
            jnp.where(first_lane, near_w, own_w) + jnp.where(last_lane, near_e, own_e),
            jnp.where(first_lane, own_w, near_w) + jnp.where(last_lane, own_e, near_e),
        )

    def chunks(margin):
        first, last = HALO - margin, HALO + rows + margin
        return [(a, min(a + 8, last)) for a in range(first, last, 8)]

    def smooth_sweep(src, dst, margin, emit=None):
        for a, b in chunks(margin):
            own, near = src[0][a:b], src[1][a:b]
            beside = sides(own, near)
            for ref, value, both, kappa, out in (
                (src[0], own, beside[0], kappa_o, dst[0]),
                (src[1], near, beside[1], kappa_h, dst[1]),
            ):
                if emit is not None and ref is src[1]:
                    continue
                total = ref[a - 1 : b - 1] + ref[a + 1 : b + 1] + both
                value = value + kappa[a:b] * (total - 4.0 * value)
                if emit is None:
                    out[a:b] = value
                else:
                    emit(a, b, value)

    def adjoint_sweep(src, dst, margin, emit=None, near_too=True):
        for a, b in chunks(margin):
            scaled = [
                kappa[a - 1 : b + 1] * ref[a - 1 : b + 1]
                for ref, kappa in ((src[0], kappa_o), (src[1], kappa_h))
            ]
            beside = sides(scaled[0][1:-1], scaled[1][1:-1])
            for which in (0, 1):
                if which and not near_too:
                    continue
                t = scaled[which]
                value = src[which][a:b] + (t[:-2] + t[2:] + beside[which] - 4.0 * t[1:-1])
                if emit is None:
                    dst[which][a:b] = value
                else:
                    emit(which, a, b, value)

    work, following = (work_o, work_h), (next_o, next_h)

    row_waits("alpha", alpha_o, SWEEPS)
    row_waits("kappa", kappa_o, SWEEPS)
    pack_waits("pack", pack_in)
    for e in range(rows + 2 * HALO):
        g, j = divmod(e, GROUP)
        alpha_h[e] = unpacked(lambda peer: pack_in[peer, g, 0], j)
        kappa_h[e] = unpacked(lambda peer: pack_in[peer, g, 1], j)

    for step in range(STEPS):
        term = terms.at[step]

        def emit_term(a, b, value):
            term[a - HALO : b - HALO] = wx_o[a:b] * value

        smooth_sweep((alpha_o, alpha_h), work, SWEEPS - 1)
        src, dst = work, following
        for sweep in range(1, SWEEPS):
            last = sweep == SWEEPS - 1
            smooth_sweep(src, dst, SWEEPS - 1 - sweep, emit_term if last else None)
            src, dst = dst, src

        for hop in range(1, members):
            target = lax.rem(mem + hop, members)
            send(
                None,
                term.at[pl.ds(target * tile_rows, tile_rows)],
                pieces.at[step, hop],
                numbers["sum", step, hop],
                numbers["sum", step, hop],
                device(hop, 0, 0),
            )
        total = term[pl.ds(mem * tile_rows, tile_rows)]
        if step == 0:
            row_waits("kappa_far", kappa_o, HALO - SWEEPS, SWEEPS)
            row_waits("x", wx_o, HALO)
            pack_waits("packx", packx_in)
            for e in range(rows + 2 * HALO):
                g, j = divmod(e, GROUP)
                wx_h[e] = unpacked(lambda peer: packx_in[peer, g], j)
            for side, i, spot in others():
                if side is None:
                    await_in(None, cells_all.at[spot], numbers["cells", i])
                else:
                    await_in(has[side], cells_all.at[spot], numbers["cells_row", side] + i)
            for _, _, spot in others():
                hot(spot, cells_all[spot])
        for hop in range(1, members):
            await_in(None, pieces.at[step, hop], numbers["sum", step, hop])
            total = total + pieces[step, hop]

        flipped = jnp.transpose(total.reshape(spots, LANES))
        hot_rows, hot_cols = rows_hot[mine], cols_hot[mine]
        observed = jnp.zeros((LANES, slots), jnp.float32)
        for half in halves(flipped):
            observed = observed + jnp.dot(half, hot_rows, preferred_element_type=jnp.float32)
        observed = jnp.sum(
            observed * hot_cols.astype(jnp.float32), axis=0, keepdims=True
        )
        misfit = (observed - innovations) * masked_weight
        pulled = jnp.clip(misfit, -huber_edge, huber_edge) * masked_weight
        pulled_out[step] = pulled
        to_group(step, pulled_out.at[step], pulled_in.at[step], ("tile", step))
        tile = spread(mine, pulled)
        edge_out[step] = packed(lambda j: tile[j], tile_rows)

        force_o, edges = forcing_o.at[step], edge_in.at[step]
        for side in (-1, 1):
            near = mem - (0 if side < 0 else members - edge_tiles)
            inside = near < edge_tiles if side < 0 else near >= 0
            condition = jnp.logical_and(has[side], inside)
            spot = near + (edge_tiles + members if side < 0 else 0)
            for peer, lon_hop in enumerate(peers):
                for hop in range(members):
                    send(
                        condition,
                        edge_out.at[step],
                        edges.at[far(peer), spot],
                        numbers["corner_out", step, side, peer] + hop,
                        numbers["corner", step, -side, far(peer)] + near,
                        device(hop, side, lon_hop),
                    )
        for peer, lon_hop in enumerate(peers):
            for hop in range(members):
                send(
                    None,
                    edge_out.at[step],
                    edges.at[far(peer), edge_tiles + mem],
                    numbers["edge", step, peer, hop],
                    numbers["edge", step, far(peer), hop],
                    device(hop, 0, lon_hop),
                )
        force_o[pl.ds(HALO + mem * tile_rows, tile_rows)] = tile

        for side, i, spot in others():
            if side is None:
                await_in(None, pulled_in.at[step, spot], numbers["tile", step, i])
            else:
                await_in(has[side], pulled_in.at[step, spot], numbers["row", step, side] + i)
        for _, _, spot in others():
            force_o[pl.ds(spot * tile_rows, tile_rows)] = spread(spot, pulled_in[step, spot])
        for peer in range(len(peers)):
            for hop in range(members):
                source = lax.rem(mem + members - hop, members)
                await_in(
                    None, edges.at[peer, edge_tiles + source], numbers["edge", step, peer, hop]
                )
        for side in (-1, 1):
            for i in range(edge_tiles):
                spot = i + (0 if side < 0 else edge_tiles + members)
                for peer in range(len(peers)):
                    await_in(
                        has[side],
                        edges.at[peer, spot],
                        numbers["corner", step, side, peer] + i,
                    )

        margin = HALO - step * SWEEPS
        for e in range(HALO - margin, HALO + rows + margin):
            t, j = divmod(e, tile_rows)
            forcing_h[e] = unpacked(lambda peer: edges[peer, t], j)
        for a, b in chunks(margin):
            work_o[a:b] = wx_o[a:b] * force_o[a:b]
            work_h[a:b] = wx_h[a:b] * forcing_h[a:b]

        final = step == STEPS - 1
        inside_top = (lat > 0).astype(jnp.float32)
        inside_bottom = (lat < lat_count - 1).astype(jnp.float32)

        def emit_alpha(which, a, b, value):
            held = (alpha_o, alpha_h)[which]
            old = held[a:b]
            if final:
                fresh = ((1.0 - step_length) / step_length) * old - value
                for r in range(a, b):
                    out_ref[pl.ds(r - HALO, levels, stride=rows), :] = fresh[r - a]
                return
            fresh = old - step_length * (old + value)
            for r in range(a, b):
                row = fresh[r - a]
                if r < HALO:
                    row = row * inside_top
                elif r >= HALO + rows:
                    row = row * inside_bottom
                held[r] = row

        if step == 0:
            settle("alpha")
        src, dst = work, following
        for sweep in range(SWEEPS):
            last = sweep == SWEEPS - 1
            adjoint_sweep(
                src, dst, margin - 1 - sweep, emit_alpha if last else None, not (last and final)
            )
            src, dst = dst, src

    settle()


def fused(members, lat_count, lon_count, tile_rows, x, control, kappa, cells, counts, innov, prec):
    _, levels, rows, columns = x.shape
    peers = 1 if lon_count == 2 else 2
    edge_tiles = HALO // tile_rows
    slots = cells.shape[1]
    groups = rows // GROUP
    _, sent, received = copy_plan(members, peers, edge_tiles)
    vregs = lambda *lead: pltpu.VMEM(lead + (SUBLANES, LANES), jnp.float32)
    deep = rows + 2 * HALO
    tiles = members + 2 * edge_tiles
    vmem = pl.BlockSpec(memory_space=pltpu.VMEM)
    place = pl.BlockSpec(memory_space=pltpu.HBM)
    in_hbm = lambda array: pltpu.with_memory_space_constraint(array, pltpu.HBM)
    flat = lambda dtype: pltpu.VMEM((levels * rows, columns), dtype)
    out = pl.pallas_call(
        functools.partial(kernel, members, lat_count, lon_count, tile_rows),
        out_shape=jax.ShapeDtypeStruct((levels * rows, columns), jnp.float32),
        in_specs=[place] * 4 + [pl.BlockSpec(memory_space=pltpu.SMEM)] + [place] * 2,
        out_specs=vmem,
        scratch_shapes=[
            flat(x.dtype),
            flat(jnp.float32),
            flat(jnp.float32),
            pltpu.VMEM(cells.shape, cells.dtype),
            pltpu.VMEM(innov.shape, innov.dtype),
            pltpu.VMEM(prec.shape, prec.dtype),
            pltpu.SemaphoreType.DMA((6,)),
            flat(jnp.float32),
        ]
        + [vregs(deep)] * 10
        + [
            vregs(STEPS, deep),
            vregs(deep),
            vregs(groups, 2),
            vregs(peers, groups + 2, 2),
            vregs(groups),
            vregs(peers, groups + 2),
            vregs(STEPS),
            vregs(STEPS, peers, tiles),
            vregs(STEPS, rows),
            vregs(STEPS, members, tile_rows),
            pltpu.VMEM((STEPS, 1, slots), jnp.float32),
            pltpu.VMEM((STEPS, tiles, 1, slots), jnp.float32),
            pltpu.VMEM((tiles, 1, slots), jnp.int32),
            pltpu.VMEM((tiles, tile_rows * levels, slots), jnp.bfloat16),
            pltpu.VMEM((tiles, LANES, slots), jnp.bfloat16),
            pltpu.SemaphoreType.DMA((sent,)),
            pltpu.SemaphoreType.DMA((received,)),
        ],
        compiler_params=pltpu.CompilerParams(
            collective_id=0, has_side_effects=True, vmem_limit_bytes=24 * 2**20
        ),
    )(
        in_hbm(x.reshape(levels * rows, columns)),
        in_hbm(control.reshape(levels * rows, columns)),
        in_hbm(kappa.reshape(levels * rows, columns)),
        in_hbm(cells),
        counts,
        in_hbm(innov),
        in_hbm(prec),
    )
    return (step_length * out).reshape(1, levels, rows, columns)


def fits(members, lat_count, lon_count, x, cells):
    _, levels, rows, columns = x.shape
    tile_rows = rows // members
    return (
        levels == SUBLANES
        and columns == LANES
        and rows % members == 0
        and rows % GROUP == 0
        and rows >= 2 * HALO
        and HALO % tile_rows == 0
        and tile_rows <= GROUP
        and HALO // tile_rows <= members
        and lon_count > 1
        and cells.shape[0] == 1
    )


def picks_plan(members):

    keys = []
    for field in ("alpha", "kappa", "kappa_far", "x"):
        keys += [(field, side) for side in (-1, 1)]
    keys += [("pack", 0), ("packx", 0)]
    keys += [(name, side) for name in ("corner", "far") for side in (-1, 1)]
    keys += [("obs", hop) for hop in range(1, members)] + [("obs_lon",)]
    keys += [("obs_edge", side, lon_hop) for side in (-1, 1) for lon_hop in (0, 1)]
    for step in range(STEPS):
        keys += [
            ("pick", step, hop, side, lon_hop)
            for hop in range(members)
            for side in (-1, 0, 1)
            for lon_hop in (0, 1)
        ]
    return {key: number for number, key in enumerate(keys)}


def picks_kernel(
    members,
    lat_count,
    x_in,
    control_in,
    kappa_in,
    cells_in,
    counts_ref,
    innovations_in,
    precision_in,
    out_ref,
    x_ref,
    cells_ref,
    innovations_ref,
    precision_ref,
    load_sems,
    x_flat,
    alpha_n,
    kappa_n,
    wx_n,
    alpha_o,
    kappa_o,
    wx_o,
    damp_o,
    work_o,
    next_o,
    path_o,
    alpha_d,
    kappa_d,
    wx_d,
    damp_d,
    work_d,
    next_d,
    path_d,
    near_d,
    edge_alpha,
    edge_kappa,
    edge_x,
    pack_out,
    packx_out,
    pack_in,
    packx_in,
    corner_out,
    corner_in,
    far_out,
    far_in,
    term,
    obs_out,
    obs_in,
    weights_all,
    values_all,
    picks_out,
    picks_in,
    rows_hot,
    cols_hot,
    rows_near,
    cols_near,
    send_sems,
    recv_sems,
):
    levels = SUBLANES
    rows = x_ref.shape[0] // levels
    slots = cells_ref.shape[1]
    blocks_count = members + 2
    tile_rows = rows // members
    spots = tile_rows * levels
    numbers = picks_plan(members)
    weight = 1.0 / math.sqrt(members - 1)
    mem = lax.axis_index("mem")
    lat = lax.axis_index("lat")
    lon = lax.axis_index("lon")
    has = {-1: lat > 0, 0: None, 1: lat < lat_count - 1}
    first, last = members, members + 1
    start_of = {t: HALO + t * tile_rows for t in range(members)}
    start_of[first], start_of[last] = 0, HALO + rows

    def guarded(condition, run):
        if condition is None:
            run()
        else:
            pl.when(condition)(run)

    def both(one, other):
        return other if one is None else jnp.logical_and(one, other)

    def device(mem_hop, lat_hop, lon_hop):
        return (
            lax.rem(mem + mem_hop, members) if mem_hop else mem,
            lat + lat_hop if lat_hop else lat,
            1 - lon if lon_hop else lon,
        )

    def remote(src, dst, send_number, recv_number, target):
        return pltpu.make_async_remote_copy(
            src_ref=src,
            dst_ref=dst,
            send_sem=send_sems.at[send_number],
            recv_sem=recv_sems.at[recv_number],
            device_id=target,
            device_id_type=MESH,
        )

    pending = []

    def send(condition, copies):
        for src, dst, send_key, recv_key, target in copies:
            copy = remote(src, dst, numbers[send_key], numbers[recv_key], target)
            guarded(condition, copy.start)
        pending.append((condition, [(src, key) for src, _, key, _, _ in copies]))

    def settle(name=None):
        kept = []
        for condition, copies in pending:
            chosen = [c for c in copies if name is None or c[1][0] == name]
            others = [c for c in copies if not (name is None or c[1][0] == name)]

            def run(chosen=chosen):
                for src, key in chosen:
                    remote(src, src, numbers[key], 0, device(0, 0, 1)).wait_send()

            if chosen:
                guarded(condition, run)
            if others:
                kept.append((condition, others))
        pending[:] = kept

    def await_in(condition, arrivals):
        def run():
            for dst, key in arrivals:
                remote(dst, dst, 0, numbers[key], device(0, 0, 1)).wait_recv()

        guarded(condition, run)

    def rows_in(source, target, first_sem):
        return [
            pltpu.make_async_copy(
                source.at[pl.ds(level * rows, rows)],
                target.at[pl.ds(0, rows), level],
                load_sems.at[first_sem + level],
            )
            for level in range(levels)
        ]

    alpha_loads = rows_in(control_in, alpha_n, 0)
    kappa_loads = rows_in(kappa_in, kappa_n, levels)
    loads = [
        pltpu.make_async_copy(src, dst, load_sems.at[2 * levels + number])
        for number, (src, dst) in enumerate(
            (
                (x_in, x_ref),
                (cells_in, cells_ref),
                (innovations_in, innovations_ref),
                (precision_in, precision_ref),
            )
        )
    ]
    barrier = pltpu.get_barrier_semaphore()

    def greet(*hops):
        pl.semaphore_signal(barrier, inc=1, device_id=device(*hops), device_id_type=MESH)

    for side in (-1, 1):

        def greet_side(side=side):
            for lon_hop in (1, 0):
                greet(0, side, lon_hop)

        guarded(has[side], greet_side)
    greet(0, 0, 1)
    for hop in range(1, members):
        greet(hop, 0, 0)

    for load in alpha_loads + kappa_loads + loads:
        load.start()

    lane = lax.broadcasted_iota(jnp.int32, (1, SUBLANES, LANES), 2)
    slot = lax.rem(lax.div(lane[0] + HALO, SLOT), LANES // SLOT)
    half_turn = LANES // 2

    def turned(value, lanes, axis=1):
        lanes %= LANES
        return pltpu.roll(value, lanes, axis) if lanes else value

    def into_frames(source, target):
        for r in range(rows):
            block = r // GROUP + 1
            target[HALO + r] = turned(source[r], SLOT * block)

    def by_slot(rows_of, i):
        total = rows_of[GROUP + i]
        for block in range(2, members + 1):
            total = jnp.where(slot == block, rows_of[GROUP * block + i], total)
        return total

    low_slots = (slot >= 1) & (slot <= members)
    up_frame = SLOT * (blocks_count - 1)

    for load in alpha_loads:
        load.wait()
    into_frames(alpha_n, alpha_o)
    for r in range(SWEEPS):
        edge_alpha[r] = turned(alpha_n[r], up_frame)
    for load in kappa_loads:
        load.wait()
    into_frames(kappa_n, kappa_o)
    for r in range(HALO):
        edge_kappa[r] = turned(kappa_n[r], up_frame)
    for i in range(GROUP):
        pack_out[i] = jnp.where(
            low_slots, by_slot(alpha_o, i), turned(by_slot(kappa_o, i), half_turn)
        )

    def gathered(rows_of, wanted):
        total = None
        for place, row in enumerate(wanted):
            shifted = turned(rows_of(row), SLOT * place - SLOT * (row // GROUP))
            total = shifted if total is None else jnp.where(slot % len(wanted) == place, shifted, total)
        return total

    def edge_rows(side, begin, end):
        block = 1 if side < 0 else members
        return [GROUP * block + i for i in range(begin, end)]

    for side in (-1, 1):
        begin = 0 if side < 0 else GROUP - SWEEPS
        corner_out[max(side, 0)] = gathered(
            lambda row: pack_out[row % GROUP], edge_rows(side, begin, begin + SWEEPS)
        )

    for load in loads[1:]:
        load.wait()
    cells = cells_ref[...]
    column = lax.rem(cells, LANES)
    tile_row = lax.rem(lax.div(cells, LANES), tile_rows)
    level = lax.div(cells, LANES * tile_rows)
    live = (
        lax.broadcasted_iota(jnp.int32, (1, slots), 1) < counts_ref[0]
    ).astype(jnp.float32)
    my_obs = jnp.concatenate(
        [
            column.astype(jnp.float32),
            (tile_row * levels + level).astype(jnp.float32),
            precision_ref[...] * live,
            innovations_ref[...],
        ],
        axis=0,
    )
    obs_out[...] = my_obs
    obs_in[0, mem] = my_obs
    near_lat = (lat > 0).astype(jnp.int32) + (lat < lat_count - 1).astype(jnp.int32)
    pl.semaphore_wait(barrier, members + 2 * near_lat)

    def row_copy(name, side, natural, edge, field, width, skip=0):
        if side < 0:
            src, dst = edge.at[pl.ds(skip, width)], field.at[pl.ds(HALO + rows + skip, width)]
        else:
            src = natural.at[pl.ds(rows - width - skip, width)]
            dst = field.at[pl.ds(HALO - width - skip, width)]
        return src, dst, (name, side), (name, -side), device(0, side, 0)

    def row_arrival(name, field, width, side, skip=0):
        start = HALO - width - skip if side < 0 else HALO + rows + skip
        return field.at[pl.ds(start, width)], (name, side)

    def side_copy(name, source, target, side):
        at, to = max(side, 0), max(-side, 0)
        return source.at[at], target.at[to], (name, side), (name, -side), device(0, side, 1)

    def side_arrival(name, target, side):
        return target.at[max(side, 0)], (name, side)

    def whole_copy(name, source, target):
        return source, target, (name, 0), (name, 0), device(0, 0, 1)

    for side in (-1, 1):
        send(has[side], [side_copy("corner", corner_out, corner_in, side)])
    send(None, [whole_copy("pack", pack_out, pack_in)])
    send(
        None,
        [
            (obs_out, obs_in.at[0, mem], ("obs", hop), ("obs", hop), device(hop, 0, 0))
            for hop in range(1, members)
        ],
    )

    for side in (-1, 1):
        send(
            has[side],
            [
                row_copy("alpha", side, alpha_n, edge_alpha, alpha_o, SWEEPS),
                row_copy("kappa", side, kappa_n, edge_kappa, kappa_o, SWEEPS),
            ],
        )

    loads[0].wait()
    x_flat[...] = weight * x_ref[...].astype(jnp.float32)
    for r in range(rows):
        wx_n[r] = x_flat[pl.ds(r, levels, stride=rows), :]
    into_frames(wx_n, wx_o)
    for r in range(HALO):
        edge_x[r] = turned(wx_n[r], up_frame)
    for i in range(GROUP // 2):
        packx_out[i] = jnp.where(
            low_slots, by_slot(wx_o, i), turned(by_slot(wx_o, i + GROUP // 2), half_turn)
        )
    for side in (-1, 1):
        begin = SWEEPS if side < 0 else 0
        far_out[max(side, 0), 0] = gathered(lambda row: wx_o[row], edge_rows(side, 0, GROUP))
        far_out[max(side, 0), 1] = gathered(
            lambda row: kappa_o[row], edge_rows(side, begin, begin + GROUP - SWEEPS)
        )
    for side in (-1, 1):
        send(
            has[side],
            [
                side_copy("far", far_out, far_in, side),
                row_copy(
                    "kappa_far", side, kappa_n, edge_kappa, kappa_o, HALO - SWEEPS, SWEEPS
                ),
                row_copy("x", side, wx_n, edge_x, wx_o, HALO),
            ],
        )
    send(None, [whole_copy("packx", packx_out, packx_in)])

    zero_rows = jnp.zeros((HALO, SUBLANES, LANES), jnp.float32)
    for side in (-1, 1):

        def clear(side=side):
            start = 0 if side < 0 else HALO + rows
            tile = first if side < 0 else last
            for ref in (alpha_o, kappa_o, wx_o):
                ref[start : start + HALO] = zero_rows
            corner_in[max(side, 0)] = zero_rows[0]
            far_in[max(side, 0)] = zero_rows[:2]
            for lon_hop in (0, 1):
                obs_in[lon_hop, tile] = jnp.zeros((4, slots), jnp.float32)
                for step in range(STEPS):
                    for hop in range(members):
                        picks_in[step, hop, lon_hop, tile : tile + 1] = jnp.zeros(
                            (1, slots), jnp.float32
                        )

        guarded(jnp.logical_not(has[side]), clear)

    lane_of = lax.broadcasted_iota(jnp.int32, (LANES, slots), 0).astype(jnp.float32)
    spot_of = lax.broadcasted_iota(jnp.int32, (spots, slots), 0).astype(jnp.float32)

    def hot(lon_hop, tile):
        place = obs_in.at[lon_hop, tile]
        column = place[0:1, :]
        in_frame = column + float(SLOT * (start_of[tile] // GROUP))
        in_frame = jnp.where(in_frame >= LANES, in_frame - LANES, in_frame)
        row_ones = (spot_of == place[1:2, :]).astype(jnp.float32).astype(jnp.bfloat16)
        if lon_hop:
            inside = (column >= HALO) & (column < LANES - HALO)
            in_frame = jnp.where(inside, -1.0, in_frame)
        column_ones = (lane_of == in_frame).astype(jnp.float32).astype(jnp.bfloat16)
        if lon_hop:
            rows_near[:, tile * slots : (tile + 1) * slots] = row_ones
            cols_near[:, tile * slots : (tile + 1) * slots] = column_ones
        else:
            rows_hot[tile] = row_ones
            cols_hot[tile] = column_ones
        weights_all[lon_hop, tile : tile + 1, :] = place[2:3, :]
        values_all[lon_hop, tile : tile + 1, :] = place[3:4, :]

    def halves(value):
        high = value.astype(jnp.bfloat16)
        return high, (value - high.astype(jnp.float32)).astype(jnp.bfloat16)

    def beside(own, deep, begin, end, deep_too):
        deep_w, deep_e = pltpu.roll(deep, 1, 2), pltpu.roll(deep, LANES - 1, 2)
        west, east = [deep_w[i] for i in range(GROUP)], [deep_e[i] for i in range(GROUP)]
        for block in range(blocks_count):
            a, b = max(begin, GROUP * block), min(end, GROUP * (block + 1))
            if a >= b:
                continue
            i, j = a - GROUP * block, b - GROUP * block
            around = own(a - 1, b + 1)
            middle = around[1:-1]
            up = [around[r] for r in range(b - a)]
            down = [around[r + 2] for r in range(b - a)]
            if i == 0:
                up[0] = turned(up[0], SLOT)
            if j == GROUP:
                down[-1] = turned(down[-1], -SLOT)
            own_w, own_e = pltpu.roll(middle, 1, 2), pltpu.roll(middle, LANES - 1, 2)
            at_w = lane == SLOT * block % LANES
            at_e = lane == (SLOT * block - 1) % LANES
            total = (
                jnp.where(at_w, deep_w[i:j], own_w)
                + jnp.where(at_e, deep_e[i:j], own_e)
                + (jnp.stack(up) + jnp.stack(down))
            )
            if deep_too:
                for r in range(i, j):
                    west[r] = jnp.where(at_w[0], own_w[r - i], west[r])
                    east[r] = jnp.where(at_e[0], own_e[r - i], east[r])
            yield block, a, b, total
        if deep_too:
            up = [turned(deep[GROUP - 1], SLOT)] + [deep[i] for i in range(GROUP - 1)]
            down = [deep[i] for i in range(1, GROUP)] + [turned(deep[0], -SLOT)]
            yield None, 0, GROUP, (
                jnp.stack(west) + jnp.stack(east) + (jnp.stack(up) + jnp.stack(down))
            )

    def smooth_sweep(src, dst, margin, emit=None):
        begin, end = HALO - margin, HALO + rows + margin
        own = lambda a, b: src[0][a:b]
        for block, a, b, total in beside(own, src[1][...], begin, end, emit is None):
            if block is None:
                dst[1][...] = damp_d[...] * src[1][...] + kappa_d[...] * total
                continue
            value = damp_o[a:b] * src[0][a:b] + kappa_o[a:b] * total
            if emit is None:
                dst[0][a:b] = value
            else:
                emit(a, b, value)

    path = [(path_o.at[n], path_d.at[n]) for n in range(SWEEPS)]

    def path_sum(which, part):
        total = path[0][which][part]
        for n in range(1, SWEEPS):
            total = total + path[n][which][part]
        return total

    def adjoint(margin, emit, deep_too):
        for n in range(SWEEPS - 1):
            smooth_sweep(path[n], path[n + 1], margin - 1 - n)
        margin -= SWEEPS
        begin, end = HALO - margin, HALO + rows + margin
        own = lambda a, b: path_sum(0, slice(a, b))
        deep = path_sum(1, slice(None))
        for block, a, b, total in beside(own, deep, begin, end, deep_too):
            if block is None:
                emit(block, a, b, work_d[...] + (total - 4.0 * deep))
            else:
                emit(block, a, b, work_o[a:b] + (total - 4.0 * own(a, b)))

    work, following = (work_o, work_d), (next_o, next_d)

    for hop in range(1, members):
        await_in(None, [(obs_in.at[0, lax.rem(mem + members - hop, members)], ("obs", hop))])
    for side in (-1, 1):
        tile, place = (0, last) if side < 0 else (members - 1, first)
        send(
            has[side],
            [
                (
                    obs_in.at[0, tile],
                    obs_in.at[lon_hop, place],
                    ("obs_edge", side, lon_hop),
                    ("obs_edge", -side, lon_hop),
                    device(0, side, lon_hop),
                )
                for lon_hop in (1, 0)
            ],
        )
    whole = pl.ds(0, members)
    send(
        None,
        [(obs_in.at[0, whole], obs_in.at[1, whole], ("obs_lon",), ("obs_lon",), device(0, 0, 1))],
    )
    for tile in range(members):
        hot(0, tile)

    for side in (-1, 1):
        await_in(
            has[side],
            [
                row_arrival("alpha", alpha_o, SWEEPS, side),
                row_arrival("kappa", kappa_o, SWEEPS, side),
                side_arrival("corner", corner_in, side),
            ],
        )
    await_in(None, [(pack_in, ("pack", 0))])

    def damp(begin, end):
        damp_o[begin:end] = 1.0 - 4.0 * kappa_o[begin:end]

    def at_block(value, place, block):
        return turned(value, SLOT * block - SLOT * place)

    for i in range(GROUP):
        part = pack_in[i]
        block = blocks_count - 1 if i < SWEEPS else 0
        ends = corner_in[0 if block == 0 else 1]
        at_end = slot == block
        alpha_d[i] = jnp.where(at_end, at_block(ends, i % SWEEPS, block), part)
        kappa_d[i] = jnp.where(
            at_end, at_block(ends, i % SWEEPS + SWEEPS, block), turned(part, half_turn)
        )
    damp(HALO - SWEEPS, HALO + rows + SWEEPS)
    damp_d[...] = 1.0 - 4.0 * kappa_d[...]

    for step in range(STEPS):

        def emit_term(a, b, value):
            term[a - HALO : b - HALO] = wx_o[a:b] * value

        smooth_sweep((alpha_o, alpha_d), work, SWEEPS - 1)
        src, dst = work, following
        for sweep in range(1, SWEEPS):
            smooth_sweep(
                src, dst, SWEEPS - 1 - sweep, emit_term if sweep == SWEEPS - 1 else None
            )
            src, dst = dst, src

        for tile in range(members):
            flat = term[tile * tile_rows : (tile + 1) * tile_rows].reshape(spots, LANES)
            high, low = halves(flat)
            cols = cols_hot[tile]
            picked = jnp.dot(high, cols, preferred_element_type=jnp.float32) + jnp.dot(
                low, cols, preferred_element_type=jnp.float32
            )
            picks = jnp.sum(
                picked * rows_hot[tile].astype(jnp.float32), axis=0, keepdims=True
            )
            picks_out[step, tile : tile + 1, :] = picks

        def pick_copy(hop, side, lon_hop):
            target = picks_in.at[step, hop, lon_hop]
            if side == 0:
                src, dst = picks_out.at[step], target.at[pl.ds(0, members)]
            elif side < 0:
                src, dst = picks_out.at[step, pl.ds(0, 1)], target.at[pl.ds(last, 1)]
            else:
                src = picks_out.at[step, pl.ds(members - 1, 1)]
                dst = target.at[pl.ds(first, 1)]
            return (
                src,
                dst,
                ("pick", step, hop, side, lon_hop),
                ("pick", step, hop, -side, lon_hop),
                device(hop, side, lon_hop),
            )

        for side in (-1, 1):
            send(
                has[side],
                [pick_copy(hop, side, lon_hop) for lon_hop in (1, 0) for hop in range(members)],
            )
        send(None, [pick_copy(hop, 0, 1) for hop in range(members)])
        send(None, [pick_copy(hop, 0, 0) for hop in range(1, members)])

        if step == 0:
            for side in (-1, 1):
                await_in(
                    has[side],
                    [
                        row_arrival("kappa_far", kappa_o, HALO - SWEEPS, side, SWEEPS),
                        row_arrival("x", wx_o, HALO, side),
                        side_arrival("far", far_in, side),
                    ],
                )
            await_in(None, [(packx_in, ("packx", 0))])
            for i in range(GROUP):
                part = packx_in[i % (GROUP // 2)]
                value = part if i < GROUP // 2 else turned(part, half_turn)
                for block, index in ((0, 0), (blocks_count - 1, 1)):
                    value = jnp.where(slot == block, at_block(far_in[index, 0], i, block), value)
                wx_d[i] = value
                block = 0 if i < SWEEPS else blocks_count - 1
                ends = at_block(far_in[0 if block == 0 else 1, 1], i % SWEEPS, block)
                kappa_d[i] = jnp.where(slot == block, ends, kappa_d[i])
            damp(0, HALO - SWEEPS)
            damp(HALO + rows + SWEEPS, rows + 2 * HALO)
            damp_d[...] = 1.0 - 4.0 * kappa_d[...]
            for side, tile in ((-1, first), (1, last)):
                for lon_hop in (0, 1):
                    await_in(
                        has[side], [(obs_in.at[lon_hop, tile], ("obs_edge", side, lon_hop))]
                    )
            await_in(None, [(obs_in.at[1, whole], ("obs_lon",))])
            for lon_hop in (0, 1):
                for tile in range(members + 2):
                    if (lon_hop, tile) not in [(0, t) for t in range(members)]:
                        hot(lon_hop, tile)
        if step == STEPS - 1:
            settle()

        def pulled_rows(lon_hop, a, b, observed=None):
            total = observed
            for hop in range(members):
                if hop == 0 and observed is not None:
                    continue
                piece = picks_in[step, hop, lon_hop, a:b, :]
                total = piece if total is None else total + piece
            masked_weight = weights_all[lon_hop, a:b, :]
            misfit = (total - values_all[lon_hop, a:b, :]) * masked_weight
            return jnp.clip(misfit, -huber_edge, huber_edge) * masked_weight

        def placed(rows_of, cols_of, pulled):
            left = jnp.concatenate([rows_of * half for half in halves(pulled)], axis=0)
            field = lax.dot_general(
                left, cols_of, (((1,), (1,)), ((), ())), preferred_element_type=jnp.float32
            )
            return (field[:spots] + field[spots:]).reshape(tile_rows, SUBLANES, LANES)

        def spread(tile, pulled):
            a = start_of[tile]
            b = a + tile_rows
            source = wx_o[a:b] * placed(rows_hot[tile], cols_hot[tile], pulled)
            work_o[a:b] = source
            path_o[0, a:b] = kappa_o[a:b] * source

        def arrivals(lon_hop, side):
            tile, count = {-1: (first, 1), 0: (0, members), 1: (last, 1)}[side]
            return [
                (
                    picks_in.at[step, hop, lon_hop, pl.ds(tile, count)],
                    ("pick", step, hop, side, lon_hop),
                )
                for hop in range(members)
                if (hop, lon_hop, side) != (0, 0, 0)
            ]

        await_in(None, arrivals(0, 0))
        pulled = pulled_rows(0, 0, members, picks_out[step])
        for tile in range(members):
            spread(tile, pulled[tile : tile + 1])
        def placed_near(a, b):
            pulled = pulled_rows(1, a, b)
            pulled = jnp.concatenate([pulled[t : t + 1] for t in range(b - a)], axis=1)
            part = slice(a * slots, b * slots)
            return placed(rows_near[:, part], cols_near[:, part], pulled)

        await_in(None, arrivals(1, 0))
        near_d[...] = placed_near(0, members)
        for side in (-1, 1):
            await_in(has[side], arrivals(0, side) + arrivals(1, side))
        pulled = pulled_rows(0, first, last + 1)
        for tile in (first, last):
            spread(tile, pulled[tile - first : tile - first + 1])
        source = wx_d[...] * (near_d[...] + placed_near(first, last + 1))
        work_d[...] = source
        path_d[0] = kappa_d[...] * source

        margin = HALO - step * SWEEPS
        final = step == STEPS - 1
        inside_top = (lat > 0).astype(jnp.float32)
        inside_bottom = (lat < lat_count - 1).astype(jnp.float32)

        def emit_alpha(block, a, b, value):
            held = alpha_d if block is None else alpha_o
            old = held[a:b]
            if final:
                fresh = ((1.0 - step_length) / step_length) * old - value
                fresh = turned(fresh, -SLOT * block, 2)
                for r in range(a, b):
                    out_ref[pl.ds(r - HALO, levels, stride=rows), :] = fresh[r - a]
                return
            fresh = old - step_length * (old + value)
            if block is None:
                fresh = fresh * jnp.where(
                    slot == 0,
                    inside_top,
                    jnp.where(slot == blocks_count - 1, inside_bottom, 1.0),
                )
            elif block == 0:
                fresh = fresh * inside_top
            elif block == blocks_count - 1:
                fresh = fresh * inside_bottom
            held[a:b] = fresh

        adjoint(margin, emit_alpha, not final)


def fused_picks(members, lat_count, x, control, kappa, cells, counts, innov, prec):
    _, levels, rows, columns = x.shape
    slots = cells.shape[1]
    spots = rows // members * levels
    count = len(picks_plan(members))
    vregs = lambda *lead: pltpu.VMEM(lead + (SUBLANES, LANES), jnp.float32)
    floats = lambda *shape: pltpu.VMEM(shape, jnp.float32)
    deep = rows + 2 * HALO
    tiles = members + 2
    place = pl.BlockSpec(memory_space=pltpu.HBM)
    in_hbm = lambda array: pltpu.with_memory_space_constraint(array, pltpu.HBM)
    flat = lambda dtype: pltpu.VMEM((levels * rows, columns), dtype)
    out = pl.pallas_call(
        functools.partial(picks_kernel, members, lat_count),
        out_shape=jax.ShapeDtypeStruct((levels * rows, columns), jnp.float32),
        in_specs=[place] * 4 + [pl.BlockSpec(memory_space=pltpu.SMEM)] + [place] * 2,
        out_specs=pl.BlockSpec(memory_space=pltpu.VMEM),
        scratch_shapes=[
            flat(x.dtype),
            pltpu.VMEM(cells.shape, cells.dtype),
            floats(*innov.shape),
            floats(*prec.shape),
            pltpu.SemaphoreType.DMA((2 * levels + 4,)),
            flat(jnp.float32),
        ]
        + [vregs(rows)] * 3
        + [vregs(deep)] * 6
        + [vregs(SWEEPS, deep)]
        + [vregs(GROUP)] * 6
        + [vregs(SWEEPS, GROUP), vregs(GROUP)]
        + [vregs(SWEEPS), vregs(HALO), vregs(HALO)]
        + [vregs(GROUP), vregs(GROUP // 2)] * 2
        + [vregs(2)] * 2
        + [vregs(2, 2)] * 2
        + [
            vregs(rows),
            floats(4, slots),
            floats(2, tiles, 4, slots),
            floats(2, tiles, slots),
            floats(2, tiles, slots),
            floats(STEPS, members, slots),
            floats(STEPS, members, 2, tiles, slots),
            pltpu.VMEM((tiles, spots, slots), jnp.bfloat16),
            pltpu.VMEM((tiles, LANES, slots), jnp.bfloat16),
            pltpu.VMEM((spots, tiles * slots), jnp.bfloat16),
            pltpu.VMEM((LANES, tiles * slots), jnp.bfloat16),
            pltpu.SemaphoreType.DMA((count,)),
            pltpu.SemaphoreType.DMA((count,)),
        ],
        compiler_params=pltpu.CompilerParams(
            collective_id=1, has_side_effects=True, vmem_limit_bytes=24 * 2**20
        ),
    )(
        in_hbm(x.reshape(levels * rows, columns)),
        in_hbm(control.reshape(levels * rows, columns)),
        in_hbm(kappa.reshape(levels * rows, columns)),
        in_hbm(cells),
        counts,
        in_hbm(innov),
        in_hbm(prec),
    )
    return (step_length * out).reshape(1, levels, rows, columns)


def fits_picks(members, lat_count, lon_count, x, cells):
    return (
        fits(members, lat_count, lon_count, x, cells)
        and lon_count == 2
        and 2 <= members
        and (members + 2) * SLOT <= LANES
        and x.shape[2] // members == HALO == GROUP == 2 * SWEEPS
        and cells.shape[1] % LANES == 0
    )


def on_device(members, lat_count, lon_count, x, control, kappa, cells, counts, innov, prec):
    if not fits(members, lat_count, lon_count, x, cells):
        return per_device(x, control, kappa, cells, counts, innov, prec)
    if fits_picks(members, lat_count, lon_count, x, cells):
        return fused_picks(members, lat_count, x, control, kappa, cells, counts, innov, prec)
    tile_rows = x.shape[2] // members
    return fused(
        members, lat_count, lon_count, tile_rows, x, control, kappa, cells, counts, innov, prec
    )


def solution(mesh):
    return jax.shard_map(
        functools.partial(
            on_device, mesh.shape["mem"], mesh.shape["lat"], mesh.shape["lon"]
        ),
        mesh=mesh,
        in_specs=(
            P("mem", None, "lat", "lon"),
            P("mem", None, "lat", "lon"),
            P(None, "lat", "lon"),
            P(("mem", "lat", "lon"), None),
            P(("mem", "lat", "lon")),
            P(("mem", "lat", "lon"), None),
            P(("mem", "lat", "lon"), None),
        ),
        out_specs=P("mem", None, "lat", "lon"),
        check_vma=False,
    )
```
